32 devices in a mesh: left: 8 (over y, x, core), right: 4 (over z).
Axes of the slice: x: 2, y: 2, z: 4, core: 2. Of those that a mesh axis runs over, the one named last changes fastest.
Arguments:
- left_freq: float32 [16384], P('left'), as said below
- right_freq: float32 [16384], P('right'), as said below
- left_dirs: float32 [16, 16384], P(None, 'left'), may hold values from -6 to 6
- left_data: float32 [16, 16384], P(None, 'left'), may hold values from -6 to 6
- right_dirs: float32 [16, 16384], P(None, 'right'), may hold values from -6 to 6
- right_data: float32 [16, 16384], P(None, 'right'), may hold values from -6 to 6
- col_sketch: bfloat16 [16384, 256], P('right'), may hold values from -0.047265625 to 0.047265625
- row_sketch: bfloat16 [16384, 256], P('left'), may hold values from -0.047265625 to 0.047265625
Outputs:
- row_scaled: float32 [16384, 256], P(('left', 'right'))
- col_scaled: float32 [16384, 256], P('right')
- lower_reduced: float32 [256, 256], replicated
- shifted_reduced: float32 [256, 256], replicated
The draws below stay inside these ranges and needn't reach their ends.
Inputs may be any that keep to these rules, and one draw needn't show every extreme that they name: left_freq[i] = 1 + (k + e) / 16384 with k distinct whole numbers of 0 to 16383 and |e| at most 0.2. right_freq[j] = 1 + (k + 0.5 + e) / 16384 with k distinct whole numbers of 0 to 16383 and |e| at most 0.2; left and right frequencies share the spacing 1 / 16384, so every left and right frequency differ by 0.1 / 16384 or more.
All inputs are finite; a program needn't handle non-finite values.
Results may differ from the reference program's by a relative error of at most 0.0089.
Values sent between devices are 32-bit elements; how exact they have to be, the bound alone decides.
A program may use at most 256 MiB of HBM per device.

```python
import math
import jax
import jax.numpy as jnp
from jax import lax

ROWS_DEV = 2048
SKETCH = 256
PORTS = 16
COLS_DEV = 4096
NR = 16384
NC = 16384


def jitter_values(key, count):
    return jax.random.uniform(key, (count,), jnp.float32, -0.15, 0.15)


def draw_left_freq(key, part):
    own_key = jax.random.fold_in(key, 31)
    index_all = jnp.arange(NR, dtype=jnp.int32)
    slots = NR // ROWS_DEV
    grid_pos = index_all % ROWS_DEV * slots + index_all // ROWS_DEV
    jitter = jitter_values(own_key, NR)
    return (1.0 + (grid_pos.astype(jnp.float32) + jitter) / NR).astype(jnp.float32)


def draw_right_freq(key, part):
    own_key = jax.random.fold_in(key, 57)
    index_all = jnp.arange(NC, dtype=jnp.int32)
    slots = NC // COLS_DEV
    grid_pos = index_all % COLS_DEV * slots + index_all // COLS_DEV
    jitter = jitter_values(own_key, NC)
    return (1.0 + (grid_pos.astype(jnp.float32) + 0.5 + jitter) / NR).astype(jnp.float32)


def sketch_values(key, row_total):
    base_key = jax.random.fold_in(key, 11)
    order_key = jax.random.fold_in(key, 12)
    marks_key = jax.random.fold_in(key, 13)
    signs_key = jax.random.fold_in(key, 14)
    inverse_root = float(row_total) ** (-0.5)
    base = jnp.clip(jax.random.normal(base_key, (row_total, SKETCH), jnp.float32), -6.0, 6.0) * inverse_root
    spread = inverse_root
    pair_count = SKETCH // 4
    order = jax.random.permutation(order_key, SKETCH).astype(jnp.int32)
    rank = jnp.argsort(order).astype(jnp.int32)
    pair_index = rank % pair_count
    is_copy = (rank >= pair_count) & (rank < 2 * pair_count)
    is_paired = rank < 2 * pair_count
    source = jnp.where(is_copy, order[pair_index], jnp.arange(SKETCH, dtype=jnp.int32)).astype(jnp.int32)
    picks = jax.random.randint(marks_key, (row_total, pair_count), 0, 16, dtype=jnp.int32) == 0
    marked = picks[:, pair_index] & is_paired[None, :]
    signs = (jax.random.randint(signs_key, (row_total, SKETCH), 0, 2, dtype=jnp.int32) * 2 - 1).astype(jnp.float32)
    small_step = 0.0016 * spread
    copied = base[:, source]
    values = jnp.where(marked, jnp.where(is_copy[None, :], small_step * signs, 0.0), copied)
    return values.astype(jnp.bfloat16)


def draw_col_sketch(key, part):
    return sketch_values(jax.random.fold_in(key, 71), NC)


def draw_row_sketch(key, part):
    return sketch_values(jax.random.fold_in(key, 73), NR)


def steps_of(rng, shape, split, low, top_value):
    def one(dim, blocks):
        heights = jax.random.uniform(jax.random.fold_in(jax.random.fold_in(rng, 6), dim), (blocks,), jnp.float32, low / len(split), top_value / len(split))
        return jnp.repeat(jnp.exp(heights), shape[dim] // blocks).reshape((-1,) + (1,) * (len(shape) - dim - 1))

    gain = one(*split[0])
    for cut in split[1:]:
        gain = gain * one(*cut)
    return gain


def gaussian(rng, dims, deviation, reach, pieces=(), kind=jnp.bfloat16):
    loudness = steps_of(rng, dims, pieces, -0.22, 0.18) if pieces else 1.0
    drawn = jax.random.normal(rng, dims, jnp.float32) * deviation * loudness
    return jnp.minimum(jnp.maximum(drawn, -reach), reach).astype(kind)


def setup_inputs(seed: int = 0) -> dict:
    key_list = jax.random.split(jax.random.key(seed), 9)
    return {
        "left_freq": draw_left_freq(jax.random.fold_in(key_list[8], 71), 0),
        "right_freq": draw_right_freq(jax.random.fold_in(key_list[8], 71), 0),
        "left_dirs": gaussian(key_list[2], (PORTS, NR), 1.0, 6.0, ((1, 8),), jnp.float32),
        "left_data": gaussian(key_list[3], (PORTS, NR), 1.0, 6.0, ((1, 8),), jnp.float32),
        "right_dirs": gaussian(key_list[4], (PORTS, NC), 1.0, 6.0, ((1, 4),), jnp.float32),
        "right_data": gaussian(key_list[5], (PORTS, NC), 1.0, 6.0, ((1, 4),), jnp.float32),
        "col_sketch": draw_col_sketch(jax.random.fold_in(key_list[8], 71), 0),
        "row_sketch": draw_row_sketch(jax.random.fold_in(key_list[8], 71), 0),
    }


precise = lax.Precision.HIGHEST

def build_tiles(freq_rows, dirs_rows, data_rows, right_freq, right_dirs, right_data, total_rows):
    direct = lax.dot_general(data_rows.astype(jnp.float32), right_dirs.astype(jnp.float32), (((0,), (0,)), ((), ())), precision=precise, preferred_element_type=jnp.float32)
    crossed = lax.dot_general(dirs_rows.astype(jnp.float32), right_data.astype(jnp.float32), (((0,), (0,)), ((), ())), precision=precise, preferred_element_type=jnp.float32)
    spacing_gap = total_rows * (freq_rows[:, None] - right_freq[None, :])
    lower_tile = ((direct - crossed) / spacing_gap).astype(jnp.bfloat16)
    shift_tile = ((freq_rows[:, None] * direct - right_freq[None, :] * crossed) / spacing_gap).astype(jnp.bfloat16)
    return (lower_tile, shift_tile)

def factor_pass(basis, shifted_flag):
    gram_sum = lax.dot_general(basis.astype(jnp.float32), basis.astype(jnp.float32), (((0,), (0,)), ((), ())), precision=precise, preferred_element_type=jnp.float32)
    width = gram_sum.shape[0]
    identity = jnp.eye(width, dtype=jnp.float32)
    if shifted_flag:
        gram_sum = gram_sum + 1e-05 * jnp.trace(gram_sum) / width * identity
    factor = jnp.linalg.cholesky(gram_sum)
    inverse = jax.scipy.linalg.solve_triangular(factor, identity, lower=True)
    return lax.dot_general(basis.astype(jnp.float32), inverse.astype(jnp.float32), (((1,), (1,)), ((), ())), precision=precise, preferred_element_type=jnp.float32)

def orthonormalize(image):
    return factor_pass(factor_pass(image, True), False)

def reference(left_freq, right_freq, left_dirs, left_data, right_dirs, right_data, col_sketch, row_sketch):
    blocks = NR // ROWS_DEV
    freq_blocks = left_freq.reshape(blocks, ROWS_DEV)
    dirs_blocks = left_dirs.reshape(PORTS, blocks, ROWS_DEV).transpose(1, 0, 2)
    data_blocks = left_data.reshape(PORTS, blocks, ROWS_DEV).transpose(1, 0, 2)
    sketch_blocks = row_sketch.reshape(blocks, ROWS_DEV, SKETCH)

    def first_sweep(running, block_in):
        freq_rows, dirs_rows, data_rows, sketch_rows = block_in
        lower_tile, shift_tile = build_tiles(freq_rows, dirs_rows, data_rows, right_freq, right_dirs, right_data, NR)
        rows_out = jnp.dot(lower_tile.astype(jnp.float32), col_sketch.astype(jnp.float32), preferred_element_type=jnp.float32)
        running = running + lax.dot_general(lower_tile.astype(jnp.float32), sketch_rows.astype(jnp.float32), (((0,), (0,)), ((), ())), preferred_element_type=jnp.float32)
        return (running, rows_out)
    col_image, row_blocks = lax.scan(first_sweep, jnp.zeros((NC, SKETCH), jnp.float32), (freq_blocks, dirs_blocks, data_blocks, sketch_blocks))
    row_image = row_blocks.reshape(NR, SKETCH)
    row_basis = orthonormalize(row_image)
    col_basis = orthonormalize(col_image)
    col_round = col_basis.astype(jnp.bfloat16)
    basis_blocks = row_basis.reshape(blocks, ROWS_DEV, SKETCH)

    def second_sweep(running, block_in):
        freq_rows, dirs_rows, data_rows, basis_rows = block_in
        lower_tile, shift_tile = build_tiles(freq_rows, dirs_rows, data_rows, right_freq, right_dirs, right_data, NR)
        lower_applied = jnp.dot(lower_tile.astype(jnp.float32), col_round.astype(jnp.float32), preferred_element_type=jnp.float32)
        shift_applied = jnp.dot(shift_tile.astype(jnp.float32), col_round.astype(jnp.float32), preferred_element_type=jnp.float32)
        lower_part = lax.dot_general(basis_rows.astype(jnp.float32), lower_applied.astype(jnp.float32), (((0,), (0,)), ((), ())), precision=precise, preferred_element_type=jnp.float32)
        shift_part = lax.dot_general(basis_rows.astype(jnp.float32), shift_applied.astype(jnp.float32), (((0,), (0,)), ((), ())), precision=precise, preferred_element_type=jnp.float32)
        return ((running[0] + lower_part, running[1] + shift_part), None)
    start_sums = (jnp.zeros((SKETCH, SKETCH), jnp.float32), jnp.zeros((SKETCH, SKETCH), jnp.float32))
    reduced_pair, unused_out = lax.scan(second_sweep, start_sums, (freq_blocks, dirs_blocks, data_blocks, basis_blocks))
    return (row_basis * math.sqrt(NR), col_basis * math.sqrt(NC), reduced_pair[0], reduced_pair[1])
```

```python
import functools
import math

import jax
import jax.numpy as jnp
from jax import lax
from jax.experimental import pallas as pl
from jax.experimental.pallas import tpu as pltpu
from jax.sharding import PartitionSpec as P

precise = lax.Precision.HIGHEST
F32 = jnp.float32
BF16 = jnp.bfloat16
LEFT_PARTS = (0, 0, 1, 0, 1, 2)
RIGHT_PARTS = (0, 1, 0, 2, 1, 0)


def tdot(a, b, precision=None):
    return lax.dot_general(
        a, b, (((0,), (0,)), ((), ())), precision=precision, preferred_element_type=F32
    )


def split3(x):
    one = x.astype(BF16).astype(F32)
    rest = x - one
    two = rest.astype(BF16).astype(F32)
    return (one, two, (rest - two).astype(BF16).astype(F32))


def stack_parts(first, second, order):
    a, b = split3(first), split3(second)
    pieces = [a[p] for p in order] + [b[p] for p in order]
    pad = jnp.zeros((256 - 12 * first.shape[0], first.shape[1]), F32)
    return jnp.concatenate(pieces + [pad], axis=0)


def tile_kernel(
    total, rows_step,
    lf_ref, rf_ref, ld_ref, la_ref, rd_ref, ra_ref, cs_ref, rs_ref,
    tile_ref, row_ref, col_ref,
    left_scr, sketch_scr, freq_scr,
):
    step = pl.program_id(0)
    rows = left_scr.shape[0]

    @pl.when(step == 0)
    def _():
        for r in range(0, rows, 512):
            wide = jnp.broadcast_to(lf_ref[:, r:r + 512], (128, 512))
            freq_scr[r:r + 512, :] = wide.T[:, 0:1]
            stacked = stack_parts(la_ref[:, r:r + 512], -ld_ref[:, r:r + 512], LEFT_PARTS)
            left_scr[r:r + 512, :] = stacked.T.astype(BF16)
            sketch_scr[:, r:r + 512] = rs_ref[r:r + 512, :].astype(F32).T.astype(BF16)
        row_ref[...] = jnp.zeros_like(row_ref)

    right = stack_parts(rd_ref[...], ra_ref[...], RIGHT_PARTS).astype(BF16)
    freq = rf_ref[...]
    acc = jnp.zeros((256, right.shape[1]), F32)
    for chunk in range(rows // rows_step):
        sl = pl.ds(chunk * rows_step, rows_step)
        numer = jnp.dot(left_scr[sl, :], right, preferred_element_type=F32)
        gap = total * (freq_scr[sl, :] - freq)
        tile = (numer / gap).astype(BF16)
        tile_ref[sl, :] = tile
        row_ref[sl, :] += jnp.dot(tile, cs_ref[...], preferred_element_type=F32)
        acc += jnp.dot(sketch_scr[:, sl], tile, preferred_element_type=F32)
    col_ref[...] = acc.T


def build(lf, rf, ld, la, rd, ra, cs, rs, total):
    rows, cols = lf.shape[0], rf.shape[0]
    ports, width = ld.shape[0], cs.shape[1]
    tc = 256
    fixed = lambda j: (0, 0)
    return pl.pallas_call(
        functools.partial(tile_kernel, float(total), 256),
        grid=(cols // tc,),
        in_specs=[
            pl.BlockSpec((1, rows), fixed),
            pl.BlockSpec((1, tc), lambda j: (0, j)),
            pl.BlockSpec((ports, rows), fixed),
            pl.BlockSpec((ports, rows), fixed),
            pl.BlockSpec((ports, tc), lambda j: (0, j)),
            pl.BlockSpec((ports, tc), lambda j: (0, j)),
            pl.BlockSpec((tc, width), lambda j: (j, 0)),
            pl.BlockSpec((rows, width), fixed),
        ],
        out_specs=[
            pl.BlockSpec((rows, tc), lambda j: (0, j)),
            pl.BlockSpec((rows, width), fixed),
            pl.BlockSpec((tc, width), lambda j: (j, 0)),
        ],
        out_shape=[
            jax.ShapeDtypeStruct((rows, cols), BF16),
            jax.ShapeDtypeStruct((rows, width), F32),
            jax.ShapeDtypeStruct((cols, width), F32),
        ],
        scratch_shapes=[
            pltpu.VMEM((rows, 256), BF16),
            pltpu.VMEM((width, rows), BF16),
            pltpu.VMEM((rows, 1), F32),
        ],
        compiler_params=pltpu.CompilerParams(
            dimension_semantics=("arbitrary",), vmem_limit_bytes=40 << 20
        ),
        name="tiles",
    )(lf[None, :], rf[None, :], ld, la, rd, ra, cs, rs)


BLOCK = 32


def triangle(width):
    return [(i, j) for i in range(width // 128) for j in range(i, width // 128)]


def store_gram(dst, m, gram):
    for n, (i, j) in enumerate(triangle(gram.shape[0])):
        dst[m, n * 128:(n + 1) * 128, :] = gram[i * 128:(i + 1) * 128, j * 128:(j + 1) * 128]


def factor(shifted, t_ref, out_ref, work):
    width = out_ref.shape[-1]
    row_id = lax.broadcasted_iota(jnp.int32, (width, width), 0)
    col_id = lax.broadcasted_iota(jnp.int32, (width, width), 1)
    eye = (row_id == col_id).astype(F32)
    for m in range(2):
        work[m, :, 0:width] = jnp.zeros((width, width), F32)
        for n, (i, j) in enumerate(triangle(width)):
            work[m, i * 128:(i + 1) * 128, j * 128:(j + 1) * 128] = t_ref[m, n * 128:(n + 1) * 128, :]
        if shifted:
            gram = work[m, :, 0:width]
            trace = jnp.sum(jnp.sum(gram * eye, axis=1, keepdims=True), axis=0, keepdims=True)
            work[m, :, 0:width] = gram + (1e-05 * trace / width) * eye
        work[m, :, width:] = eye
    brow = lax.broadcasted_iota(jnp.int32, (BLOCK, BLOCK), 0)
    bcol = lax.broadcasted_iota(jnp.int32, (BLOCK, BLOCK), 1)
    small_eye = (brow == bcol).astype(F32)
    low = lax.broadcasted_iota(jnp.int32, (BLOCK, 2 * BLOCK), 0)
    for k in range(0, width, BLOCK):
        pairs = [
            jnp.concatenate([work[m, k:k + BLOCK, k:k + BLOCK], small_eye], axis=1)
            for m in range(2)
        ]
        for s in range(BLOCK):
            tops = [1.0 / pair[s:s + 1, s:s + 1] for pair in pairs]
            columns = [jnp.where(low > s, pair[:, s:s + 1], 0.0) for pair in pairs]
            pairs = [
                pair - column * (pair[s:s + 1, :] * top)
                for pair, column, top in zip(pairs, columns, tops)
            ]
        lo = k + BLOCK
        start, stop = k // 128 * 128, width + (lo + 127) // 128 * 128
        solved = []
        for m in range(2):
            diag = jnp.sum(pairs[m][:, 0:BLOCK] * small_eye, axis=1, keepdims=True)
            inv = pairs[m][:, BLOCK:] * lax.rsqrt(diag)
            solved.append(
                jnp.dot(
                    inv, work[m, k:lo, start:stop], precision=precise,
                    preferred_element_type=F32,
                )
            )
        for m in range(2):
            out_ref[m, k:lo, 0:stop - width] = solved[m][:, width - start:]
            if stop < 2 * width:
                out_ref[m, k:lo, stop - width:] = jnp.zeros((BLOCK, 2 * width - stop), F32)
        if lo < width:
            deltas = [tdot(rows[:, lo - start:width - start], rows, precise) for rows in solved]
            for m in range(2):
                work[m, lo:, start:stop] = work[m, lo:, start:stop] - deltas[m]


def apply_inverse(basis, inverse, precision):
    return lax.dot_general(
        basis, inverse, (((1,), (1,)), ((), ())), precision=precision, preferred_element_type=F32
    )


def places():
    me, deep = lax.axis_index("left"), lax.axis_index("right")
    core = lax.rem(me, 2)
    return me, deep, core, me // 2


def chip_peer(chip, core, offset, chips):
    return {"left": lax.rem(chip + offset, chips) * 2 + core}


def greet(chips, deeps):
    me, deep, core, chip = places()
    barrier = pltpu.get_barrier_semaphore()
    peers = [{"left": chip * 2 + (1 - core)}]
    peers += [chip_peer(chip, core, o, chips) for o in range(1, chips)]
    peers += [{"right": lax.rem(deep + o, deeps)} for o in range(1, deeps)]
    for peer in peers:
        pl.semaphore_signal(
            barrier, inc=1, device_id=peer, device_id_type=pl.DeviceIdType.MESH
        )
    pl.semaphore_wait(barrier, len(peers))


def send(src, dst, sems, slot, peer):
    copy = pltpu.make_async_remote_copy(
        src_ref=src,
        dst_ref=dst,
        send_sem=sems.at[0, slot],
        recv_sem=sems.at[1, slot],
        device_id=peer,
        device_id_type=pl.DeviceIdType.MESH,
    )
    copy.start()
    return copy


def scatter_kernel(
    chips, deeps, row_ref, col_ref, row_out, col_out,
    deep_buf, core_buf, half_buf, chip_buf, deep_sem, core_sem, chip_sem,
):
    me, deep, core, chip = places()
    greet(chips, deeps)
    share, half, piece = row_out.shape[0], core_buf.shape[0], col_out.shape[0]
    pair = send(
        col_ref.at[pl.ds((1 - core) * half, half)], core_buf, core_sem, 0,
        {"left": chip * 2 + (1 - core)},
    )
    deep_copies = []
    for o in range(1, deeps):
        peer = lax.rem(deep + o, deeps)
        deep_copies.append(
            send(
                row_ref.at[pl.ds(peer * share, share)], deep_buf.at[o - 1], deep_sem, o - 1,
                {"right": peer},
            )
        )
    pair.wait()

    @pl.loop(0, chips)
    def _(p):
        sl = pl.ds(p * piece, piece)
        half_buf[sl, :] = col_ref[pl.ds(core * half + p * piece, piece), :] + core_buf[sl, :]

    chip_copies = []
    for o in range(1, chips):
        peer = lax.rem(chip + o, chips)
        chip_copies.append(
            send(
                half_buf.at[pl.ds(peer * piece, piece)], chip_buf.at[o - 1], chip_sem, o - 1,
                {"left": peer * 2 + core},
            )
        )
    col_out[...] = half_buf[pl.ds(chip * piece, piece), :]
    row_out[...] = row_ref[pl.ds(deep * share, share), :]
    for o in range(1, chips):
        chip_copies[o - 1].wait()
        col_out[...] += chip_buf[o - 1]
    for o in range(1, deeps):
        deep_copies[o - 1].wait()
        row_out[...] += deep_buf[o - 1]


def vmem_specs(n):
    return [pl.BlockSpec(memory_space=pltpu.VMEM)] * n


def sem_pair(n):
    return pltpu.SemaphoreType.DMA((2, n))


def comm_params(cid):
    return pltpu.CompilerParams(
        collective_id=cid, has_side_effects=True, vmem_limit_bytes=40 << 20
    )


def scatter(row_image, col_image):
    chips, deeps = lax.axis_size("left") // 2, lax.axis_size("right")
    rows, width = row_image.shape
    cols = col_image.shape[0]
    share, half, piece = rows // deeps, cols // 2, cols // 2 // chips
    return pl.pallas_call(
        functools.partial(scatter_kernel, chips, deeps),
        in_specs=vmem_specs(2),
        out_specs=vmem_specs(2),
        out_shape=[
            jax.ShapeDtypeStruct((share, width), F32),
            jax.ShapeDtypeStruct((piece, width), F32),
        ],
        scratch_shapes=[
            pltpu.VMEM((deeps - 1, share, width), F32),
            pltpu.VMEM((half, width), F32),
            pltpu.VMEM((half, width), F32),
            pltpu.VMEM((chips - 1, piece, width), F32),
            sem_pair(deeps - 1), sem_pair(1), sem_pair(chips - 1),
        ],
        compiler_params=comm_params(1),
        name="scatter",
    )(row_image, col_image)


def reduce_kernel(
    chips, deeps, x_ref, out_ref,
    core_buf, half_buf, chip_buf, deep_buf,
    core_sem, chip_sem, deep_sem, back_sem, last_sem,
):
    me, deep, core, chip = places()
    greet(chips, deeps)
    half, piece = core_buf.shape[0], chip_buf.shape[1]
    sibling = {"left": chip * 2 + (1 - core)}
    send(x_ref.at[pl.ds((1 - core) * half, half)], core_buf, core_sem, 0, sibling).wait()
    half_buf[...] = x_ref[pl.ds(core * half, half), :] + core_buf[...]
    copies = []
    for o in range(1, chips):
        peer = lax.rem(chip + o, chips)
        copies.append(
            send(
                half_buf.at[pl.ds(peer * piece, piece)], chip_buf.at[o - 1], chip_sem, o - 1,
                {"left": peer * 2 + core},
            )
        )
    part = half_buf[pl.ds(chip * piece, piece), :]
    for o in range(1, chips):
        copies[o - 1].wait()
        part = part + chip_buf[o - 1]
    deep_buf[deep] = part
    copies = []
    for o in range(1, deeps):
        copies.append(
            send(
                deep_buf.at[deep], deep_buf.at[deep], deep_sem, o - 1,
                {"right": lax.rem(deep + o, deeps)},
            )
        )
    for copy in copies:
        copy.wait()
    part = deep_buf[0]
    for d in range(1, deeps):
        part = part + deep_buf[d]
    mine = pl.ds(core * half + chip * piece, piece)
    out_ref[mine, :] = part
    copies = []
    for o in range(1, chips):
        copies.append(
            send(
                out_ref.at[mine], out_ref.at[mine], back_sem, o - 1,
                chip_peer(chip, core, o, chips),
            )
        )
    for copy in copies:
        copy.wait()
    own = pl.ds(core * half, half)
    send(out_ref.at[own], out_ref.at[own], last_sem, 0, sibling).wait()


def reduce_all(x, cid):
    chips, deeps = lax.axis_size("left") // 2, lax.axis_size("right")
    rows, width = x.shape
    half, piece = rows // 2, rows // 2 // chips
    return pl.pallas_call(
        functools.partial(reduce_kernel, chips, deeps),
        in_specs=vmem_specs(1),
        out_specs=vmem_specs(1)[0],
        out_shape=jax.ShapeDtypeStruct(x.shape, F32),
        scratch_shapes=[
            pltpu.VMEM((half, width), F32),
            pltpu.VMEM((half, width), F32),
            pltpu.VMEM((chips - 1, piece, width), F32),
            pltpu.VMEM((deeps, piece, width), F32),
            sem_pair(1), sem_pair(chips - 1), sem_pair(deeps - 1), sem_pair(chips - 1),
            sem_pair(1),
        ],
        compiler_params=comm_params(cid),
        name="reduce",
    )(x)


def sum_all(chips, deeps, x, total, core_buf, half_buf, chip_buf, deep_buf, sems):
    me, deep, core, chip = places()
    core_sem, chip_sem, deep_sem, back_sem, last_sem = sems
    piece = chip_buf.shape[1]
    sibling = {"left": chip * 2 + (1 - core)}
    part_of = lambda q: pl.ds(pl.multiple_of(q * piece, 8), piece)
    firsts = []
    for o in range(1, chips + 1):
        q = part_of(lax.rem(chip + o, chips))
        firsts.append(send(x.at[1 - core, q], core_buf.at[q], core_sem, o - 1, sibling))
    copies = []
    for o in range(1, chips + 1):
        peer = lax.rem(chip + o, chips)
        q = part_of(peer)
        firsts[o - 1].wait()
        half_buf[q, :] = x[core, q, :] + core_buf[q, :]
        if o < chips:
            copies.append(
                send(half_buf.at[q], chip_buf.at[o - 1], chip_sem, o - 1, {"left": peer * 2 + core})
            )
    mine = part_of(chip)
    part = half_buf[mine, :]
    for o in range(1, chips):
        copies[o - 1].wait()
        part = part + chip_buf[o - 1]
    deep_buf[deep] = part
    copies = []
    for o in range(1, deeps):
        copies.append(
            send(
                deep_buf.at[deep], deep_buf.at[deep], deep_sem, o - 1,
                {"right": lax.rem(deep + o, deeps)},
            )
        )
    for copy in copies:
        copy.wait()
    part = deep_buf[0]
    for d in range(1, deeps):
        part = part + deep_buf[d]
    total[core, mine, :] = part
    copies = []
    for o in range(1, chips):
        copies.append(
            send(
                total.at[core, mine], total.at[core, mine], back_sem, o - 1,
                chip_peer(chip, core, o, chips),
            )
        )
    lasts = [send(total.at[core, mine], total.at[core, mine], last_sem, 0, sibling)]
    for o in range(1, chips):
        copies[o - 1].wait()
        q = part_of(lax.rem(chip + chips - o, chips))
        lasts.append(send(total.at[core, q], total.at[core, q], last_sem, o, sibling))
    for copy in lasts:
        copy.wait()


def middle_kernel(
    chips, deeps, row_ref, col_ref, row_out, col_out, inv_out,
    x_buf, total, core_buf, half_buf, chip_buf, deep_buf, work, inv1, inv2,
    core_sem, chip_sem, deep_sem, back_sem, last_sem, row_sem, col_sem, pair_sem,
):
    me, deep, core, chip = places()
    greet(chips, deeps)
    share, block = row_ref.shape[0], col_ref.shape[0]
    sibling = {"left": chip * 2 + (1 - core)}
    cols_mine = pl.ds(pl.multiple_of((core * chips + chip) * block, 8), block)

    def reduce_round(n, row, col):
        store_gram(x_buf.at[n], 0, tdot(row, row, precise))
        store_gram(x_buf.at[n], 1, tdot(col, col, precise))
        sum_all(
            chips, deeps, x_buf.at[n], total.at[n], core_buf.at[n], half_buf.at[n],
            chip_buf.at[n], deep_buf.at[n],
            [s.at[n] for s in (core_sem, chip_sem, deep_sem, back_sem, last_sem)],
        )

    def row_half(n):
        half = share // 2
        src = pl.ds(n * half, half)
        dst = pl.ds(pl.multiple_of(deep * share + n * half, 8), half)
        return [
            send(
                row_ref.at[src], row_out.at[dst], row_sem.at[n], o - 1,
                {"right": lax.rem(deep + o, deeps)},
            )
            for o in range(1, deeps)
        ]

    reduce_round(0, row_ref[...], col_ref[...])
    row_copies = row_half(0)
    col_copies = [
        send(
            col_ref, col_out.at[cols_mine], col_sem, o - 1, chip_peer(chip, core, o, chips)
        )
        for o in range(1, chips)
    ]
    row_out[pl.ds(pl.multiple_of(deep * share, 8), share), :] = row_ref[...]
    col_out[cols_mine, :] = col_ref[...]
    factor(True, total.at[0], inv1, work)
    row_own = apply_inverse(row_ref[...], inv1[0], precise)
    col_own = apply_inverse(col_ref[...], inv1[1], precise)
    for copy in col_copies:
        copy.wait()
    own = pl.ds(pl.multiple_of(core * chips * block, 8), chips * block)
    pair = send(col_out.at[own], col_out.at[own], pair_sem, 0, sibling)
    reduce_round(1, row_own, col_own)
    row_copies += row_half(1)
    factor(False, total.at[1], inv2, work)
    for m in range(2):
        inv_out[m] = jnp.dot(inv2[m], inv1[m], precision=precise, preferred_element_type=F32)
    pair.wait()
    for copy in row_copies:
        copy.wait()


def middle(row_own, col_own):
    chips, deeps = lax.axis_size("left") // 2, lax.axis_size("right")
    width = row_own.shape[1]
    high = 128 * len(triangle(width))
    piece = high // chips
    sems = lambda n: pltpu.SemaphoreType.DMA((2, 2, n))
    return pl.pallas_call(
        functools.partial(middle_kernel, chips, deeps),
        in_specs=vmem_specs(2),
        out_specs=vmem_specs(3),
        out_shape=[
            jax.ShapeDtypeStruct((row_own.shape[0] * deeps, width), F32),
            jax.ShapeDtypeStruct((col_own.shape[0] * chips * 2, width), F32),
            jax.ShapeDtypeStruct((2, width, width), F32),
        ],
        scratch_shapes=[
            pltpu.VMEM((2, 2, high, 128), F32),
            pltpu.VMEM((2, 2, high, 128), F32),
            pltpu.VMEM((2, high, 128), F32),
            pltpu.VMEM((2, high, 128), F32),
            pltpu.VMEM((2, chips - 1, piece, 128), F32),
            pltpu.VMEM((2, deeps, piece, 128), F32),
            pltpu.VMEM((2, width, 2 * width), F32),
            pltpu.VMEM((2, width, width), F32),
            pltpu.VMEM((2, width, width), F32),
            sems(chips), sems(chips - 1), sems(deeps - 1), sems(chips - 1), sems(chips),
            sems(deeps - 1), sem_pair(chips - 1), sem_pair(1),
        ],
        compiler_params=comm_params(2),
        name="middle",
    )(row_own, col_own)


def project_kernel(lf_ref, tile_ref, v_ref, q_ref, out_ref):
    @pl.when(pl.program_id(0) == 0)
    def _():
        out_ref[...] = jnp.zeros_like(out_ref)

    applied = jnp.dot(tile_ref[...], v_ref[...], preferred_element_type=F32)
    freq = jnp.broadcast_to(lf_ref[...], (128, lf_ref.shape[1])).T[:, 0:1]
    both = jnp.concatenate([applied, applied * freq], axis=1)
    both_hi = both.astype(BF16)
    both_lo = (both - both_hi.astype(F32)).astype(BF16)
    q = q_ref[...].T
    q_hi = q.astype(BF16)
    q_lo = (q - q_hi.astype(F32)).astype(BF16)
    out_ref[...] += jnp.dot(
        jnp.concatenate([q_hi, q_hi, q_lo], axis=1),
        jnp.concatenate([both_hi, both_lo, both_hi], axis=0),
        preferred_element_type=F32,
    )


def project(lf, tile, v, q):
    rows, cols = tile.shape
    width = v.shape[1]
    block = 256
    return pl.pallas_call(
        project_kernel,
        grid=(rows // block,),
        in_specs=[
            pl.BlockSpec((1, block), lambda i: (0, i)),
            pl.BlockSpec((block, cols), lambda i: (i, 0)),
            pl.BlockSpec((cols, width), lambda i: (0, 0)),
            pl.BlockSpec((block, width), lambda i: (i, 0)),
        ],
        out_specs=pl.BlockSpec((width, 2 * width), lambda i: (0, 0)),
        out_shape=jax.ShapeDtypeStruct((width, 2 * width), F32),
        compiler_params=pltpu.CompilerParams(
            dimension_semantics=("arbitrary",), vmem_limit_bytes=32 << 20
        ),
        name="project",
    )(lf[None, :], tile, v, q)


def body(lf, rf, ld, la, rd, ra, cs, rs):
    rows, cols = lf.shape[0], rf.shape[0]
    width = cs.shape[1]
    left_n, right_n = lax.axis_size("left"), lax.axis_size("right")
    total_rows, total_cols = rows * left_n, cols * right_n
    tile, row_image, col_image = build(lf, rf, ld, la, rd, ra, cs, rs, total_rows)
    row_own, col_own = scatter(row_image, col_image)
    row_full, col_full, inverse = middle(row_own, col_own)
    row_part = apply_inverse(row_own, inverse[0], precise)
    row_full = apply_inverse(row_full, inverse[0], precise)
    col_full = apply_inverse(col_full, inverse[1], precise)
    col_round = col_full.astype(BF16)
    reduced = project(lf, tile, col_round, row_full)
    low_rank = jnp.dot(
        lax.dot_general(row_full, ld, (((0,), (1,)), ((), ())), precision=precise),
        jnp.dot(ra, col_round.astype(F32), precision=precise) * (1.0 / total_rows),
        precision=precise,
    )
    reduced = jnp.concatenate([reduced[:, :width], reduced[:, width:] + low_rank], axis=0)
    reduced = reduce_all(reduced, 3)
    return (
        row_part * math.sqrt(total_rows),
        col_full * math.sqrt(total_cols),
        reduced[:width],
        reduced[width:],
    )


def solution(mesh):
    in_specs = (
        P("left"), P("right"), P(None, "left"), P(None, "left"),
        P(None, "right"), P(None, "right"), P("right", None), P("left", None),
    )
    out_specs = (P(("left", "right"), None), P("right", None), P(), P())
    return jax.shard_map(body, mesh=mesh, in_specs=in_specs, out_specs=out_specs, check_vma=False)
```

```python
import functools
import math

import jax
import jax.numpy as jnp
from jax import lax
from jax.experimental import pallas as pl
from jax.experimental.pallas import tpu as pltpu
from jax.sharding import PartitionSpec as P

precise = lax.Precision.HIGHEST
F32 = jnp.float32
BF16 = jnp.bfloat16
LEFT_PARTS = (0, 0, 1, 0, 1, 2)
RIGHT_PARTS = (0, 1, 0, 2, 1, 0)


def tdot(a, b, precision=None):
    return lax.dot_general(
        a, b, (((0,), (0,)), ((), ())), precision=precision, preferred_element_type=F32
    )


def split3(x):
    one = x.astype(BF16).astype(F32)
    rest = x - one
    two = rest.astype(BF16).astype(F32)
    return (one, two, (rest - two).astype(BF16).astype(F32))


def stack_parts(first, second, order):
    a, b = split3(first), split3(second)
    pieces = [a[p] for p in order] + [b[p] for p in order]
    pad = jnp.zeros((256 - 12 * first.shape[0], first.shape[1]), F32)
    return jnp.concatenate(pieces + [pad], axis=0)


UNIT = 512


def places():
    me, deep = lax.axis_index("left"), lax.axis_index("right")
    core = lax.rem(me, 2)
    return me, deep, core, me // 2


def chip_peer(chip, core, offset, chips):
    return {"left": lax.rem(chip + offset, chips) * 2 + core}


def peers_of(chips, deeps):
    me, deep, core, chip = places()
    peers = [{"left": chip * 2 + (1 - core)}]
    peers += [chip_peer(chip, core, o, chips) for o in range(1, chips)]
    peers += [{"right": lax.rem(deep + o, deeps)} for o in range(1, deeps)]
    return peers


def greet_start(chips, deeps):
    barrier = pltpu.get_barrier_semaphore()
    for peer in peers_of(chips, deeps):
        pl.semaphore_signal(
            barrier, inc=1, device_id=peer, device_id_type=pl.DeviceIdType.MESH
        )


def greet_end(chips, deeps):
    pl.semaphore_wait(pltpu.get_barrier_semaphore(), chips + deeps - 1)


def greet(chips, deeps):
    greet_start(chips, deeps)
    greet_end(chips, deeps)


def send(src, dst, sems, slot, peer):
    copy = pltpu.make_async_remote_copy(
        src_ref=src,
        dst_ref=dst,
        send_sem=sems.at[0, slot],
        recv_sem=sems.at[1, slot],
        device_id=peer,
        device_id_type=pl.DeviceIdType.MESH,
    )
    copy.start()
    return copy


def reversed_bits(p, bits):
    return sum(((p >> i) & 1) << (bits - 1 - i) for i in range(bits))


def tiles_kernel(
    total, chips, deeps,
    lf_any, rf_any, ld_any, la_any, rd_any, ra_any, cs_any, rs_any,
    tile_ref, row_out, col_out,
    lf_ref, rf_ref, ld_ref, la_ref, rd_ref, ra_ref, cs_ref, rs_ref,
    left_scr, right_scr, sketch_scr, freq_scr, row_acc, col_acc, col_part,
    row_buf, core_buf, half_buf, chip_buf,
    in_sem, row_sem, core_sem, chip_sem,
):
    me, deep, core, chip = places()
    rows, cols = tile_ref.shape
    width = row_out.shape[1]
    chunks, blocks = rows // UNIT, cols // UNIT
    steps = deeps.bit_length() - 1
    share, seg = rows // deeps, UNIT // deeps
    order = [reversed_bits(p, steps) for p in range(deeps)]
    sibling = {"left": chip * 2 + (1 - core)}
    loads = [
        pltpu.make_async_copy(src, dst, in_sem.at[n])
        for n, (src, dst) in enumerate(
            [
                (lf_any, lf_ref), (la_any, la_ref), (ld_any, ld_ref), (rs_any, rs_ref),
                (rf_any, rf_ref), (rd_any, rd_ref), (ra_any, ra_ref), (cs_any, cs_ref),
            ]
        )
    ]
    for load in loads:
        load.start()
    greet_start(chips, deeps)

    @pl.loop(0, chunks)
    def _(c):
        row_acc[c] = jnp.zeros((UNIT, width), F32)

    @pl.loop(0, blocks)
    def _(b):
        col_acc[b] = jnp.zeros((width, UNIT), F32)

    for load in loads[:4]:
        load.wait()
    for r in range(0, rows, UNIT):
        wide = jnp.broadcast_to(lf_ref[:, r:r + UNIT] * total, (128, UNIT))
        freq_scr[r:r + UNIT, :] = wide.T
        stacked = stack_parts(la_ref[:, r:r + UNIT], -ld_ref[:, r:r + UNIT], LEFT_PARTS)
        left_scr[r:r + UNIT, :] = stacked.T.astype(BF16)
    for c in range(chunks):
        part = jnp.concatenate(
            [rs_ref[d * share + c * seg:d * share + (c + 1) * seg, :] for d in order], axis=0
        )
        sketch_scr[c] = part.astype(F32).T.astype(BF16)
    for load in loads[4:]:
        load.wait()

    @pl.loop(0, blocks)
    def _(b):
        cl = pl.ds(pl.multiple_of(b * UNIT, UNIT), UNIT)
        right_scr[:, cl] = stack_parts(rd_ref[:, cl], ra_ref[:, cl], RIGHT_PARTS).astype(BF16)

    def tiles(c, low, high, last):
        own = [pl.ds(d * share + c * seg, seg) for d in order]

        @pl.loop(low, high)
        def _(b):
            cl = pl.ds(pl.multiple_of(b * UNIT, UNIT), UNIT)
            left = jnp.concatenate([left_scr[sl, :] for sl in own], axis=0)
            freq = jnp.concatenate([freq_scr[sl, :] for sl in own], axis=0)
            numer = jnp.dot(left, right_scr[:, cl], preferred_element_type=F32)
            gap = jnp.concatenate([freq] * (UNIT // 128), axis=1) - rf_ref[:, cl] * total
            tile = (numer / gap).astype(BF16)
            for p, sl in enumerate(own):
                tile_ref[sl, cl] = tile[p * seg:(p + 1) * seg, :]
            row_acc[c] += jnp.dot(tile, cs_ref[cl, :], preferred_element_type=F32)
            part = jnp.dot(sketch_scr[c], tile, preferred_element_type=F32)
            if last:
                col_part[cl, :] = (col_acc[b] + part).T
            else:
                col_acc[b] += part

    def bit(s):
        return lax.rem(deep // (1 << s), 2)

    def segment(s):
        start, size = 0, UNIT
        for t in range(s):
            size = size // 2
            start = start + bit(t) * size
        return start, size

    def halve(c, s):
        start, size = segment(s)
        half = size // 2
        src = pl.ds(pl.multiple_of(start + (1 - bit(s)) * half, 8), half)
        slot = pl.ds(UNIT - size, half)
        return send(
            row_acc.at[c, src], row_buf.at[c, slot], row_sem.at[c], s,
            {"right": deep + (1 - 2 * bit(s)) * (1 << s)},
        )

    def settle(c, s, copy):
        copy.wait()
        start, size = segment(s)
        half = size // 2
        mine = pl.ds(pl.multiple_of(start + bit(s) * half, 8), half)
        value = row_acc[c, mine, :] + row_buf[c, UNIT - size:UNIT - size + half, :]
        if s == steps - 1:
            row_out[c * seg:(c + 1) * seg, :] = value
            return None
        row_acc[c, mine, :] = value
        return halve(c, s + 1)

    half_cols, quarter = cols // 2, cols // 4
    piece = quarter // chips

    def pair_start(h):
        copies = []
        for o in range(1, chips + 1):
            peer = lax.rem(chip + o, chips)
            at = pl.multiple_of(peer * piece, 8)
            src = pl.ds(h * half_cols + (1 - core) * quarter + at, piece)
            copies.append(
                send(
                    col_part.at[src], core_buf.at[h, pl.ds(at, piece)], core_sem.at[h], o - 1,
                    sibling,
                )
            )
        return copies

    def pair_end(h, copies):
        sent = []
        for o in range(1, chips + 1):
            peer = lax.rem(chip + o, chips)
            at = pl.multiple_of(peer * piece, 8)
            copies[o - 1].wait()
            dst = pl.ds(at, piece)
            half_buf[h, dst, :] = (
                col_part[pl.ds(h * half_cols + core * quarter + at, piece), :]
                + core_buf[h, dst, :]
            )
            if o < chips:
                sent.append(
                    send(
                        half_buf.at[h, dst], chip_buf.at[h, o - 1], chip_sem.at[h], o - 1,
                        {"left": peer * 2 + core},
                    )
                )
        return sent

    def chip_end(h, copies):
        value = half_buf[h, pl.ds(pl.multiple_of(chip * piece, 8), piece), :]
        for o in range(1, chips):
            copies[o - 1].wait()
            value = value + chip_buf[h, o - 1]
        col_out[h * piece:(h + 1) * piece, :] = value

    z = [None] * chunks
    mid = blocks // 2
    early = chunks // 2
    for c in range(early):
        tiles(c, 0, blocks, False)
        if c == 0:
            greet_end(chips, deeps)
        z[c] = halve(c, 0)
    for c in range(early, chunks):
        tiles(c, 0, mid, c == chunks - 1)
        if c == early:
            z[0] = settle(0, 0, z[0])
    pair = pair_start(0)
    for c in range(early, chunks):
        tiles(c, mid, blocks, c == chunks - 1)
        z[c] = halve(c, 0)
        if c == early:
            chip_first = pair_end(0, pair)
            for e in range(1, early):
                z[e] = settle(e, 0, z[e])
    pair = pair_start(1)
    chip_second = pair_end(1, pair)
    for s in range(1, steps):
        for c in range(early):
            z[c] = settle(c, s, z[c])
    for s in range(steps):
        for c in range(early, chunks):
            z[c] = settle(c, s, z[c])
        if s == 0:
            chip_end(0, chip_first)
    chip_end(1, chip_second)


def build(lf, rf, ld, la, rd, ra, cs, rs, total):
    rows, cols = lf.shape[0], rf.shape[0]
    ports, width = ld.shape[0], cs.shape[1]
    chips, deeps = lax.axis_size("left") // 2, lax.axis_size("right")
    steps = deeps.bit_length() - 1
    chunks, blocks = rows // UNIT, cols // UNIT
    piece = cols // 4 // chips
    args = (lf[None, :], rf[None, :], ld, la, rd, ra, cs, rs)
    sems = lambda n, m: pltpu.SemaphoreType.DMA((n, 2, m))
    return pl.pallas_call(
        functools.partial(tiles_kernel, float(total), chips, deeps),
        in_specs=[pl.BlockSpec(memory_space=pltpu.HBM)] * 8,
        out_specs=vmem_specs(3),
        out_shape=[
            jax.ShapeDtypeStruct((rows, cols), BF16),
            jax.ShapeDtypeStruct((rows // deeps, width), F32),
            jax.ShapeDtypeStruct((2 * piece, width), F32),
        ],
        scratch_shapes=[pltpu.VMEM(x.shape, x.dtype) for x in args] + [
            pltpu.VMEM((rows, 256), BF16),
            pltpu.VMEM((256, cols), BF16),
            pltpu.VMEM((chunks, width, UNIT), BF16),
            pltpu.VMEM((rows, 128), F32),
            pltpu.VMEM((chunks, UNIT, width), F32),
            pltpu.VMEM((blocks, width, UNIT), F32),
            pltpu.VMEM((cols, width), F32),
            pltpu.VMEM((chunks, UNIT, width), F32),
            pltpu.VMEM((2, cols // 4, width), F32),
            pltpu.VMEM((2, cols // 4, width), F32),
            pltpu.VMEM((2, chips - 1, piece, width), F32),
            pltpu.SemaphoreType.DMA((8,)),
            sems(chunks, steps), sems(2, chips), sems(2, chips - 1),
        ],
        compiler_params=pltpu.CompilerParams(
            collective_id=1, has_side_effects=True, vmem_limit_bytes=44 << 20
        ),
        name="tiles",
    )(*args)


BLOCK = 64
GROUP = 8


def triangle(width):
    return [(i, j) for i in range(width // 128) for j in range(i, width // 128)]


def store_gram(dst, m, gram):
    for n, (i, j) in enumerate(triangle(gram.shape[0])):
        dst[m, n * 128:(n + 1) * 128, :] = gram[i * 128:(i + 1) * 128, j * 128:(j + 1) * 128]


def factor(shifted, t_ref, out_ref, work):
    width = out_ref.shape[-1]
    row_id = lax.broadcasted_iota(jnp.int32, (width, width), 0)
    col_id = lax.broadcasted_iota(jnp.int32, (width, width), 1)
    eye = (row_id == col_id).astype(F32)
    for m in range(2):
        work[m, :, 0:width] = jnp.zeros((width, width), F32)
        for n, (i, j) in enumerate(triangle(width)):
            work[m, i * 128:(i + 1) * 128, j * 128:(j + 1) * 128] = t_ref[m, n * 128:(n + 1) * 128, :]
        if shifted:
            gram = work[m, :, 0:width]
            trace = jnp.sum(jnp.sum(gram * eye, axis=1, keepdims=True), axis=0, keepdims=True)
            work[m, :, 0:width] = gram + (1e-05 * trace / width) * eye
        work[m, :, width:] = eye
    brow = lax.broadcasted_iota(jnp.int32, (BLOCK, BLOCK), 0)
    bcol = lax.broadcasted_iota(jnp.int32, (BLOCK, BLOCK), 1)
    small_eye = (brow == bcol).astype(F32)
    low = lax.broadcasted_iota(jnp.int32, (BLOCK, 2 * BLOCK), 0)
    for k in range(0, width, BLOCK):
        pairs = [
            jnp.concatenate([work[m, k:k + BLOCK, k:k + BLOCK], small_eye], axis=1)
            for m in range(2)
        ]
        for base in range(0, BLOCK, GROUP):
            copies = [
                [jnp.broadcast_to(pair[:, s:s + 1], low.shape) for s in range(base, base + GROUP)]
                for pair in pairs
            ]
            for i in range(GROUP):
                s = base + i
                for m in range(2):
                    wide = copies[m]
                    top = 1.0 / wide[i][s:s + 1, :]
                    column = jnp.where(low > s, wide[i], 0.0)
                    for j in range(i + 1, GROUP):
                        wide[j] = wide[j] - column * (wide[j][s:s + 1, :] * top)
                    pairs[m] = pairs[m] - column * (pairs[m][s:s + 1, :] * top)
        lo = k + BLOCK
        start, stop = k // 128 * 128, width + (lo + 127) // 128 * 128
        solved = []
        for m in range(2):
            diag = jnp.sum(pairs[m][:, 0:BLOCK] * small_eye, axis=1, keepdims=True)
            inv = pairs[m][:, BLOCK:] * lax.rsqrt(diag)
            solved.append(
                jnp.dot(
                    inv, work[m, k:lo, start:stop], precision=precise,
                    preferred_element_type=F32,
                )
            )
        for m in range(2):
            out_ref[m, k:lo, 0:stop - width] = solved[m][:, width - start:]
            if stop < 2 * width:
                out_ref[m, k:lo, stop - width:] = jnp.zeros((BLOCK, 2 * width - stop), F32)
        if lo < width:
            deltas = [tdot(rows[:, lo - start:width - start], rows, precise) for rows in solved]
            for m in range(2):
                work[m, lo:, start:stop] = work[m, lo:, start:stop] - deltas[m]


def apply_inverse(basis, inverse, precision):
    return lax.dot_general(
        basis, inverse, (((1,), (1,)), ((), ())), precision=precision, preferred_element_type=F32
    )


def vmem_specs(n):
    return [pl.BlockSpec(memory_space=pltpu.VMEM)] * n


def sem_pair(n):
    return pltpu.SemaphoreType.DMA((2, n))


def comm_params(cid):
    return pltpu.CompilerParams(
        collective_id=cid, has_side_effects=True, vmem_limit_bytes=20 << 20
    )


def reduce_kernel(
    chips, deeps, x_ref, out_ref,
    core_buf, half_buf, chip_buf, deep_buf,
    core_sem, chip_sem, deep_sem, back_sem, last_sem,
):
    me, deep, core, chip = places()
    greet(chips, deeps)
    half, piece = core_buf.shape[0], chip_buf.shape[1]
    sibling = {"left": chip * 2 + (1 - core)}
    send(x_ref.at[pl.ds((1 - core) * half, half)], core_buf, core_sem, 0, sibling).wait()
    half_buf[...] = x_ref[pl.ds(core * half, half), :] + core_buf[...]
    copies = []
    for o in range(1, chips):
        peer = lax.rem(chip + o, chips)
        copies.append(
            send(
                half_buf.at[pl.ds(peer * piece, piece)], chip_buf.at[o - 1], chip_sem, o - 1,
                {"left": peer * 2 + core},
            )
        )
    part = half_buf[pl.ds(chip * piece, piece), :]
    for o in range(1, chips):
        copies[o - 1].wait()
        part = part + chip_buf[o - 1]
    deep_buf[deep] = part
    copies = []
    for o in range(1, deeps):
        copies.append(
            send(
                deep_buf.at[deep], deep_buf.at[deep], deep_sem, o - 1,
                {"right": lax.rem(deep + o, deeps)},
            )
        )
    for copy in copies:
        copy.wait()
    part = deep_buf[0]
    for d in range(1, deeps):
        part = part + deep_buf[d]
    mine = pl.ds(core * half + chip * piece, piece)
    out_ref[mine, :] = part
    copies = []
    for o in range(1, chips):
        copies.append(
            send(
                out_ref.at[mine], out_ref.at[mine], back_sem, o - 1,
                chip_peer(chip, core, o, chips),
            )
        )
    for copy in copies:
        copy.wait()
    own = pl.ds(core * half, half)
    send(out_ref.at[own], out_ref.at[own], last_sem, 0, sibling).wait()


def reduce_all(x, cid):
    chips, deeps = lax.axis_size("left") // 2, lax.axis_size("right")
    rows, width = x.shape
    half, piece = rows // 2, rows // 2 // chips
    return pl.pallas_call(
        functools.partial(reduce_kernel, chips, deeps),
        in_specs=vmem_specs(1),
        out_specs=vmem_specs(1)[0],
        out_shape=jax.ShapeDtypeStruct(x.shape, F32),
        scratch_shapes=[
            pltpu.VMEM((half, width), F32),
            pltpu.VMEM((half, width), F32),
            pltpu.VMEM((chips - 1, piece, width), F32),
            pltpu.VMEM((deeps, piece, width), F32),
            sem_pair(1), sem_pair(chips - 1), sem_pair(deeps - 1), sem_pair(chips - 1),
            sem_pair(1),
        ],
        compiler_params=comm_params(cid),
        name="reduce",
    )(x)


def sum_all(chips, deeps, x, total, core_buf, half_buf, chip_buf, deep_buf, sems):
    me, deep, core, chip = places()
    core_sem, chip_sem, deep_sem, back_sem, last_sem = sems
    piece = chip_buf.shape[1]
    sibling = {"left": chip * 2 + (1 - core)}
    part_of = lambda q: pl.ds(pl.multiple_of(q * piece, 8), piece)
    firsts = []
    for o in range(1, chips + 1):
        q = part_of(lax.rem(chip + o, chips))
        firsts.append(send(x.at[1 - core, q], core_buf.at[q], core_sem, o - 1, sibling))
    copies = []
    for o in range(1, chips + 1):
        peer = lax.rem(chip + o, chips)
        q = part_of(peer)
        firsts[o - 1].wait()
        half_buf[q, :] = x[core, q, :] + core_buf[q, :]
        if o < chips:
            copies.append(
                send(half_buf.at[q], chip_buf.at[o - 1], chip_sem, o - 1, {"left": peer * 2 + core})
            )
    mine = part_of(chip)
    part = half_buf[mine, :]
    for o in range(1, chips):
        copies[o - 1].wait()
        part = part + chip_buf[o - 1]
    deep_buf[deep] = part
    copies = []
    for o in range(1, deeps):
        copies.append(
            send(
                deep_buf.at[deep], deep_buf.at[deep], deep_sem, o - 1,
                {"right": lax.rem(deep + o, deeps)},
            )
        )
    for copy in copies:
        copy.wait()
    part = deep_buf[0]
    for d in range(1, deeps):
        part = part + deep_buf[d]
    total[core, mine, :] = part
    copies = []
    for o in range(1, chips):
        copies.append(
            send(
                total.at[core, mine], total.at[core, mine], back_sem, o - 1,
                chip_peer(chip, core, o, chips),
            )
        )
    lasts = [send(total.at[core, mine], total.at[core, mine], last_sem, 0, sibling)]
    for o in range(1, chips):
        copies[o - 1].wait()
        q = part_of(lax.rem(chip + chips - o, chips))
        lasts.append(send(total.at[core, q], total.at[core, q], last_sem, o, sibling))
    for copy in lasts:
        copy.wait()


def middle_kernel(
    chips, deeps, row_ref, col_ref, row_out, col_out, inv_out,
    x_buf, total, core_buf, half_buf, chip_buf, deep_buf, work, inv1, inv2,
    core_sem, chip_sem, deep_sem, back_sem, last_sem, row_sem, col_sem, pair_sem,
):
    me, deep, core, chip = places()
    greet(chips, deeps)
    share, block = row_ref.shape[0], col_ref.shape[0] // 2
    sibling = {"left": chip * 2 + (1 - core)}
    quarter = chips * block
    cols_at = lambda h, c: pl.multiple_of(h * 2 * quarter + core * quarter + c * block, 8)

    def reduce_round(n, row, col):
        store_gram(x_buf.at[n], 0, tdot(row, row, precise))
        store_gram(x_buf.at[n], 1, tdot(col, col, precise))
        sum_all(
            chips, deeps, x_buf.at[n], total.at[n], core_buf.at[n], half_buf.at[n],
            chip_buf.at[n], deep_buf.at[n],
            [s.at[n] for s in (core_sem, chip_sem, deep_sem, back_sem, last_sem)],
        )

    def row_half(n):
        half = share // 2
        src = pl.ds(n * half, half)
        dst = pl.ds(pl.multiple_of(deep * share + n * half, 8), half)
        return [
            send(
                row_ref.at[src], row_out.at[dst], row_sem.at[n], o - 1,
                {"right": lax.rem(deep + o, deeps)},
            )
            for o in range(1, deeps)
        ]

    reduce_round(0, row_ref[...], col_ref[...])
    row_copies = row_half(0)
    col_copies = [
        send(
            col_ref.at[pl.ds(h * block, block)], col_out.at[pl.ds(cols_at(h, chip), block)],
            col_sem.at[h], o - 1, chip_peer(chip, core, o, chips),
        )
        for h in range(2)
        for o in range(1, chips)
    ]
    row_out[pl.ds(pl.multiple_of(deep * share, 8), share), :] = row_ref[...]
    for h in range(2):
        col_out[pl.ds(cols_at(h, chip), block), :] = col_ref[h * block:(h + 1) * block, :]
    factor(True, total.at[0], inv1, work)
    row_own = apply_inverse(row_ref[...], inv1[0], precise)
    col_own = apply_inverse(col_ref[...], inv1[1], precise)
    for copy in col_copies:
        copy.wait()
    pair = []
    for h in range(2):
        own = pl.ds(cols_at(h, 0), quarter)
        pair.append(send(col_out.at[own], col_out.at[own], pair_sem, h, sibling))
    reduce_round(1, row_own, col_own)
    row_copies += row_half(1)
    factor(False, total.at[1], inv2, work)
    for m in range(2):
        inv_out[m] = jnp.dot(inv2[m], inv1[m], precision=precise, preferred_element_type=F32)
    for copy in pair + row_copies:
        copy.wait()


def middle(row_own, col_own):
    chips, deeps = lax.axis_size("left") // 2, lax.axis_size("right")
    width = row_own.shape[1]
    high = 128 * len(triangle(width))
    piece = high // chips
    sems = lambda n: pltpu.SemaphoreType.DMA((2, 2, n))
    return pl.pallas_call(
        functools.partial(middle_kernel, chips, deeps),
        in_specs=vmem_specs(2),
        out_specs=vmem_specs(3),
        out_shape=[
            jax.ShapeDtypeStruct((row_own.shape[0] * deeps, width), F32),
            jax.ShapeDtypeStruct((col_own.shape[0] * chips * 2, width), F32),
            jax.ShapeDtypeStruct((2, width, width), F32),
        ],
        scratch_shapes=[
            pltpu.VMEM((2, 2, high, 128), F32),
            pltpu.VMEM((2, 2, high, 128), F32),
            pltpu.VMEM((2, high, 128), F32),
            pltpu.VMEM((2, high, 128), F32),
            pltpu.VMEM((2, chips - 1, piece, 128), F32),
            pltpu.VMEM((2, deeps, piece, 128), F32),
            pltpu.VMEM((2, width, 2 * width), F32),
            pltpu.VMEM((2, width, width), F32),
            pltpu.VMEM((2, width, width), F32),
            sems(chips), sems(chips - 1), sems(deeps - 1), sems(chips - 1), sems(chips),
            sems(deeps - 1), sems(chips - 1), sem_pair(2),
        ],
        compiler_params=comm_params(2),
        name="middle",
    )(row_own, col_own)


def project_kernel(lf_ref, tile_ref, v_ref, q_ref, out_ref):
    @pl.when(pl.program_id(0) == 0)
    def _():
        out_ref[...] = jnp.zeros_like(out_ref)

    applied = jnp.dot(tile_ref[...], v_ref[...], preferred_element_type=F32)
    freq = jnp.broadcast_to(lf_ref[...], (128, lf_ref.shape[1])).T[:, 0:1]
    both = jnp.concatenate([applied, applied * freq], axis=1)
    both_hi = both.astype(BF16)
    both_lo = (both - both_hi.astype(F32)).astype(BF16)
    q = q_ref[...].T
    q_hi = q.astype(BF16)
    q_lo = (q - q_hi.astype(F32)).astype(BF16)
    out_ref[...] += jnp.dot(
        jnp.concatenate([q_hi, q_hi, q_lo], axis=1),
        jnp.concatenate([both_hi, both_lo, both_hi], axis=0),
        preferred_element_type=F32,
    )


def project(lf, tile, v, q):
    rows, cols = tile.shape
    width = v.shape[1]
    block = 256
    return pl.pallas_call(
        project_kernel,
        grid=(rows // block,),
        in_specs=[
            pl.BlockSpec((1, block), lambda i: (0, i)),
            pl.BlockSpec((block, cols), lambda i: (i, 0)),
            pl.BlockSpec((cols, width), lambda i: (0, 0)),
            pl.BlockSpec((block, width), lambda i: (i, 0)),
        ],
        out_specs=pl.BlockSpec((width, 2 * width), lambda i: (0, 0)),
        out_shape=jax.ShapeDtypeStruct((width, 2 * width), F32),
        compiler_params=pltpu.CompilerParams(
            dimension_semantics=("arbitrary",), vmem_limit_bytes=32 << 20
        ),
        name="project",
    )(lf[None, :], tile, v, q)


def body(lf, rf, ld, la, rd, ra, cs, rs):
    rows, cols = lf.shape[0], rf.shape[0]
    width = cs.shape[1]
    left_n, right_n = lax.axis_size("left"), lax.axis_size("right")
    total_rows, total_cols = rows * left_n, cols * right_n
    tile, row_own, col_own = build(lf, rf, ld, la, rd, ra, cs, rs, total_rows)
    row_full, col_full, inverse = middle(row_own, col_own)
    row_part = apply_inverse(row_own, inverse[0], precise)
    row_full = apply_inverse(row_full, inverse[0], precise)
    col_full = apply_inverse(col_full, inverse[1], precise)
    col_round = col_full.astype(BF16)
    reduced = project(lf, tile, col_round, row_full)
    low_rank = jnp.dot(
        lax.dot_general(row_full, ld, (((0,), (1,)), ((), ())), precision=precise),
        jnp.dot(ra, col_round.astype(F32), precision=precise) * (1.0 / total_rows),
        precision=precise,
    )
    reduced = jnp.concatenate([reduced[:, :width], reduced[:, width:] + low_rank], axis=0)
    reduced = reduce_all(reduced, 3)
    return (
        row_part * math.sqrt(total_rows),
        col_full * math.sqrt(total_cols),
        reduced[:width],
        reduced[width:],
    )


def solution(mesh):
    in_specs = (
        P("left"), P("right"), P(None, "left"), P(None, "left"),
        P(None, "right"), P(None, "right"), P("right", None), P("left", None),
    )
    out_specs = (P(("left", "right"), None), P("right", None), P(), P())
    return jax.shard_map(body, mesh=mesh, in_specs=in_specs, out_specs=out_specs, check_vma=False)
```

```python
import functools
import math

import jax
import jax.numpy as jnp
from jax import lax
from jax.experimental import pallas as pl
from jax.experimental.pallas import tpu as pltpu
from jax.sharding import PartitionSpec as P

precise = lax.Precision.HIGHEST
F32 = jnp.float32
BF16 = jnp.bfloat16
LEFT_PARTS = (0, 0, 1, 0, 1, 2)
RIGHT_PARTS = (0, 1, 0, 2, 1, 0)


def tdot(a, b, precision=None):
    return lax.dot_general(
        a, b, (((0,), (0,)), ((), ())), precision=precision, preferred_element_type=F32
    )


def split3(x):
    one = x.astype(BF16).astype(F32)
    rest = x - one
    two = rest.astype(BF16).astype(F32)
    return (one, two, (rest - two).astype(BF16).astype(F32))


def stack_parts(first, second, order):
    a, b = split3(first), split3(second)
    pieces = [a[p] for p in order] + [b[p] for p in order]
    pad = jnp.zeros((256 - 12 * first.shape[0], first.shape[1]), F32)
    return jnp.concatenate(pieces + [pad], axis=0)


UNIT = 512


def places():
    me, deep = lax.axis_index("left"), lax.axis_index("right")
    core = lax.rem(me, 2)
    return me, deep, core, me // 2


def chip_peer(chip, core, offset, chips):
    return {"left": lax.rem(chip + offset, chips) * 2 + core}


def peers_of(chips, deeps):
    me, deep, core, chip = places()
    peers = [{"left": chip * 2 + (1 - core)}]
    peers += [chip_peer(chip, core, o, chips) for o in range(1, chips)]
    peers += [{"right": lax.rem(deep + o, deeps)} for o in range(1, deeps)]
    return peers


def greet_start(chips, deeps):
    barrier = pltpu.get_barrier_semaphore()
    for peer in peers_of(chips, deeps):
        pl.semaphore_signal(
            barrier, inc=1, device_id=peer, device_id_type=pl.DeviceIdType.MESH
        )


def greet_end(chips, deeps):
    pl.semaphore_wait(pltpu.get_barrier_semaphore(), chips + deeps - 1)


def greet(chips, deeps):
    greet_start(chips, deeps)
    greet_end(chips, deeps)


def send(src, dst, sems, slot, peer):
    copy = pltpu.make_async_remote_copy(
        src_ref=src,
        dst_ref=dst,
        send_sem=sems.at[0, slot],
        recv_sem=sems.at[1, slot],
        device_id=peer,
        device_id_type=pl.DeviceIdType.MESH,
    )
    copy.start()
    return copy


def reversed_bits(p, bits):
    return sum(((p >> i) & 1) << (bits - 1 - i) for i in range(bits))


def images(
    total, chips, deeps, anys, refs, tile_ref, row_out, col_out,
    left_scr, right_scr, sketch_scr, freq_scr, row_acc, col_acc, col_part,
    row_buf, core_buf, chip_buf,
    in_sem, row_sem, core_sem, chip_sem,
):
    lf_any, rf_any, ld_any, la_any, rd_any, ra_any, cs_any, rs_any = anys
    lf_ref, rf_ref, ld_ref, la_ref, rd_ref, ra_ref, cs_ref, rs_ref = refs
    me, deep, core, chip = places()
    rows, cols = tile_ref.shape
    width = row_out.shape[1]
    chunks, blocks = rows // UNIT, cols // UNIT
    steps = deeps.bit_length() - 1
    share, seg = rows // deeps, UNIT // deeps
    order = [reversed_bits(p, steps) for p in range(deeps)]
    sibling = {"left": chip * 2 + (1 - core)}
    loads = [
        pltpu.make_async_copy(src, dst, in_sem.at[n])
        for n, (src, dst) in enumerate(
            [
                (lf_any, lf_ref), (la_any, la_ref), (ld_any, ld_ref), (rs_any, rs_ref),
                (rf_any, rf_ref), (rd_any, rd_ref), (ra_any, ra_ref), (cs_any, cs_ref),
            ]
        )
    ]
    for load in loads:
        load.start()
    greet_start(chips, deeps)

    @pl.loop(0, chunks)
    def _(c):
        row_acc[c] = jnp.zeros((UNIT, width), F32)

    @pl.loop(0, blocks)
    def _(b):
        col_acc[b] = jnp.zeros((width, UNIT), F32)

    for load in loads[:4]:
        load.wait()
    for r in range(0, rows, UNIT):
        wide = jnp.broadcast_to(lf_ref[:, r:r + UNIT] * total, (128, UNIT))
        freq_scr[r:r + UNIT, :] = wide.T
        stacked = stack_parts(la_ref[:, r:r + UNIT], -ld_ref[:, r:r + UNIT], LEFT_PARTS)
        left_scr[r:r + UNIT, :] = stacked.T.astype(BF16)
    for c in range(chunks):
        part = jnp.concatenate(
            [rs_ref[d * share + c * seg:d * share + (c + 1) * seg, :] for d in order], axis=0
        )
        sketch_scr[c] = part.astype(F32).T.astype(BF16)
    for load in loads[4:]:
        load.wait()

    @pl.loop(0, blocks)
    def _(b):
        cl = pl.ds(pl.multiple_of(b * UNIT, UNIT), UNIT)
        right_scr[:, cl] = stack_parts(rd_ref[:, cl], ra_ref[:, cl], RIGHT_PARTS).astype(BF16)

    def tiles(c, low, high, last):
        own = [pl.ds(d * share + c * seg, seg) for d in order]

        @pl.loop(low, high)
        def _(b):
            cl = pl.ds(pl.multiple_of(b * UNIT, UNIT), UNIT)
            left = jnp.concatenate([left_scr[sl, :] for sl in own], axis=0)
            freq = jnp.concatenate([freq_scr[sl, :] for sl in own], axis=0)
            numer = jnp.dot(left, right_scr[:, cl], preferred_element_type=F32)
            gap = jnp.concatenate([freq] * (UNIT // 128), axis=1) - rf_ref[:, cl] * total
            tile = (numer / gap).astype(BF16)
            for p, sl in enumerate(own):
                tile_ref[sl, cl] = tile[p * seg:(p + 1) * seg, :]
            row_acc[c] += jnp.dot(tile, cs_ref[cl, :], preferred_element_type=F32)
            part = jnp.dot(sketch_scr[c], tile, preferred_element_type=F32)
            if last:
                col_part[cl, :] = (col_acc[b] + part).T
            else:
                col_acc[b] += part

    def bit(s):
        return lax.rem(deep // (1 << s), 2)

    def segment(s):
        start, size = 0, UNIT
        for t in range(s):
            size = size // 2
            start = start + bit(t) * size
        return start, size

    def halve(c, s):
        start, size = segment(s)
        half = size // 2
        src = pl.ds(pl.multiple_of(start + (1 - bit(s)) * half, 8), half)
        slot = pl.ds(UNIT - size, half)
        return send(
            row_acc.at[c, src], row_buf.at[c, slot], row_sem.at[c], s,
            {"right": deep + (1 - 2 * bit(s)) * (1 << s)},
        )

    def settle(c, s, copy):
        copy.wait()
        start, size = segment(s)
        half = size // 2
        mine = pl.ds(pl.multiple_of(start + bit(s) * half, 8), half)
        value = row_acc[c, mine, :] + row_buf[c, UNIT - size:UNIT - size + half, :]
        if s == steps - 1:
            row_out[c * seg:(c + 1) * seg, :] = value
            return None
        row_acc[c, mine, :] = value
        return halve(c, s + 1)

    half_cols, quarter = cols // 2, cols // 4
    piece = quarter // chips

    def pair_start(h):
        copies = []
        for o in range(1, chips + 1):
            peer = lax.rem(chip + o, chips)
            at = pl.multiple_of(peer * piece, 8)
            src = pl.ds(h * half_cols + (1 - core) * quarter + at, piece)
            copies.append(
                send(
                    col_part.at[src], core_buf.at[h, pl.ds(at, piece)], core_sem.at[h], o - 1,
                    sibling,
                )
            )
        return copies

    def pair_end(h, copies):
        sent = []
        for o in range(1, chips + 1):
            peer = lax.rem(chip + o, chips)
            at = pl.multiple_of(peer * piece, 8)
            copies[o - 1].wait()
            dst = pl.ds(at, piece)
            core_buf[h, dst, :] += col_part[pl.ds(h * half_cols + core * quarter + at, piece), :]
            if o < chips:
                sent.append(
                    send(
                        core_buf.at[h, dst], chip_buf.at[h, o - 1], chip_sem.at[h], o - 1,
                        {"left": peer * 2 + core},
                    )
                )
        return sent

    def chip_end(h, copies):
        value = core_buf[h, pl.ds(pl.multiple_of(chip * piece, 8), piece), :]
        for o in range(1, chips):
            copies[o - 1].wait()
            value = value + chip_buf[h, o - 1]
        col_out[h * piece:(h + 1) * piece, :] = value

    z = [None] * chunks
    mid = blocks // 2
    early = chunks // 2
    for c in range(early):
        tiles(c, 0, blocks, False)
        if c == 0:
            greet_end(chips, deeps)
        z[c] = halve(c, 0)
    for c in range(early, chunks):
        tiles(c, 0, mid, c == chunks - 1)
        if c == early:
            z[0] = settle(0, 0, z[0])
    pair = pair_start(0)
    for c in range(early, chunks):
        tiles(c, mid, blocks, c == chunks - 1)
        z[c] = halve(c, 0)
        if c == early:
            chip_first = pair_end(0, pair)
            for e in range(1, early):
                z[e] = settle(e, 0, z[e])
    pair = pair_start(1)
    chip_second = pair_end(1, pair)
    for s in range(1, steps):
        for c in range(early):
            z[c] = settle(c, s, z[c])
    for s in range(steps):
        for c in range(early, chunks):
            z[c] = settle(c, s, z[c])
        if s == 0:
            chip_end(0, chip_first)
    chip_end(1, chip_second)


BLOCK = 64
GROUP = 8


def triangle(width):
    return [(i, j) for i in range(width // 128) for j in range(i, width // 128)]


def store_gram(dst, m, gram):
    for n, (i, j) in enumerate(triangle(gram.shape[0])):
        dst[m, n * 128:(n + 1) * 128, :] = gram[i * 128:(i + 1) * 128, j * 128:(j + 1) * 128]


def factor(shifted, t_ref, out_ref, work):
    width = out_ref.shape[-1]
    row_id = lax.broadcasted_iota(jnp.int32, (width, width), 0)
    col_id = lax.broadcasted_iota(jnp.int32, (width, width), 1)
    eye = (row_id == col_id).astype(F32)
    for m in range(2):
        work[m, :, 0:width] = jnp.zeros((width, width), F32)
        for n, (i, j) in enumerate(triangle(width)):
            work[m, i * 128:(i + 1) * 128, j * 128:(j + 1) * 128] = t_ref[m, n * 128:(n + 1) * 128, :]
        if shifted:
            gram = work[m, :, 0:width]
            trace = jnp.sum(jnp.sum(gram * eye, axis=1, keepdims=True), axis=0, keepdims=True)
            work[m, :, 0:width] = gram + (1e-05 * trace / width) * eye
        work[m, :, width:] = eye
    brow = lax.broadcasted_iota(jnp.int32, (BLOCK, BLOCK), 0)
    bcol = lax.broadcasted_iota(jnp.int32, (BLOCK, BLOCK), 1)
    small_eye = (brow == bcol).astype(F32)
    low = lax.broadcasted_iota(jnp.int32, (BLOCK, 2 * BLOCK), 0)
    for k in range(0, width, BLOCK):
        pairs = [
            jnp.concatenate([work[m, k:k + BLOCK, k:k + BLOCK], small_eye], axis=1)
            for m in range(2)
        ]
        for base in range(0, BLOCK, GROUP):
            copies = [
                [jnp.broadcast_to(pair[:, s:s + 1], low.shape) for s in range(base, base + GROUP)]
                for pair in pairs
            ]
            for i in range(GROUP):
                s = base + i
                for m in range(2):
                    wide = copies[m]
                    top = 1.0 / wide[i][s:s + 1, :]
                    column = jnp.where(low > s, wide[i], 0.0)
                    for j in range(i + 1, GROUP):
                        wide[j] = wide[j] - column * (wide[j][s:s + 1, :] * top)
                    pairs[m] = pairs[m] - column * (pairs[m][s:s + 1, :] * top)
        lo = k + BLOCK
        start, stop = k // 128 * 128, width + (lo + 127) // 128 * 128
        solved = []
        for m in range(2):
            diag = jnp.sum(pairs[m][:, 0:BLOCK] * small_eye, axis=1, keepdims=True)
            inv = pairs[m][:, BLOCK:] * lax.rsqrt(diag)
            solved.append(
                jnp.dot(
                    inv, work[m, k:lo, start:stop], precision=precise,
                    preferred_element_type=F32,
                )
            )
        for m in range(2):
            out_ref[m, k:lo, 0:stop - width] = solved[m][:, width - start:]
            if stop < 2 * width:
                out_ref[m, k:lo, stop - width:] = jnp.zeros((BLOCK, 2 * width - stop), F32)
        if lo < width:
            deltas = [tdot(rows[:, lo - start:width - start], rows, precise) for rows in solved]
            for m in range(2):
                work[m, lo:, start:stop] = work[m, lo:, start:stop] - deltas[m]


def apply_inverse(basis, inverse, precision):
    return lax.dot_general(
        basis, inverse, (((1,), (1,)), ((), ())), precision=precision, preferred_element_type=F32
    )


def sum_all(chips, deeps, x, total, core_buf, chip_buf, deep_buf, sems):
    me, deep, core, chip = places()
    core_sem, chip_sem, deep_sem, back_sem, last_sem = sems
    piece = chip_buf.shape[1]
    sibling = {"left": chip * 2 + (1 - core)}
    part_of = lambda q: pl.ds(pl.multiple_of(q * piece, 8), piece)
    firsts = []
    for o in range(1, chips + 1):
        q = part_of(lax.rem(chip + o, chips))
        firsts.append(send(x.at[1 - core, q], core_buf.at[q], core_sem, o - 1, sibling))
    copies = []
    for o in range(1, chips + 1):
        peer = lax.rem(chip + o, chips)
        q = part_of(peer)
        firsts[o - 1].wait()
        core_buf[q, :] += x[core, q, :]
        if o < chips:
            copies.append(
                send(core_buf.at[q], chip_buf.at[o - 1], chip_sem, o - 1, {"left": peer * 2 + core})
            )
    mine = part_of(chip)
    part = core_buf[mine, :]
    for o in range(1, chips):
        copies[o - 1].wait()
        part = part + chip_buf[o - 1]
    deep_buf[deep] = part
    copies = []
    for o in range(1, deeps):
        copies.append(
            send(
                deep_buf.at[deep], deep_buf.at[deep], deep_sem, o - 1,
                {"right": lax.rem(deep + o, deeps)},
            )
        )
    for copy in copies:
        copy.wait()
    part = deep_buf[0]
    for d in range(1, deeps):
        part = part + deep_buf[d]
    total[core, mine, :] = part
    copies = []
    for o in range(1, chips):
        copies.append(
            send(
                total.at[core, mine], total.at[core, mine], back_sem, o - 1,
                chip_peer(chip, core, o, chips),
            )
        )
    lasts = [send(total.at[core, mine], total.at[core, mine], last_sem, 0, sibling)]
    for o in range(1, chips):
        copies[o - 1].wait()
        q = part_of(lax.rem(chip + chips - o, chips))
        lasts.append(send(total.at[core, q], total.at[core, q], last_sem, o, sibling))
    for copy in lasts:
        copy.wait()


def whole_kernel(total, chips, deeps, *args):
    anys, (row_out, col_out, red_out), refs, rest = args[:8], args[8:11], args[11:19], args[19:]
    (
        tile_ref, row_own, col_own, left_scr, right_scr, sketch_scr, freq_scr, row_acc, col_acc,
        col_part, row_buf, core_buf, chip_buf, row_full, col_full,
        x_buf, t_buf, sum_core, sum_chip, sum_deep, x_last, t_last, last_core, last_chip, last_deep,
        work, inv1, inv2, in_sem, out_sem, row_sem, core_sem, chip_sem, row_all, col_all, pair_all,
        *sum_sems,
    ) = rest
    lf_ref, rf_ref, ld_ref, la_ref, rd_ref, ra_ref, cs_ref, rs_ref = refs
    me, deep, core, chip = places()
    sibling = {"left": chip * 2 + (1 - core)}
    images(
        total, chips, deeps, anys, refs, tile_ref, row_own, col_own,
        left_scr, right_scr, sketch_scr, freq_scr, row_acc, col_acc, col_part,
        row_buf, core_buf, chip_buf, in_sem, row_sem, core_sem, chip_sem,
    )
    rows, cols = tile_ref.shape
    width = row_out.shape[1]
    chunks, blocks = rows // UNIT, cols // UNIT
    share, block = rows // deeps, col_own.shape[0] // 2
    seg, quarter = share // chunks, chips * block
    cols_at = lambda h, c: pl.multiple_of(h * 2 * quarter + core * quarter + c * block, 8)

    def sum_round(n, row, col):
        store_gram(x_buf.at[n], 0, tdot(row, row, precise))
        store_gram(x_buf.at[n], 1, tdot(col, col, precise))
        sum_all(
            chips, deeps, x_buf.at[n], t_buf.at[n], sum_core.at[n], sum_chip.at[n],
            sum_deep.at[n], [s.at[n] for s in sum_sems],
        )

    def row_spread(c):
        src = pl.ds(c * seg, seg)
        dst = pl.ds(pl.multiple_of(deep * share + c * seg, 8), seg)
        return [
            send(
                row_own.at[src], row_full.at[dst], row_all.at[c], o - 1,
                {"right": lax.rem(deep + o, deeps)},
            )
            for o in range(1, deeps)
        ]

    row_copies = row_spread(0)
    sum_round(0, row_own[...], col_own[...])
    col_copies = [
        send(
            col_own.at[pl.ds(h * block, block)], col_full.at[pl.ds(cols_at(h, chip), block)],
            col_all.at[h], o - 1, chip_peer(chip, core, o, chips),
        )
        for h in range(2)
        for o in range(1, chips)
    ]
    for c in range(1, chunks - 1):
        row_copies += row_spread(c)
    row_full[pl.ds(pl.multiple_of(deep * share, 8), share), :] = row_own[...]
    for h in range(2):
        col_full[pl.ds(cols_at(h, chip), block), :] = col_own[h * block:(h + 1) * block, :]
    factor(True, t_buf.at[0], inv1, work)
    sum_round(
        1,
        apply_inverse(row_own[...], inv1[0], precise),
        apply_inverse(col_own[...], inv1[1], precise),
    )
    row_copies += row_spread(chunks - 1)
    for copy in col_copies:
        copy.wait()
    pair = []
    for h in range(2):
        own = pl.ds(cols_at(h, 0), quarter)
        pair.append(send(col_full.at[own], col_full.at[own], pair_all, h, sibling))
    factor(False, t_buf.at[1], inv2, work)
    for m in range(2):
        inv1[m] = jnp.dot(inv2[m], inv1[m], precision=precise, preferred_element_type=F32)
    row_out[...] = apply_inverse(row_own[...], inv1[0], precise)
    for copy in pair:
        copy.wait()
    work[0, 0:16, 0:width] = jnp.zeros((16, width), F32)

    @pl.loop(0, blocks)
    def _(b):
        cl = pl.ds(pl.multiple_of(b * UNIT, UNIT), UNIT)
        value = apply_inverse(col_full[cl, :], inv1[1], precise)
        col_part[cl, :] = value
        pltpu.make_async_copy(col_part.at[cl], col_out.at[cl], out_sem.at[b]).start()
        rounded = value.astype(BF16)
        cs_ref[cl, :] = rounded
        work[0, 0:16, 0:width] += jnp.dot(
            ra_ref[:, cl], rounded.astype(F32), precision=precise, preferred_element_type=F32
        )

    for copy in row_copies:
        copy.wait()
    low = work[0, 0:16, 0:width] * (1.0 / total)
    for m in range(2):
        for n in range(width // 128):
            x_last[m, n * width:(n + 1) * width, :] = jnp.zeros((width, 128), F32)

    @pl.loop(0, chunks)
    def _(c):
        sl = pl.ds(pl.multiple_of(c * UNIT, UNIT), UNIT)
        applied = jnp.dot(tile_ref[sl, :], cs_ref[...], preferred_element_type=F32)
        freq = jnp.concatenate([freq_scr[sl, :] * (1.0 / total)] * (width // 128), axis=1)
        both = jnp.concatenate([applied, applied * freq + tdot(ld_ref[:, sl], low, precise)], axis=1)
        both_hi = both.astype(BF16)
        both_lo = (both - both_hi.astype(F32)).astype(BF16)
        q = apply_inverse(row_full[sl, :], inv1[0], precise).T
        q_hi = q.astype(BF16)
        q_lo = (q - q_hi.astype(F32)).astype(BF16)
        part = jnp.dot(
            jnp.concatenate([q_hi, q_hi, q_lo], axis=1),
            jnp.concatenate([both_hi, both_lo, both_hi], axis=0),
            preferred_element_type=F32,
        )
        for m in range(2):
            for n in range(width // 128):
                at = m * width + n * 128
                x_last[m, n * width:(n + 1) * width, :] += part[:, at:at + 128]

    sum_all(
        chips, deeps, x_last, t_last, last_core, last_chip, last_deep, [s.at[2] for s in sum_sems]
    )
    for m in range(2):
        for n in range(width // 128):
            red_out[m, :, n * 128:(n + 1) * 128] = t_last[m, n * width:(n + 1) * width, :]
    for b in range(blocks):
        cl = pl.ds(b * UNIT, UNIT)
        pltpu.make_async_copy(col_part.at[cl], col_out.at[cl], out_sem.at[b]).wait()


def body(lf, rf, ld, la, rd, ra, cs, rs):
    rows, cols = lf.shape[0], rf.shape[0]
    ports, width = ld.shape[0], cs.shape[1]
    left_n, right_n = lax.axis_size("left"), lax.axis_size("right")
    total_rows, total_cols = rows * left_n, cols * right_n
    chips, deeps = left_n // 2, right_n
    steps = deeps.bit_length() - 1
    chunks, blocks = rows // UNIT, cols // UNIT
    block, share = cols // 4 // chips, rows // deeps
    high, full = 128 * len(triangle(width)), width * width // 128
    args = (lf[None, :], rf[None, :], ld, la, rd, ra, cs, rs)
    sems = lambda n, m: pltpu.SemaphoreType.DMA((n, 2, m))
    row_basis, col_basis, reduced = pl.pallas_call(
        functools.partial(whole_kernel, float(total_rows), chips, deeps),
        in_specs=[pl.BlockSpec(memory_space=pl.ANY)] * 8,
        out_specs=[
            pl.BlockSpec(memory_space=pltpu.VMEM),
            pl.BlockSpec(memory_space=pl.ANY),
            pl.BlockSpec(memory_space=pltpu.VMEM),
        ],
        out_shape=[
            jax.ShapeDtypeStruct((share, width), F32),
            jax.ShapeDtypeStruct((cols, width), F32),
            jax.ShapeDtypeStruct((2, width, width), F32),
        ],
        scratch_shapes=[pltpu.VMEM(x.shape, x.dtype) for x in args] + [
            pltpu.VMEM((rows, cols), BF16),
            pltpu.VMEM((share, width), F32),
            pltpu.VMEM((2 * block, width), F32),
            pltpu.VMEM((rows, 256), BF16),
            pltpu.VMEM((256, cols), BF16),
            pltpu.VMEM((chunks, width, UNIT), BF16),
            pltpu.VMEM((rows, 128), F32),
            pltpu.VMEM((chunks, UNIT, width), F32),
            pltpu.VMEM((blocks, width, UNIT), F32),
            pltpu.VMEM((cols, width), F32),
            pltpu.VMEM((chunks, UNIT, width), F32),
            pltpu.VMEM((2, cols // 4, width), F32),
            pltpu.VMEM((2, chips - 1, block, width), F32),
            pltpu.VMEM((rows, width), F32),
            pltpu.VMEM((cols, width), F32),
            pltpu.VMEM((2, 2, high, 128), F32),
            pltpu.VMEM((2, 2, high, 128), F32),
            pltpu.VMEM((2, high, 128), F32),
            pltpu.VMEM((2, chips - 1, high // chips, 128), F32),
            pltpu.VMEM((2, deeps, high // chips, 128), F32),
            pltpu.VMEM((2, full, 128), F32),
            pltpu.VMEM((2, full, 128), F32),
            pltpu.VMEM((full, 128), F32),
            pltpu.VMEM((chips - 1, full // chips, 128), F32),
            pltpu.VMEM((deeps, full // chips, 128), F32),
            pltpu.VMEM((2, width, 2 * width), F32),
            pltpu.VMEM((2, width, width), F32),
            pltpu.VMEM((2, width, width), F32),
            pltpu.SemaphoreType.DMA((8,)),
            pltpu.SemaphoreType.DMA((blocks,)),
            sems(chunks, steps), sems(2, chips), sems(2, chips - 1),
            sems(chunks, deeps - 1), sems(2, chips - 1), pltpu.SemaphoreType.DMA((2, 2)),
            sems(3, chips), sems(3, chips - 1), sems(3, deeps - 1), sems(3, chips - 1),
            sems(3, chips),
        ],
        compiler_params=pltpu.CompilerParams(
            collective_id=1, has_side_effects=True, vmem_limit_bytes=63 << 20
        ),
        name="loewner",
    )(*args)
    return (
        row_basis * math.sqrt(total_rows),
        col_basis * math.sqrt(total_cols),
        reduced[0],
        reduced[1],
    )


def solution(mesh):
    in_specs = (
        P("left"), P("right"), P(None, "left"), P(None, "left"),
        P(None, "right"), P(None, "right"), P("right", None), P("left", None),
    )
    out_specs = (P(("left", "right"), None), P("right", None), P(), P())
    return jax.shard_map(body, mesh=mesh, in_specs=in_specs, out_specs=out_specs, check_vma=False)
```

```python
import functools
import math

import jax
import jax.numpy as jnp
from jax import lax
from jax.experimental import pallas as pl
from jax.experimental.pallas import tpu as pltpu
from jax.sharding import PartitionSpec as P

precise = lax.Precision.HIGHEST
F32 = jnp.float32
BF16 = jnp.bfloat16
LEFT_PARTS = (0, 0, 1, 0, 1, 2)
RIGHT_PARTS = (0, 1, 0, 2, 1, 0)


def tdot(a, b, precision=None):
    return lax.dot_general(
        a, b, (((0,), (0,)), ((), ())), precision=precision, preferred_element_type=F32
    )


def split3(x):
    one = x.astype(BF16).astype(F32)
    rest = x - one
    two = rest.astype(BF16).astype(F32)
    return (one, two, (rest - two).astype(BF16).astype(F32))


def join_parts(x, order, axis):
    parts = split3(x)
    return jnp.concatenate([parts[p].astype(BF16) for p in order], axis=axis)


def stack_parts(first, second, order):
    a, b = split3(first), split3(second)
    pieces = [a[p] for p in order] + [b[p] for p in order]
    pad = jnp.zeros((256 - 12 * first.shape[0], first.shape[1]), F32)
    return jnp.concatenate(pieces + [pad], axis=0)


UNIT = 512


def places():
    me, deep = lax.axis_index("left"), lax.axis_index("right")
    core = lax.rem(me, 2)
    return me, deep, core, me // 2


def chip_peer(chip, core, offset, chips):
    return {"left": lax.rem(chip + offset, chips) * 2 + core}


def peers_of(chips, deeps):
    me, deep, core, chip = places()
    peers = [{"left": chip * 2 + (1 - core)}]
    peers += [chip_peer(chip, core, o, chips) for o in range(1, chips)]
    peers += [{"right": lax.rem(deep + o, deeps)} for o in range(1, deeps)]
    return peers


def greet_start(chips, deeps):
    barrier = pltpu.get_barrier_semaphore()
    for peer in peers_of(chips, deeps):
        pl.semaphore_signal(
            barrier, inc=1, device_id=peer, device_id_type=pl.DeviceIdType.MESH
        )


def greet_end(chips, deeps):
    pl.semaphore_wait(pltpu.get_barrier_semaphore(), chips + deeps - 1)


def greet(chips, deeps):
    greet_start(chips, deeps)
    greet_end(chips, deeps)


def send(src, dst, sems, slot, peer):
    copy = pltpu.make_async_remote_copy(
        src_ref=src,
        dst_ref=dst,
        send_sem=sems.at[0, slot],
        recv_sem=sems.at[1, slot],
        device_id=peer,
        device_id_type=pl.DeviceIdType.MESH,
    )
    copy.start()
    return copy


def reversed_bits(p, bits):
    return sum(((p >> i) & 1) << (bits - 1 - i) for i in range(bits))


def images(
    total, chips, deeps, anys, refs, tile_ref, row_out, col_out,
    left_scr, right_scr, sketch_scr, freq_scr, row_acc, col_acc, col_part,
    row_buf, core_buf, chip_buf,
    in_sem, row_sem, core_sem, chip_sem,
):
    lf_any, rf_any, ld_any, la_any, rd_any, ra_any, cs_any, rs_any = anys
    lf_ref, rf_ref, ld_ref, la_ref, rd_ref, ra_ref, cs_ref, rs_ref = refs
    me, deep, core, chip = places()
    rows, cols = tile_ref.shape
    width = row_out.shape[1]
    chunks, blocks = rows // UNIT, cols // UNIT
    steps = deeps.bit_length() - 1
    share, seg = rows // deeps, UNIT // deeps
    order = [reversed_bits(p, steps) for p in range(deeps)]
    sibling = {"left": chip * 2 + (1 - core)}
    loads = [
        pltpu.make_async_copy(src, dst, in_sem.at[n])
        for n, (src, dst) in enumerate(
            [
                (lf_any, lf_ref), (la_any, la_ref), (ld_any, ld_ref), (rs_any, rs_ref),
                (rf_any, rf_ref), (rd_any, rd_ref), (ra_any, ra_ref), (cs_any, cs_ref),
            ]
        )
    ]
    for load in loads:
        load.start()
    greet_start(chips, deeps)

    @pl.loop(0, chunks)
    def _(c):
        row_acc[c] = jnp.zeros((UNIT, width), F32)

    @pl.loop(0, blocks)
    def _(b):
        col_acc[b] = jnp.zeros((width, UNIT), F32)

    for load in loads[:4]:
        load.wait()
    for r in range(0, rows, UNIT):
        wide = jnp.broadcast_to(lf_ref[:, r:r + UNIT] * total, (128, UNIT))
        freq_scr[r:r + UNIT, :] = wide.T
        stacked = stack_parts(la_ref[:, r:r + UNIT], -ld_ref[:, r:r + UNIT], LEFT_PARTS)
        left_scr[r:r + UNIT, :] = stacked.T.astype(BF16)
    for c in range(chunks):
        part = jnp.concatenate(
            [rs_ref[d * share + c * seg:d * share + (c + 1) * seg, :] for d in order], axis=0
        )
        sketch_scr[c] = part.astype(F32).T.astype(BF16)
    for load in loads[4:]:
        load.wait()

    @pl.loop(0, blocks)
    def _(b):
        cl = pl.ds(pl.multiple_of(b * UNIT, UNIT), UNIT)
        right_scr[:, cl] = stack_parts(rd_ref[:, cl], ra_ref[:, cl], RIGHT_PARTS).astype(BF16)

    def tiles(c, low, high, last):
        own = [pl.ds(d * share + c * seg, seg) for d in order]

        @pl.loop(low, high)
        def _(b):
            cl = pl.ds(pl.multiple_of(b * UNIT, UNIT), UNIT)
            left = jnp.concatenate([left_scr[sl, :] for sl in own], axis=0)
            freq = jnp.concatenate([freq_scr[sl, :] for sl in own], axis=0)
            numer = jnp.dot(left, right_scr[:, cl], preferred_element_type=F32)
            gap = jnp.concatenate([freq] * (UNIT // 128), axis=1) - rf_ref[:, cl] * total
            tile = (numer / gap).astype(BF16)
            for p, sl in enumerate(own):
                tile_ref[sl, cl] = tile[p * seg:(p + 1) * seg, :]
            row_acc[c] += jnp.dot(tile, cs_ref[cl, :], preferred_element_type=F32)
            part = jnp.dot(sketch_scr[c], tile, preferred_element_type=F32)
            if last:
                col_part[cl, :] = (col_acc[b] + part).T
            else:
                col_acc[b] += part

    def bit(s):
        return lax.rem(deep // (1 << s), 2)

    def segment(s):
        start, size = 0, UNIT
        for t in range(s):
            size = size // 2
            start = start + bit(t) * size
        return start, size

    def halve(c, s):
        start, size = segment(s)
        half = size // 2
        src = pl.ds(pl.multiple_of(start + (1 - bit(s)) * half, 8), half)
        slot = pl.ds(UNIT - size, half)
        return send(
            row_acc.at[c, src], row_buf.at[c, slot], row_sem.at[c], s,
            {"right": deep + (1 - 2 * bit(s)) * (1 << s)},
        )

    def settle(c, s, copy):
        copy.wait()
        start, size = segment(s)
        half = size // 2
        mine = pl.ds(pl.multiple_of(start + bit(s) * half, 8), half)
        value = row_acc[c, mine, :] + row_buf[c, UNIT - size:UNIT - size + half, :]
        if s == steps - 1:
            row_out[c * seg:(c + 1) * seg, :] = value
            return None
        row_acc[c, mine, :] = value
        return halve(c, s + 1)

    half_cols, quarter = cols // 2, cols // 4
    piece = quarter // chips

    def pair_start(h):
        copies = []
        for o in range(1, chips + 1):
            peer = lax.rem(chip + o, chips)
            at = pl.multiple_of(peer * piece, 8)
            src = pl.ds(h * half_cols + (1 - core) * quarter + at, piece)
            copies.append(
                send(
                    col_part.at[src], core_buf.at[h, pl.ds(at, piece)], core_sem.at[h], o - 1,
                    sibling,
                )
            )
        return copies

    def pair_end(h, copies):
        sent = []
        for o in range(1, chips + 1):
            peer = lax.rem(chip + o, chips)
            at = pl.multiple_of(peer * piece, 8)
            copies[o - 1].wait()
            dst = pl.ds(at, piece)
            core_buf[h, dst, :] += col_part[pl.ds(h * half_cols + core * quarter + at, piece), :]
            if o < chips:
                sent.append(
                    send(
                        core_buf.at[h, dst], chip_buf.at[h, o - 1], chip_sem.at[h], o - 1,
                        {"left": peer * 2 + core},
                    )
                )
        return sent

    def chip_end(h, copies):
        value = core_buf[h, pl.ds(pl.multiple_of(chip * piece, 8), piece), :]
        for o in range(1, chips):
            copies[o - 1].wait()
            value = value + chip_buf[h, o - 1]
        col_out[h * piece:(h + 1) * piece, :] = value

    z = [None] * chunks
    mid = blocks // 2
    early = chunks // 2
    for c in range(early):
        tiles(c, 0, blocks, False)
        if c == 0:
            greet_end(chips, deeps)
        z[c] = halve(c, 0)
    for c in range(early, chunks):
        tiles(c, 0, mid, c == chunks - 1)
        if c == early:
            z[0] = settle(0, 0, z[0])
    pair = pair_start(0)
    for c in range(early, chunks):
        tiles(c, mid, blocks, c == chunks - 1)
        z[c] = halve(c, 0)
        if c == early:
            chip_first = pair_end(0, pair)
            for e in range(1, early):
                z[e] = settle(e, 0, z[e])
    pair = pair_start(1)
    chip_second = pair_end(1, pair)
    for s in range(1, steps):
        for c in range(early):
            z[c] = settle(c, s, z[c])
    for s in range(steps):
        for c in range(early, chunks):
            z[c] = settle(c, s, z[c])
        if s == 0:
            chip_end(0, chip_first)
    chip_end(1, chip_second)


BLOCK = 64
GROUP = 8


def triangle(width):
    return [(i, j) for i in range(width // 128) for j in range(i, width // 128)]


def store_gram(dst, m, gram):
    for n, (i, j) in enumerate(triangle(gram.shape[0])):
        dst[m, n * 128:(n + 1) * 128, :] = gram[i * 128:(i + 1) * 128, j * 128:(j + 1) * 128]


def factor(shifted, t_ref, out_ref, work):
    width = out_ref.shape[-1]
    row_id = lax.broadcasted_iota(jnp.int32, (width, width), 0)
    col_id = lax.broadcasted_iota(jnp.int32, (width, width), 1)
    eye = (row_id == col_id).astype(F32)
    for m in range(2):
        work[m, :, 0:width] = jnp.zeros((width, width), F32)
        for n, (i, j) in enumerate(triangle(width)):
            work[m, i * 128:(i + 1) * 128, j * 128:(j + 1) * 128] = t_ref[m, n * 128:(n + 1) * 128, :]
        if shifted:
            gram = work[m, :, 0:width]
            trace = jnp.sum(jnp.sum(gram * eye, axis=1, keepdims=True), axis=0, keepdims=True)
            work[m, :, 0:width] = gram + (1e-05 * trace / width) * eye
        work[m, :, width:] = eye
    brow = lax.broadcasted_iota(jnp.int32, (BLOCK, BLOCK), 0)
    bcol = lax.broadcasted_iota(jnp.int32, (BLOCK, BLOCK), 1)
    small_eye = (brow == bcol).astype(F32)
    low = lax.broadcasted_iota(jnp.int32, (BLOCK, 2 * BLOCK), 0)
    for k in range(0, width, BLOCK):
        pairs = [
            jnp.concatenate([work[m, k:k + BLOCK, k:k + BLOCK], small_eye], axis=1)
            for m in range(2)
        ]
        for base in range(0, BLOCK, GROUP):
            copies = [
                [jnp.broadcast_to(pair[:, s:s + 1], low.shape) for s in range(base, base + GROUP)]
                for pair in pairs
            ]
            for i in range(GROUP):
                s = base + i
                for m in range(2):
                    wide = copies[m]
                    top = 1.0 / wide[i][s:s + 1, :]
                    column = jnp.where(low > s, wide[i], 0.0)
                    for j in range(i + 1, GROUP):
                        wide[j] = wide[j] - column * (wide[j][s:s + 1, :] * top)
                    pairs[m] = pairs[m] - column * (pairs[m][s:s + 1, :] * top)
        lo = k + BLOCK
        start, stop = k // 128 * 128, width + (lo + 127) // 128 * 128
        solved = []
        for m in range(2):
            diag = jnp.sum(pairs[m][:, 0:BLOCK] * small_eye, axis=1, keepdims=True)
            inv = pairs[m][:, BLOCK:] * lax.rsqrt(diag)
            solved.append(
                jnp.dot(
                    inv, work[m, k:lo, start:stop], precision=precise,
                    preferred_element_type=F32,
                )
            )
        for m in range(2):
            out_ref[m, k:lo, 0:stop - width] = solved[m][:, width - start:]
            if stop < 2 * width:
                out_ref[m, k:lo, stop - width:] = jnp.zeros((BLOCK, 2 * width - stop), F32)
        if lo < width:
            deltas = [tdot(rows[:, lo - start:width - start], rows, precise) for rows in solved]
            for m in range(2):
                work[m, lo:, start:stop] = work[m, lo:, start:stop] - deltas[m]


def apply_inverse(basis, inverse, precision):
    return lax.dot_general(
        basis, inverse, (((1,), (1,)), ((), ())), precision=precision, preferred_element_type=F32
    )


def sum_all(chips, deeps, x, total, core_buf, chip_buf, deep_buf, sems):
    me, deep, core, chip = places()
    core_sem, chip_sem, deep_sem, back_sem, last_sem = sems
    piece = chip_buf.shape[1]
    sibling = {"left": chip * 2 + (1 - core)}
    part_of = lambda q: pl.ds(pl.multiple_of(q * piece, 8), piece)
    firsts = []
    for o in range(1, chips + 1):
        q = part_of(lax.rem(chip + o, chips))
        firsts.append(send(x.at[1 - core, q], core_buf.at[q], core_sem, o - 1, sibling))
    copies = []
    for o in range(1, chips + 1):
        peer = lax.rem(chip + o, chips)
        q = part_of(peer)
        firsts[o - 1].wait()
        core_buf[q, :] += x[core, q, :]
        if o < chips:
            copies.append(
                send(core_buf.at[q], chip_buf.at[o - 1], chip_sem, o - 1, {"left": peer * 2 + core})
            )
    mine = part_of(chip)
    part = core_buf[mine, :]
    for o in range(1, chips):
        copies[o - 1].wait()
        part = part + chip_buf[o - 1]
    deep_buf[deep] = part
    copies = []
    for o in range(1, deeps):
        copies.append(
            send(
                deep_buf.at[deep], deep_buf.at[deep], deep_sem, o - 1,
                {"right": lax.rem(deep + o, deeps)},
            )
        )
    for copy in copies:
        copy.wait()
    part = deep_buf[0]
    for d in range(1, deeps):
        part = part + deep_buf[d]
    total[core, mine, :] = part
    copies = []
    for o in range(1, chips):
        copies.append(
            send(
                total.at[core, mine], total.at[core, mine], back_sem, o - 1,
                chip_peer(chip, core, o, chips),
            )
        )
    lasts = [send(total.at[core, mine], total.at[core, mine], last_sem, 0, sibling)]
    for o in range(1, chips):
        copies[o - 1].wait()
        q = part_of(lax.rem(chip + chips - o, chips))
        lasts.append(send(total.at[core, q], total.at[core, q], last_sem, o, sibling))
    for copy in lasts:
        copy.wait()


def whole_kernel(total, chips, deeps, *args):
    anys, (row_out, col_out, red_out), refs, rest = args[:8], args[8:11], args[11:19], args[19:]
    (
        tile_ref, row_own, col_own, left_scr, right_scr, sketch_scr, freq_scr, row_acc, col_acc,
        col_part, row_buf, core_buf, chip_buf, row_full, col_full,
        x_buf, t_buf, sum_core, sum_chip, sum_deep, x_last, t_last, last_core, last_chip, last_deep,
        work, inv1, inv2, mix_scr, in_sem, out_sem, row_sem, core_sem, chip_sem, row_all, col_all, pair_all,
        *sum_sems,
    ) = rest
    lf_ref, rf_ref, ld_ref, la_ref, rd_ref, ra_ref, cs_ref, rs_ref = refs
    me, deep, core, chip = places()
    sibling = {"left": chip * 2 + (1 - core)}
    images(
        total, chips, deeps, anys, refs, tile_ref, row_own, col_own,
        left_scr, right_scr, sketch_scr, freq_scr, row_acc, col_acc, col_part,
        row_buf, core_buf, chip_buf, in_sem, row_sem, core_sem, chip_sem,
    )
    rows, cols = tile_ref.shape
    width, ports = row_out.shape[1], ld_ref.shape[0]
    chunks, blocks = rows // UNIT, cols // UNIT
    share, block = rows // deeps, col_own.shape[0] // 2
    seg, quarter = share // chunks, chips * block
    cols_at = lambda h, c: pl.multiple_of(h * 2 * quarter + core * quarter + c * block, 8)

    def sum_round(n, row, col):
        store_gram(x_buf.at[n], 0, tdot(row, row, precise))
        store_gram(x_buf.at[n], 1, tdot(col, col, precise))
        sum_all(
            chips, deeps, x_buf.at[n], t_buf.at[n], sum_core.at[n], sum_chip.at[n],
            sum_deep.at[n], [s.at[n] for s in sum_sems],
        )

    def row_spread(c):
        src = pl.ds(c * seg, seg)
        dst = pl.ds(pl.multiple_of(deep * share + c * seg, 8), seg)
        return [
            send(
                row_own.at[src], row_full.at[dst], row_all.at[c], o - 1,
                {"right": lax.rem(deep + o, deeps)},
            )
            for o in range(1, deeps)
        ]

    row_copies = row_spread(0)
    sum_round(0, row_own[...], col_own[...])
    col_copies = [
        send(
            col_own.at[pl.ds(h * block, block)], col_full.at[pl.ds(cols_at(h, chip), block)],
            col_all.at[h], o - 1, chip_peer(chip, core, o, chips),
        )
        for h in range(2)
        for o in range(1, chips)
    ]
    for c in range(1, chunks - 1):
        row_copies += row_spread(c)
    row_full[pl.ds(pl.multiple_of(deep * share, 8), share), :] = row_own[...]
    for h in range(2):
        col_full[pl.ds(cols_at(h, chip), block), :] = col_own[h * block:(h + 1) * block, :]
    factor(True, t_buf.at[0], inv1, work)
    sum_round(
        1,
        apply_inverse(row_own[...], inv1[0], precise),
        apply_inverse(col_own[...], inv1[1], precise),
    )
    row_copies += row_spread(chunks - 1)
    for copy in col_copies:
        copy.wait()
    pair = []
    for h in range(2):
        own = pl.ds(cols_at(h, 0), quarter)
        pair.append(send(col_full.at[own], col_full.at[own], pair_all, h, sibling))
    factor(False, t_buf.at[1], inv2, work)
    for m in range(2):
        inv1[m] = jnp.dot(inv2[m], inv1[m], precision=precise, preferred_element_type=F32)
    for m in range(2):
        mix_scr[m] = join_parts(inv1[m].T, RIGHT_PARTS, 0)

    def mixed(value, m):
        return jnp.dot(
            join_parts(value, LEFT_PARTS, 1), mix_scr[m], preferred_element_type=F32
        )

    row_out[...] = mixed(row_own[...], 0) * math.sqrt(rows * chips * 2)
    for copy in pair:
        copy.wait()
    work[0, 0:48, 0:width] = jnp.zeros((48, width), F32)

    @pl.loop(0, blocks)
    def _(b):
        cl = pl.ds(pl.multiple_of(b * UNIT, UNIT), UNIT)
        value = mixed(col_full[cl, :], 1)
        col_part[cl, :] = value * math.sqrt(cols * deeps)
        pltpu.make_async_copy(col_part.at[cl], col_out.at[cl], out_sem.at[b]).start()
        rounded = value.astype(BF16)
        cs_ref[cl, :] = rounded
        right = join_parts(ra_ref[:, cl], (0, 1, 2), 0)
        work[0, 0:48, 0:width] += jnp.dot(right, rounded, preferred_element_type=F32)

    for copy in row_copies:
        copy.wait()
    low = (work[0, 0:16, 0:width] + work[0, 16:32, 0:width] + work[0, 32:48, 0:width]) * (-1.0 / total)
    work[0, :, 0:width] = jnp.zeros((width, width), F32)
    for p in (0, 2, 5):
        at = (6 + p) * ports
        work[0, at:at + ports, 0:width] = low
    low = work[0, :, 0:width]
    work[0] = jnp.zeros((width, 2 * width), F32)
    work[1, :, 0:width] = jnp.zeros((width, width), F32)

    @pl.loop(0, chunks)
    def _(c):
        sl = pl.ds(pl.multiple_of(c * UNIT, UNIT), UNIT)
        applied = jnp.dot(tile_ref[sl, :], cs_ref[...], preferred_element_type=F32)
        freq = jnp.concatenate([freq_scr[sl, :] * (1.0 / total)] * (width // 128), axis=1)
        both = jnp.concatenate([applied.astype(BF16), (applied * freq).astype(BF16)], axis=1)
        q = mixed(row_full[sl, :], 0).T
        q_hi = q.astype(BF16)
        q_lo = (q - q_hi.astype(F32)).astype(BF16)
        work[0] += jnp.dot(q_hi, both, preferred_element_type=F32)
        left = left_scr[sl, :]
        work[1, :, 0:width] += jnp.dot(
            jnp.concatenate([q_hi, q_lo], axis=1), jnp.concatenate([left, left], axis=0),
            preferred_element_type=F32,
        )

    shifted = work[0, :, width:] + jnp.dot(
        work[1, :, 0:width], low, precision=precise, preferred_element_type=F32
    )
    for n in range(width // 128):
        x_last[0, n * width:(n + 1) * width, :] = work[0, :, n * 128:(n + 1) * 128]
        x_last[1, n * width:(n + 1) * width, :] = shifted[:, n * 128:(n + 1) * 128]

    sum_all(
        chips, deeps, x_last, t_last, last_core, last_chip, last_deep, [s.at[2] for s in sum_sems]
    )
    for m in range(2):
        for n in range(width // 128):
            red_out[m, :, n * 128:(n + 1) * 128] = t_last[m, n * width:(n + 1) * width, :]
    for b in range(blocks):
        cl = pl.ds(b * UNIT, UNIT)
        pltpu.make_async_copy(col_part.at[cl], col_out.at[cl], out_sem.at[b]).wait()


def deliver_kernel(row_in, col_in, red_in, row_out, col_out, low_out, shift_out):
    col_out[...] = col_in[...]

    @pl.when(pl.program_id(0) == 0)
    def _():
        row_out[...] = row_in[...]
        low_out[...] = red_in[0]
        shift_out[...] = red_in[1]


def deliver(row_basis, col_basis, reduced):
    shapes = [row_basis.shape, col_basis.shape, reduced.shape[1:], reduced.shape[1:]]
    width, tall = row_basis.shape[1], col_basis.shape[0] // 4
    fixed = lambda shape: pl.BlockSpec(shape, lambda i: (0,) * len(shape))
    moving = pl.BlockSpec((tall, width), lambda i: (i, 0))
    return pl.pallas_call(
        deliver_kernel,
        grid=(4,),
        in_specs=[fixed(row_basis.shape), moving, fixed(reduced.shape)],
        out_specs=[fixed(shapes[0]), moving, fixed(shapes[2]), fixed(shapes[3])],
        out_shape=[jax.ShapeDtypeStruct(shape, F32) for shape in shapes],
        name="deliver",
    )(row_basis, col_basis, reduced)


def body(lf, rf, ld, la, rd, ra, cs, rs):
    rows, cols = lf.shape[0], rf.shape[0]
    ports, width = ld.shape[0], cs.shape[1]
    left_n, right_n = lax.axis_size("left"), lax.axis_size("right")
    total_rows = rows * left_n
    chips, deeps = left_n // 2, right_n
    steps = deeps.bit_length() - 1
    chunks, blocks = rows // UNIT, cols // UNIT
    block, share = cols // 4 // chips, rows // deeps
    high, full = 128 * len(triangle(width)), width * width // 128
    args = (lf[None, :], rf[None, :], ld, la, rd, ra, cs, rs)
    sems = lambda n, m: pltpu.SemaphoreType.DMA((n, 2, m))
    row_basis, col_basis, reduced = pl.pallas_call(
        functools.partial(whole_kernel, float(total_rows), chips, deeps),
        in_specs=[pl.BlockSpec(memory_space=pl.ANY)] * 8,
        out_specs=[
            pl.BlockSpec(memory_space=pltpu.VMEM),
            pl.BlockSpec(memory_space=pl.ANY),
            pl.BlockSpec(memory_space=pltpu.VMEM),
        ],
        out_shape=[
            jax.ShapeDtypeStruct((share, width), F32),
            jax.ShapeDtypeStruct((cols, width), F32),
            jax.ShapeDtypeStruct((2, width, width), F32),
        ],
        scratch_shapes=[pltpu.VMEM(x.shape, x.dtype) for x in args] + [
            pltpu.VMEM((rows, cols), BF16),
            pltpu.VMEM((share, width), F32),
            pltpu.VMEM((2 * block, width), F32),
            pltpu.VMEM((rows, 256), BF16),
            pltpu.VMEM((256, cols), BF16),
            pltpu.VMEM((chunks, width, UNIT), BF16),
            pltpu.VMEM((rows, 128), F32),
            pltpu.VMEM((chunks, UNIT, width), F32),
            pltpu.VMEM((blocks, width, UNIT), F32),
            pltpu.VMEM((cols, width), F32),
            pltpu.VMEM((chunks, UNIT, width), F32),
            pltpu.VMEM((2, cols // 4, width), F32),
            pltpu.VMEM((2, chips - 1, block, width), F32),
            pltpu.VMEM((rows, width), F32),
            pltpu.VMEM((cols, width), F32),
            pltpu.VMEM((2, 2, high, 128), F32),
            pltpu.VMEM((2, 2, high, 128), F32),
            pltpu.VMEM((2, high, 128), F32),
            pltpu.VMEM((2, chips - 1, high // chips, 128), F32),
            pltpu.VMEM((2, deeps, high // chips, 128), F32),
            pltpu.VMEM((2, full, 128), F32),
            pltpu.VMEM((2, full, 128), F32),
            pltpu.VMEM((full, 128), F32),
            pltpu.VMEM((chips - 1, full // chips, 128), F32),
            pltpu.VMEM((deeps, full // chips, 128), F32),
            pltpu.VMEM((2, width, 2 * width), F32),
            pltpu.VMEM((2, width, width), F32),
            pltpu.VMEM((2, width, width), F32),
            pltpu.VMEM((2, 6 * width, width), BF16),
            pltpu.SemaphoreType.DMA((8,)),
            pltpu.SemaphoreType.DMA((blocks,)),
            sems(chunks, steps), sems(2, chips), sems(2, chips - 1),
            sems(chunks, deeps - 1), sems(2, chips - 1), pltpu.SemaphoreType.DMA((2, 2)),
            sems(3, chips), sems(3, chips - 1), sems(3, deeps - 1), sems(3, chips - 1),
            sems(3, chips),
        ],
        compiler_params=pltpu.CompilerParams(
            collective_id=1, has_side_effects=True, vmem_limit_bytes=63 << 20
        ),
        name="loewner",
    )(*args)
    return deliver(row_basis, col_basis, reduced)


def solution(mesh):
    in_specs = (
        P("left"), P("right"), P(None, "left"), P(None, "left"),
        P(None, "right"), P(None, "right"), P("right", None), P("left", None),
    )
    out_specs = (P(("left", "right"), None), P("right", None), P(), P())
    return jax.shard_map(body, mesh=mesh, in_specs=in_specs, out_specs=out_specs, check_vma=False)
```

```python
import functools
import math

import jax
import jax.numpy as jnp
from jax import lax
from jax.experimental import pallas as pl
from jax.experimental.pallas import tpu as pltpu
from jax.sharding import PartitionSpec as P

precise = lax.Precision.HIGHEST
F32 = jnp.float32
BF16 = jnp.bfloat16
LEFT_PARTS = (0, 0, 1, 0, 1, 2)
RIGHT_PARTS = (0, 1, 0, 2, 1, 0)


def tdot(a, b, precision=None):
    return lax.dot_general(
        a, b, (((0,), (0,)), ((), ())), precision=precision, preferred_element_type=F32
    )


def split3(x):
    one = x.astype(BF16).astype(F32)
    rest = x - one
    two = rest.astype(BF16).astype(F32)
    return (one, two, (rest - two).astype(BF16).astype(F32))


def join_parts(x, order, axis):
    parts = split3(x)
    return jnp.concatenate([parts[p].astype(BF16) for p in order], axis=axis)


def stack_parts(first, second, order):
    a, b = split3(first), split3(second)
    pieces = [a[p] for p in order] + [b[p] for p in order]
    pad = jnp.zeros((256 - 12 * first.shape[0], first.shape[1]), F32)
    return jnp.concatenate(pieces + [pad], axis=0)


UNIT = 512


def places():
    me, deep = lax.axis_index("left"), lax.axis_index("right")
    core = lax.rem(me, 2)
    return me, deep, core, me // 2


def chip_peer(chip, core, offset, chips):
    return {"left": lax.rem(chip + offset, chips) * 2 + core}


def peers_of(chips, deeps):
    me, deep, core, chip = places()
    peers = [{"left": chip * 2 + (1 - core)}]
    peers += [chip_peer(chip, core, o, chips) for o in range(1, chips)]
    peers += [{"right": lax.rem(deep + o, deeps)} for o in range(1, deeps)]
    return peers


def greet_start(chips, deeps):
    barrier = pltpu.get_barrier_semaphore()
    for peer in peers_of(chips, deeps):
        pl.semaphore_signal(
            barrier, inc=1, device_id=peer, device_id_type=pl.DeviceIdType.MESH
        )


def greet_end(chips, deeps):
    pl.semaphore_wait(pltpu.get_barrier_semaphore(), chips + deeps - 1)


def greet(chips, deeps):
    greet_start(chips, deeps)
    greet_end(chips, deeps)


def send(src, dst, sems, slot, peer):
    copy = pltpu.make_async_remote_copy(
        src_ref=src,
        dst_ref=dst,
        send_sem=sems.at[0, slot],
        recv_sem=sems.at[1, slot],
        device_id=peer,
        device_id_type=pl.DeviceIdType.MESH,
    )
    copy.start()
    return copy


def reversed_bits(p, bits):
    return sum(((p >> i) & 1) << (bits - 1 - i) for i in range(bits))


def images(
    total, chips, deeps, anys, refs, tile_ref, row_out, col_out,
    left_scr, right_scr, sketch_scr, freq_scr, row_acc, col_acc, col_part,
    row_buf, core_buf, chip_buf,
    in_sem, row_sem, core_sem, chip_sem,
):
    lf_any, rf_any, ld_any, la_any, rd_any, ra_any, cs_any, rs_any = anys
    lf_ref, rf_ref, ld_ref, la_ref, rd_ref, ra_ref, cs_ref, rs_ref = refs
    me, deep, core, chip = places()
    rows, cols = tile_ref.shape
    width = row_out.shape[1]
    chunks, blocks = rows // UNIT, cols // UNIT
    steps = deeps.bit_length() - 1
    share, seg = rows // deeps, UNIT // deeps
    order = [reversed_bits(p, steps) for p in range(deeps)]
    sibling = {"left": chip * 2 + (1 - core)}
    loads = [
        pltpu.make_async_copy(src, dst, in_sem.at[n])
        for n, (src, dst) in enumerate(
            [
                (lf_any, lf_ref), (la_any, la_ref), (ld_any, ld_ref), (rs_any, rs_ref),
                (rf_any, rf_ref), (rd_any, rd_ref), (ra_any, ra_ref), (cs_any, cs_ref),
            ]
        )
    ]
    for load in loads:
        load.start()
    greet_start(chips, deeps)

    @pl.loop(0, chunks)
    def _(c):
        row_acc[c] = jnp.zeros((UNIT, width), F32)

    @pl.loop(0, blocks)
    def _(b):
        col_acc[b] = jnp.zeros((width, UNIT), F32)

    for load in loads[:4]:
        load.wait()
    for r in range(0, rows, UNIT):
        wide = jnp.broadcast_to(lf_ref[:, r:r + UNIT] * total, (128, UNIT))
        freq_scr[r:r + UNIT, :] = wide.T
        stacked = stack_parts(la_ref[:, r:r + UNIT], -ld_ref[:, r:r + UNIT], LEFT_PARTS)
        left_scr[r:r + UNIT, :] = stacked.T.astype(BF16)
    for c in range(chunks):
        part = jnp.concatenate(
            [rs_ref[d * share + c * seg:d * share + (c + 1) * seg, :] for d in order], axis=0
        )
        sketch_scr[c] = part.astype(F32).T.astype(BF16)
    for load in loads[4:]:
        load.wait()

    @pl.loop(0, blocks)
    def _(b):
        cl = pl.ds(pl.multiple_of(b * UNIT, UNIT), UNIT)
        right_scr[:, cl] = stack_parts(rd_ref[:, cl], ra_ref[:, cl], RIGHT_PARTS).astype(BF16)

    def tiles(c, low, high, last):
        own = [pl.ds(d * share + c * seg, seg) for d in order]

        @pl.loop(low, high)
        def _(b):
            cl = pl.ds(pl.multiple_of(b * UNIT, UNIT), UNIT)
            left = jnp.concatenate([left_scr[sl, :] for sl in own], axis=0)
            freq = jnp.concatenate([freq_scr[sl, :] for sl in own], axis=0)
            numer = jnp.dot(left, right_scr[:, cl], preferred_element_type=F32)
            gap = jnp.concatenate([freq] * (UNIT // 128), axis=1) - rf_ref[:, cl] * total
            tile = (numer / gap).astype(BF16)
            for p, sl in enumerate(own):
                tile_ref[sl, cl] = tile[p * seg:(p + 1) * seg, :]
            row_acc[c] += jnp.dot(tile, cs_ref[cl, :], preferred_element_type=F32)
            part = jnp.dot(sketch_scr[c], tile, preferred_element_type=F32)
            if last:
                col_part[cl, :] = (col_acc[b] + part).T
            else:
                col_acc[b] += part

    def bit(s):
        return lax.rem(deep // (1 << s), 2)

    def segment(s):
        start, size = 0, UNIT
        for t in range(s):
            size = size // 2
            start = start + bit(t) * size
        return start, size

    def halve(c, s):
        start, size = segment(s)
        half = size // 2
        src = pl.ds(pl.multiple_of(start + (1 - bit(s)) * half, 8), half)
        slot = pl.ds(UNIT - size, half)
        return send(
            row_acc.at[c, src], row_buf.at[c, slot], row_sem.at[c], s,
            {"right": deep + (1 - 2 * bit(s)) * (1 << s)},
        )

    def settle(c, s, copy):
        copy.wait()
        start, size = segment(s)
        half = size // 2
        mine = pl.ds(pl.multiple_of(start + bit(s) * half, 8), half)
        value = row_acc[c, mine, :] + row_buf[c, UNIT - size:UNIT - size + half, :]
        if s == steps - 1:
            row_out[c * seg:(c + 1) * seg, :] = value
            return None
        row_acc[c, mine, :] = value
        return halve(c, s + 1)

    half_cols, quarter = cols // 2, cols // 4
    piece = quarter // chips

    def pair_start(h):
        copies = []
        for o in range(1, chips + 1):
            peer = lax.rem(chip + o, chips)
            at = pl.multiple_of(peer * piece, 8)
            src = pl.ds(h * half_cols + (1 - core) * quarter + at, piece)
            copies.append(
                send(
                    col_part.at[src], core_buf.at[h, pl.ds(at, piece)], core_sem.at[h], o - 1,
                    sibling,
                )
            )
        return copies

    def pair_end(h, copies):
        sent = []
        for o in range(1, chips + 1):
            peer = lax.rem(chip + o, chips)
            at = pl.multiple_of(peer * piece, 8)
            copies[o - 1].wait()
            dst = pl.ds(at, piece)
            core_buf[h, dst, :] += col_part[pl.ds(h * half_cols + core * quarter + at, piece), :]
            if o < chips:
                sent.append(
                    send(
                        core_buf.at[h, dst], chip_buf.at[h, o - 1], chip_sem.at[h], o - 1,
                        {"left": peer * 2 + core},
                    )
                )
        return sent

    def chip_end(h, copies):
        value = core_buf[h, pl.ds(pl.multiple_of(chip * piece, 8), piece), :]
        for o in range(1, chips):
            copies[o - 1].wait()
            value = value + chip_buf[h, o - 1]
        col_out[h * piece:(h + 1) * piece, :] = value

    z = [None] * chunks
    mid = blocks // 2
    early = chunks // 2
    for c in range(early):
        tiles(c, 0, blocks, False)
        if c == 0:
            greet_end(chips, deeps)
        z[c] = halve(c, 0)
    for c in range(early, chunks):
        tiles(c, 0, mid, c == chunks - 1)
        if c == early:
            z[0] = settle(0, 0, z[0])
    pair = pair_start(0)
    for c in range(early, chunks):
        tiles(c, mid, blocks, c == chunks - 1)
        z[c] = halve(c, 0)
        if c == early:
            chip_first = pair_end(0, pair)
            for e in range(1, early):
                z[e] = settle(e, 0, z[e])
    pair = pair_start(1)
    chip_second = pair_end(1, pair)
    for s in range(1, steps):
        for c in range(early):
            z[c] = settle(c, s, z[c])
    for s in range(steps):
        for c in range(early, chunks):
            z[c] = settle(c, s, z[c])
        if s == 0:
            chip_end(0, chip_first)
    chip_end(1, chip_second)


BLOCK = 64
GROUP = 8


def triangle(width):
    return [(i, j) for i in range(width // 128) for j in range(i, width // 128)]


def store_gram(dst, m, gram):
    for n, (i, j) in enumerate(triangle(gram.shape[0])):
        dst[m, n * 128:(n + 1) * 128, :] = gram[i * 128:(i + 1) * 128, j * 128:(j + 1) * 128]


def factor(shifted, t_ref, out_ref, work):
    width = out_ref.shape[-1]
    row_id = lax.broadcasted_iota(jnp.int32, (width, width), 0)
    col_id = lax.broadcasted_iota(jnp.int32, (width, width), 1)
    eye = (row_id == col_id).astype(F32)
    for m in range(2):
        work[m, :, 0:width] = jnp.zeros((width, width), F32)
        for n, (i, j) in enumerate(triangle(width)):
            work[m, i * 128:(i + 1) * 128, j * 128:(j + 1) * 128] = t_ref[m, n * 128:(n + 1) * 128, :]
        if shifted:
            gram = work[m, :, 0:width]
            trace = jnp.sum(jnp.sum(gram * eye, axis=1, keepdims=True), axis=0, keepdims=True)
            work[m, :, 0:width] = gram + (1e-05 * trace / width) * eye
        work[m, :, width:] = eye
    brow = lax.broadcasted_iota(jnp.int32, (BLOCK, BLOCK), 0)
    bcol = lax.broadcasted_iota(jnp.int32, (BLOCK, BLOCK), 1)
    small_eye = (brow == bcol).astype(F32)
    low = lax.broadcasted_iota(jnp.int32, (BLOCK, 2 * BLOCK), 0)
    for k in range(0, width, BLOCK):
        pairs = [
            jnp.concatenate([work[m, k:k + BLOCK, k:k + BLOCK], small_eye], axis=1)
            for m in range(2)
        ]
        for base in range(0, BLOCK, GROUP):
            copies = [
                [jnp.broadcast_to(pair[:, s:s + 1], low.shape) for s in range(base, base + GROUP)]
                for pair in pairs
            ]
            for i in range(GROUP):
                s = base + i
                for m in range(2):
                    wide = copies[m]
                    top = 1.0 / wide[i][s:s + 1, :]
                    column = jnp.where(low > s, wide[i], 0.0)
                    for j in range(i + 1, GROUP):
                        wide[j] = wide[j] - column * (wide[j][s:s + 1, :] * top)
                    pairs[m] = pairs[m] - column * (pairs[m][s:s + 1, :] * top)
        lo = k + BLOCK
        start, stop = k // 128 * 128, width + (lo + 127) // 128 * 128
        solved = []
        for m in range(2):
            diag = jnp.sum(pairs[m][:, 0:BLOCK] * small_eye, axis=1, keepdims=True)
            inv = pairs[m][:, BLOCK:] * lax.rsqrt(diag)
            solved.append(
                jnp.dot(
                    inv, work[m, k:lo, start:stop], precision=precise,
                    preferred_element_type=F32,
                )
            )
        for m in range(2):
            out_ref[m, k:lo, 0:stop - width] = solved[m][:, width - start:]
            if stop < 2 * width:
                out_ref[m, k:lo, stop - width:] = jnp.zeros((BLOCK, 2 * width - stop), F32)
        if lo < width:
            deltas = [tdot(rows[:, lo - start:width - start], rows, precise) for rows in solved]
            for m in range(2):
                work[m, lo:, start:stop] = work[m, lo:, start:stop] - deltas[m]
        yield


def apply_inverse(basis, inverse, precision):
    return lax.dot_general(
        basis, inverse, (((1,), (1,)), ((), ())), precision=precision, preferred_element_type=F32
    )


def sum_all(chips, deeps, x, total, core_buf, chip_buf, deep_buf, sems):
    me, deep, core, chip = places()
    core_sem, chip_sem, deep_sem, back_sem, last_sem = sems
    piece = chip_buf.shape[1]
    sibling = {"left": chip * 2 + (1 - core)}
    part_of = lambda q: pl.ds(pl.multiple_of(q * piece, 8), piece)
    firsts = []
    for o in range(1, chips + 1):
        q = part_of(lax.rem(chip + o, chips))
        firsts.append(send(x.at[1 - core, q], core_buf.at[q], core_sem, o - 1, sibling))
    yield
    copies = []
    for o in range(1, chips + 1):
        peer = lax.rem(chip + o, chips)
        q = part_of(peer)
        firsts[o - 1].wait()
        core_buf[q, :] += x[core, q, :]
        if o < chips:
            copies.append(
                send(core_buf.at[q], chip_buf.at[o - 1], chip_sem, o - 1, {"left": peer * 2 + core})
            )
    yield
    mine = part_of(chip)
    part = core_buf[mine, :]
    for o in range(1, chips):
        copies[o - 1].wait()
        part = part + chip_buf[o - 1]
    deep_buf[deep] = part
    copies = []
    for o in range(1, deeps):
        copies.append(
            send(
                deep_buf.at[deep], deep_buf.at[deep], deep_sem, o - 1,
                {"right": lax.rem(deep + o, deeps)},
            )
        )
    yield
    for copy in copies:
        copy.wait()
    part = deep_buf[0]
    for d in range(1, deeps):
        part = part + deep_buf[d]
    total[core, mine, :] = part
    copies = []
    for o in range(1, chips):
        copies.append(
            send(
                total.at[core, mine], total.at[core, mine], back_sem, o - 1,
                chip_peer(chip, core, o, chips),
            )
        )
    lasts = [send(total.at[core, mine], total.at[core, mine], last_sem, 0, sibling)]
    yield
    for o in range(1, chips):
        copies[o - 1].wait()
        q = part_of(lax.rem(chip + chips - o, chips))
        lasts.append(send(total.at[core, q], total.at[core, q], last_sem, o, sibling))
    yield
    for copy in lasts:
        copy.wait()


def whole_kernel(total, chips, deeps, *args):
    anys, (row_out, col_out, red_out), refs, rest = args[:8], args[8:11], args[11:19], args[19:]
    (
        tile_ref, row_own, col_own, left_scr, right_scr, sketch_scr, freq_scr, row_acc, col_acc,
        col_part, row_buf, core_buf, chip_buf, row_full, col_full,
        x_buf, t_buf, sum_core, sum_chip, sum_deep, x_last, t_last, last_core, last_chip, last_deep,
        work, inv1, inv2, mix_scr, low_scr, in_sem, out_sem, row_sem, core_sem, chip_sem, row_all, col_all, pair_all,
        *sum_sems,
    ) = rest
    lf_ref, rf_ref, ld_ref, la_ref, rd_ref, ra_ref, cs_ref, rs_ref = refs
    me, deep, core, chip = places()
    sibling = {"left": chip * 2 + (1 - core)}
    images(
        total, chips, deeps, anys, refs, tile_ref, row_own, col_own,
        left_scr, right_scr, sketch_scr, freq_scr, row_acc, col_acc, col_part,
        row_buf, core_buf, chip_buf, in_sem, row_sem, core_sem, chip_sem,
    )
    rows, cols = tile_ref.shape
    width, ports = row_out.shape[1], ld_ref.shape[0]
    chunks, blocks = rows // UNIT, cols // UNIT
    share, block = rows // deeps, col_own.shape[0] // 2
    seg, quarter = share // chunks, chips * block
    cols_at = lambda h, c: pl.multiple_of(h * 2 * quarter + core * quarter + c * block, 8)

    def sum_round(n, row, col):
        store_gram(x_buf.at[n], 0, tdot(row, row, precise))
        store_gram(x_buf.at[n], 1, tdot(col, col, precise))
        return sum_all(
            chips, deeps, x_buf.at[n], t_buf.at[n], sum_core.at[n], sum_chip.at[n],
            sum_deep.at[n], [s.at[n] for s in sum_sems],
        )

    def row_spread(c):
        src = pl.ds(c * seg, seg)
        dst = pl.ds(pl.multiple_of(deep * share + c * seg, 8), seg)
        return [
            send(
                row_own.at[src], row_full.at[dst], row_all.at[c], o - 1,
                {"right": lax.rem(deep + o, deeps)},
            )
            for o in range(1, deeps)
        ]

    def col_spread(h):
        return [
            send(
                col_own.at[pl.ds(h * block, block)], col_full.at[pl.ds(cols_at(h, chip), block)],
                col_all.at[h], o - 1, chip_peer(chip, core, o, chips),
            )
            for o in range(1, chips)
        ]

    def col_share(h, copies):
        for copy in copies:
            copy.wait()
        own = pl.ds(cols_at(h, 0), quarter)
        return send(col_full.at[own], col_full.at[own], pair_all, h, sibling)

    def mixed(value, m, terms):
        return jnp.dot(
            join_parts(value, LEFT_PARTS[:terms], 1), mix_scr[m, 0:terms * width, :],
            preferred_element_type=F32,
        )

    row_copies = row_spread(0)
    col_copies = [col_spread(0)]
    for _ in sum_round(0, row_own[...], col_own[...]):
        pass
    col_copies.append(col_spread(1))
    for c in range(1, chunks):
        row_copies += row_spread(c)
    row_full[pl.ds(pl.multiple_of(deep * share, 8), share), :] = row_own[...]
    for h in range(2):
        col_full[pl.ds(cols_at(h, chip), block), :] = col_own[h * block:(h + 1) * block, :]
    pair = []
    for n, _ in enumerate(factor(True, t_buf.at[0], inv1, work)):
        if n == 1:
            pair.append(col_share(0, col_copies[0]))
    pair.append(col_share(1, col_copies[1]))
    for m in range(2):
        mix_scr[m] = join_parts(inv1[m].T, RIGHT_PARTS, 0)
    row_out[...] = mixed(row_own[...], 0, 6)
    second = sum_round(1, row_out[...], mixed(col_own[...], 1, 6))
    next(second, None)
    work[0, 0:48, 0:width] = jnp.zeros((48, width), F32)

    def cols_of(which):
        per = quarter // UNIT

        @pl.loop(0, 2 * per)
        def _(i):
            b = (i // per) * 2 * per + which * per + lax.rem(i, per)
            cl = pl.ds(pl.multiple_of(b * UNIT, UNIT), UNIT)
            value = mixed(col_full[cl, :], 1, 6)
            col_part[cl, :] = value
            high = value.astype(BF16)
            low = (value - high.astype(F32)).astype(BF16)
            cs_ref[cl, :] = high
            low_scr[cl, :] = low
            right = join_parts(ra_ref[:, cl], (0, 1, 2), 0)
            work[0, 0:48, 0:width] += jnp.dot(
                jnp.concatenate([right, right], axis=1), jnp.concatenate([high, low], axis=0),
                preferred_element_type=F32,
            )

    cols_of(core)
    next(second, None)
    for copy in pair:
        copy.wait()
    cols_of(1 - core)
    next(second, None)

    def apply_rows(c):
        sl = pl.ds(pl.multiple_of(c * UNIT, UNIT), UNIT)
        tile = tile_ref[sl, :]
        row_acc[c] = jnp.dot(tile, cs_ref[...], preferred_element_type=F32) + jnp.dot(
            tile, low_scr[...], preferred_element_type=F32
        )

    for part in range(2):
        pl.loop(part * chunks // 2, (part + 1) * chunks // 2)(apply_rows)
        next(second, None)
    low = (work[0, 0:16, 0:width] + work[0, 16:32, 0:width] + work[0, 32:48, 0:width]) * (-1.0 / total)
    work[0, :, 0:width] = jnp.zeros((width, width), F32)
    for p in (0, 2, 5):
        at = (6 + p) * ports
        work[0, at:at + ports, 0:width] = low
    low = work[0, :, 0:width]
    work[0] = jnp.zeros((width, 2 * width), F32)
    work[1, :, 0:width] = jnp.zeros((width, width), F32)
    for copy in row_copies:
        copy.wait()

    @pl.loop(0, chunks)
    def _(c):
        sl = pl.ds(pl.multiple_of(c * UNIT, UNIT), UNIT)
        applied = row_acc[c]
        freq = jnp.concatenate([freq_scr[sl, :] * (1.0 / total)] * (width // 128), axis=1)
        both = jnp.concatenate([applied, applied * freq], axis=1)
        both_hi = both.astype(BF16)
        both_lo = (both - both_hi.astype(F32)).astype(BF16)
        q = mixed(row_full[sl, :], 0, 6).T
        q_hi = q.astype(BF16)
        q_lo = (q - q_hi.astype(F32)).astype(BF16)
        work[0] += jnp.dot(
            jnp.concatenate([q_hi, q_hi, q_lo], axis=1),
            jnp.concatenate([both_hi, both_lo, both_hi], axis=0),
            preferred_element_type=F32,
        )
        left = left_scr[sl, :]
        work[1, :, 0:width] += jnp.dot(
            jnp.concatenate([q_hi, q_lo], axis=1), jnp.concatenate([left, left], axis=0),
            preferred_element_type=F32,
        )

    shifted = work[0, :, width:] + jnp.dot(
        work[1, :, 0:width], low, precision=precise, preferred_element_type=F32
    )
    for n in range(width // 128):
        x_last[0, n * width:(n + 1) * width, :] = work[0, :, n * 128:(n + 1) * 128]
        x_last[1, n * width:(n + 1) * width, :] = shifted[:, n * 128:(n + 1) * 128]
    for _ in second:
        pass
    last = sum_all(
        chips, deeps, x_last, t_last, last_core, last_chip, last_deep, [s.at[2] for s in sum_sems]
    )
    next(last, None)
    for _ in factor(False, t_buf.at[1], inv2, work):
        next(last, None)
    for m in range(2):
        mix_scr[m, 0:3 * width, :] = join_parts(inv2[m].T, RIGHT_PARTS[:3], 0)

    @pl.loop(0, blocks)
    def _(b):
        cl = pl.ds(pl.multiple_of(b * UNIT, UNIT), UNIT)
        col_part[cl, :] = mixed(col_part[cl, :], 1, 3) * math.sqrt(cols * deeps)
        pltpu.make_async_copy(col_part.at[cl], col_out.at[cl], out_sem.at[b]).start()

    row_out[...] = mixed(row_out[...], 0, 3) * math.sqrt(rows * chips * 2)
    for _ in last:
        pass
    for m in range(2):
        summed = jnp.concatenate(
            [t_last[m, n * width:(n + 1) * width, :] for n in range(width // 128)], axis=1
        )
        red_out[m] = apply_inverse(
            jnp.dot(inv2[0], summed, precision=precise, preferred_element_type=F32),
            inv2[1], precise,
        )
    for b in range(blocks):
        cl = pl.ds(b * UNIT, UNIT)
        pltpu.make_async_copy(col_part.at[cl], col_out.at[cl], out_sem.at[b]).wait()


def deliver_kernel(row_in, col_in, red_in, row_out, col_out, low_out, shift_out):
    col_out[...] = col_in[...]

    @pl.when(pl.program_id(0) == 0)
    def _():
        row_out[...] = row_in[...]
        low_out[...] = red_in[0]
        shift_out[...] = red_in[1]


def deliver(row_basis, col_basis, reduced):
    shapes = [row_basis.shape, col_basis.shape, reduced.shape[1:], reduced.shape[1:]]
    width, tall = row_basis.shape[1], col_basis.shape[0] // 4
    fixed = lambda shape: pl.BlockSpec(shape, lambda i: (0,) * len(shape))
    moving = pl.BlockSpec((tall, width), lambda i: (i, 0))
    return pl.pallas_call(
        deliver_kernel,
        grid=(4,),
        in_specs=[fixed(row_basis.shape), moving, fixed(reduced.shape)],
        out_specs=[fixed(shapes[0]), moving, fixed(shapes[2]), fixed(shapes[3])],
        out_shape=[jax.ShapeDtypeStruct(shape, F32) for shape in shapes],
        name="deliver",
    )(row_basis, col_basis, reduced)


def body(lf, rf, ld, la, rd, ra, cs, rs):
    rows, cols = lf.shape[0], rf.shape[0]
    ports, width = ld.shape[0], cs.shape[1]
    left_n, right_n = lax.axis_size("left"), lax.axis_size("right")
    total_rows = rows * left_n
    chips, deeps = left_n // 2, right_n
    steps = deeps.bit_length() - 1
    chunks, blocks = rows // UNIT, cols // UNIT
    block, share = cols // 4 // chips, rows // deeps
    high, full = 128 * len(triangle(width)), width * width // 128
    args = (lf[None, :], rf[None, :], ld, la, rd, ra, cs, rs)
    sems = lambda n, m: pltpu.SemaphoreType.DMA((n, 2, m))
    row_basis, col_basis, reduced = pl.pallas_call(
        functools.partial(whole_kernel, float(total_rows), chips, deeps),
        in_specs=[pl.BlockSpec(memory_space=pl.ANY)] * 8,
        out_specs=[
            pl.BlockSpec(memory_space=pltpu.VMEM),
            pl.BlockSpec(memory_space=pl.ANY),
            pl.BlockSpec(memory_space=pltpu.VMEM),
        ],
        out_shape=[
            jax.ShapeDtypeStruct((share, width), F32),
            jax.ShapeDtypeStruct((cols, width), F32),
            jax.ShapeDtypeStruct((2, width, width), F32),
        ],
        scratch_shapes=[pltpu.VMEM(x.shape, x.dtype) for x in args] + [
            pltpu.VMEM((rows, cols), BF16),
            pltpu.VMEM((share, width), F32),
            pltpu.VMEM((2 * block, width), F32),
            pltpu.VMEM((rows, 256), BF16),
            pltpu.VMEM((256, cols), BF16),
            pltpu.VMEM((chunks, width, UNIT), BF16),
            pltpu.VMEM((rows, 128), F32),
            pltpu.VMEM((chunks, UNIT, width), F32),
            pltpu.VMEM((blocks, width, UNIT), F32),
            pltpu.VMEM((cols, width), F32),
            pltpu.VMEM((chunks, UNIT, width), F32),
            pltpu.VMEM((2, cols // 4, width), F32),
            pltpu.VMEM((2, chips - 1, block, width), F32),
            pltpu.VMEM((rows, width), F32),
            pltpu.VMEM((cols, width), F32),
            pltpu.VMEM((2, 2, high, 128), F32),
            pltpu.VMEM((2, 2, high, 128), F32),
            pltpu.VMEM((2, high, 128), F32),
            pltpu.VMEM((2, chips - 1, high // chips, 128), F32),
            pltpu.VMEM((2, deeps, high // chips, 128), F32),
            pltpu.VMEM((2, full, 128), F32),
            pltpu.VMEM((2, full, 128), F32),
            pltpu.VMEM((full, 128), F32),
            pltpu.VMEM((chips - 1, full // chips, 128), F32),
            pltpu.VMEM((deeps, full // chips, 128), F32),
            pltpu.VMEM((2, width, 2 * width), F32),
            pltpu.VMEM((2, width, width), F32),
            pltpu.VMEM((2, width, width), F32),
            pltpu.VMEM((2, 6 * width, width), BF16),
            pltpu.VMEM((cols, width), BF16),
            pltpu.SemaphoreType.DMA((8,)),
            pltpu.SemaphoreType.DMA((blocks,)),
            sems(chunks, steps), sems(2, chips), sems(2, chips - 1),
            sems(chunks, deeps - 1), sems(2, chips - 1), pltpu.SemaphoreType.DMA((2, 2)),
            sems(3, chips), sems(3, chips - 1), sems(3, deeps - 1), sems(3, chips - 1),
            sems(3, chips),
        ],
        compiler_params=pltpu.CompilerParams(
            collective_id=1, has_side_effects=True, vmem_limit_bytes=63 << 20
        ),
        name="loewner",
    )(*args)
    return deliver(row_basis, col_basis, reduced)


def solution(mesh):
    in_specs = (
        P("left"), P("right"), P(None, "left"), P(None, "left"),
        P(None, "right"), P(None, "right"), P("right", None), P("left", None),
    )
    out_specs = (P(("left", "right"), None), P("right", None), P(), P())
    return jax.shard_map(body, mesh=mesh, in_specs=in_specs, out_specs=out_specs, check_vma=False)
```

```python
import functools
import math

import jax
import jax.numpy as jnp
from jax import lax
from jax.experimental import pallas as pl
from jax.experimental.pallas import tpu as pltpu
from jax.sharding import PartitionSpec as P

precise = lax.Precision.HIGHEST
F32 = jnp.float32
BF16 = jnp.bfloat16
LEFT_PARTS = (0, 0, 1, 0, 1, 2)
RIGHT_PARTS = (0, 1, 0, 2, 1, 0)


def tdot(a, b, precision=None):
    return lax.dot_general(
        a, b, (((0,), (0,)), ((), ())), precision=precision, preferred_element_type=F32
    )


def split3(x):
    one = x.astype(BF16).astype(F32)
    rest = x - one
    two = rest.astype(BF16).astype(F32)
    return (one, two, (rest - two).astype(BF16).astype(F32))


def join_parts(x, order, axis):
    parts = split3(x)
    return jnp.concatenate([parts[p].astype(BF16) for p in order], axis=axis)


def stack_parts(first, second, order):
    a, b = split3(first), split3(second)
    pieces = [a[p] for p in order] + [b[p] for p in order]
    pad = jnp.zeros((256 - 12 * first.shape[0], first.shape[1]), F32)
    return jnp.concatenate(pieces + [pad], axis=0)


UNIT = 512


def places():
    me, deep = lax.axis_index("left"), lax.axis_index("right")
    core = lax.rem(me, 2)
    return me, deep, core, me // 2


def chip_peer(chip, core, offset, chips):
    return {"left": lax.rem(chip + offset, chips) * 2 + core}


def peers_of(chips, deeps):
    me, deep, core, chip = places()
    peers = [{"left": chip * 2 + (1 - core)}]
    peers += [chip_peer(chip, core, o, chips) for o in range(1, chips)]
    peers += [{"right": lax.rem(deep + o, deeps)} for o in range(1, deeps)]
    return peers


def greet_start(chips, deeps):
    barrier = pltpu.get_barrier_semaphore()
    for peer in peers_of(chips, deeps):
        pl.semaphore_signal(
            barrier, inc=1, device_id=peer, device_id_type=pl.DeviceIdType.MESH
        )


def greet_end(chips, deeps):
    pl.semaphore_wait(pltpu.get_barrier_semaphore(), chips + deeps - 1)


def greet(chips, deeps):
    greet_start(chips, deeps)
    greet_end(chips, deeps)


def send(src, dst, sems, slot, peer):
    copy = pltpu.make_async_remote_copy(
        src_ref=src,
        dst_ref=dst,
        send_sem=sems.at[0, slot],
        recv_sem=sems.at[1, slot],
        device_id=peer,
        device_id_type=pl.DeviceIdType.MESH,
    )
    copy.start()
    return copy


def reversed_bits(p, bits):
    return sum(((p >> i) & 1) << (bits - 1 - i) for i in range(bits))


def images(
    total, chips, deeps, anys, refs, tile_ref, row_out, col_out,
    left_scr, right_scr, sketch_scr, freq_scr, row_acc, col_acc, col_part,
    row_buf, core_buf, chip_buf,
    in_sem, row_sem, core_sem, chip_sem, on_cols,
):
    lf_any, rf_any, ld_any, la_any, rd_any, ra_any, cs_any, rs_any = anys
    lf_ref, rf_ref, ld_ref, la_ref, rd_ref, ra_ref, cs_ref, rs_ref = refs
    me, deep, core, chip = places()
    rows, cols = tile_ref.shape
    width = row_out.shape[1]
    chunks, blocks = rows // UNIT, cols // UNIT
    steps = deeps.bit_length() - 1
    share, seg = rows // deeps, UNIT // deeps
    order = [reversed_bits(p, steps) for p in range(deeps)]
    sibling = {"left": chip * 2 + (1 - core)}
    loads = [
        pltpu.make_async_copy(src, dst, in_sem.at[n])
        for n, (src, dst) in enumerate(
            [
                (lf_any, lf_ref), (la_any, la_ref), (ld_any, ld_ref), (rs_any, rs_ref),
                (rf_any, rf_ref), (rd_any, rd_ref), (ra_any, ra_ref), (cs_any, cs_ref),
            ]
        )
    ]
    for load in loads:
        load.start()
    greet_start(chips, deeps)

    @pl.loop(0, chunks)
    def _(c):
        row_acc[c] = jnp.zeros((UNIT, width), F32)

    @pl.loop(0, blocks)
    def _(b):
        col_acc[b] = jnp.zeros((width, UNIT), F32)

    for load in loads[:4]:
        load.wait()
    for r in range(0, rows, UNIT):
        wide = jnp.broadcast_to(lf_ref[:, r:r + UNIT] * total, (128, UNIT))
        freq_scr[r:r + UNIT, :] = wide.T
        stacked = stack_parts(la_ref[:, r:r + UNIT], -ld_ref[:, r:r + UNIT], LEFT_PARTS)
        left_scr[r:r + UNIT, :] = stacked.T.astype(BF16)
    for c in range(chunks):
        part = jnp.concatenate(
            [rs_ref[d * share + c * seg:d * share + (c + 1) * seg, :] for d in order], axis=0
        )
        sketch_scr[c] = part.astype(F32).T.astype(BF16)
    for load in loads[4:]:
        load.wait()

    @pl.loop(0, blocks)
    def _(b):
        cl = pl.ds(pl.multiple_of(b * UNIT, UNIT), UNIT)
        right_scr[:, cl] = stack_parts(rd_ref[:, cl], ra_ref[:, cl], RIGHT_PARTS).astype(BF16)

    def tiles(c, low, high, last):
        own = [pl.ds(d * share + c * seg, seg) for d in order]

        @pl.loop(low, high)
        def _(b):
            cl = pl.ds(pl.multiple_of(b * UNIT, UNIT), UNIT)
            left = jnp.concatenate([left_scr[sl, :] for sl in own], axis=0)
            freq = jnp.concatenate([freq_scr[sl, :] for sl in own], axis=0)
            numer = jnp.dot(left, right_scr[:, cl], preferred_element_type=F32)
            gap = jnp.concatenate([freq] * (UNIT // 128), axis=1) - rf_ref[:, cl] * total
            tile = (numer / gap).astype(BF16)
            for p, sl in enumerate(own):
                tile_ref[sl, cl] = tile[p * seg:(p + 1) * seg, :]
            row_acc[c] += jnp.dot(tile, cs_ref[cl, :], preferred_element_type=F32)
            part = jnp.dot(sketch_scr[c], tile, preferred_element_type=F32)
            if last:
                col_part[cl, :] = (col_acc[b] + part).T
            else:
                col_acc[b] += part

    def bit(s):
        return lax.rem(deep // (1 << s), 2)

    def segment(s):
        start, size = 0, UNIT
        for t in range(s):
            size = size // 2
            start = start + bit(t) * size
        return start, size

    def halve(c, s):
        start, size = segment(s)
        half = size // 2
        src = pl.ds(pl.multiple_of(start + (1 - bit(s)) * half, 8), half)
        slot = pl.ds(UNIT - size, half)
        return send(
            row_acc.at[c, src], row_buf.at[c, slot], row_sem.at[c], s,
            {"right": deep + (1 - 2 * bit(s)) * (1 << s)},
        )

    def settle(c, s, copy):
        copy.wait()
        start, size = segment(s)
        half = size // 2
        mine = pl.ds(pl.multiple_of(start + bit(s) * half, 8), half)
        value = row_acc[c, mine, :] + row_buf[c, UNIT - size:UNIT - size + half, :]
        if s == steps - 1:
            row_out[c * seg:(c + 1) * seg, :] = value
            return None
        row_acc[c, mine, :] = value
        return halve(c, s + 1)

    half_cols, quarter = cols // 2, cols // 4
    piece = quarter // chips

    def pair_start(h):
        copies = []
        for o in range(1, chips + 1):
            peer = lax.rem(chip + o, chips)
            at = pl.multiple_of(peer * piece, 8)
            src = pl.ds(h * half_cols + (1 - core) * quarter + at, piece)
            copies.append(
                send(
                    col_part.at[src], core_buf.at[h, pl.ds(at, piece)], core_sem.at[h], o - 1,
                    sibling,
                )
            )
        return copies

    def pair_end(h, copies):
        sent = []
        for o in range(1, chips + 1):
            peer = lax.rem(chip + o, chips)
            at = pl.multiple_of(peer * piece, 8)
            copies[o - 1].wait()
            dst = pl.ds(at, piece)
            core_buf[h, dst, :] += col_part[pl.ds(h * half_cols + core * quarter + at, piece), :]
            if o < chips:
                sent.append(
                    send(
                        core_buf.at[h, dst], chip_buf.at[h, o - 1], chip_sem.at[h], o - 1,
                        {"left": peer * 2 + core},
                    )
                )
        return sent

    def chip_end(h, copies):
        value = core_buf[h, pl.ds(pl.multiple_of(chip * piece, 8), piece), :]
        for o in range(1, chips):
            copies[o - 1].wait()
            value = value + chip_buf[h, o - 1]
        col_out[h * piece:(h + 1) * piece, :] = value

    z = [None] * chunks
    mid = blocks // 2
    early = chunks // 2
    for c in range(early):
        tiles(c, 0, blocks, False)
        if c == 0:
            greet_end(chips, deeps)
        z[c] = halve(c, 0)
    for c in range(early, chunks):
        tiles(c, 0, mid, c == chunks - 1)
        if c == early:
            z[0] = settle(0, 0, z[0])
    pair = pair_start(0)
    for c in range(early, chunks):
        tiles(c, mid, blocks, c == chunks - 1)
        z[c] = halve(c, 0)
        if c == early:
            chip_first = pair_end(0, pair)
            for e in range(1, early):
                z[e] = settle(e, 0, z[e])
    pair = pair_start(1)
    chip_second = pair_end(1, pair)
    for s in range(1, steps):
        for c in range(early):
            z[c] = settle(c, s, z[c])
    for s in range(steps):
        if s == steps - 1:
            chip_end(0, chip_first)
            chip_end(1, chip_second)
            on_cols()
        for c in range(early, chunks):
            z[c] = settle(c, s, z[c])


BLOCK = 64
GROUP = 8


def triangle(width):
    return [(i, j) for i in range(width // 128) for j in range(i, width // 128)]


def store_gram(dst, m, gram):
    for n, (i, j) in enumerate(triangle(gram.shape[0])):
        dst[m, n * 128:(n + 1) * 128, :] = gram[i * 128:(i + 1) * 128, j * 128:(j + 1) * 128]


def factor(shifted, t_ref, out_ref, work):
    width = out_ref.shape[-1]
    row_id = lax.broadcasted_iota(jnp.int32, (width, width), 0)
    col_id = lax.broadcasted_iota(jnp.int32, (width, width), 1)
    eye = (row_id == col_id).astype(F32)
    for m in range(2):
        work[m, :, 0:width] = jnp.zeros((width, width), F32)
        for n, (i, j) in enumerate(triangle(width)):
            work[m, i * 128:(i + 1) * 128, j * 128:(j + 1) * 128] = t_ref[m, n * 128:(n + 1) * 128, :]
        if shifted:
            gram = work[m, :, 0:width]
            trace = jnp.sum(jnp.sum(gram * eye, axis=1, keepdims=True), axis=0, keepdims=True)
            work[m, :, 0:width] = gram + (1e-05 * trace / width) * eye
        work[m, :, width:] = eye
    brow = lax.broadcasted_iota(jnp.int32, (BLOCK, BLOCK), 0)
    bcol = lax.broadcasted_iota(jnp.int32, (BLOCK, BLOCK), 1)
    small_eye = (brow == bcol).astype(F32)
    low = lax.broadcasted_iota(jnp.int32, (BLOCK, 2 * BLOCK), 0)
    for k in range(0, width, BLOCK):
        pairs = [
            jnp.concatenate([work[m, k:k + BLOCK, k:k + BLOCK], small_eye], axis=1)
            for m in range(2)
        ]
        for base in range(0, BLOCK, GROUP):
            copies = [
                [jnp.broadcast_to(pair[:, s:s + 1], low.shape) for s in range(base, base + GROUP)]
                for pair in pairs
            ]
            for i in range(GROUP):
                s = base + i
                for m in range(2):
                    wide = copies[m]
                    top = 1.0 / wide[i][s:s + 1, :]
                    column = jnp.where(low > s, wide[i], 0.0)
                    for j in range(i + 1, GROUP):
                        wide[j] = wide[j] - column * (wide[j][s:s + 1, :] * top)
                    pairs[m] = pairs[m] - column * (pairs[m][s:s + 1, :] * top)
        lo = k + BLOCK
        start, stop = k // 128 * 128, width + (lo + 127) // 128 * 128
        solved = []
        for m in range(2):
            diag = jnp.sum(pairs[m][:, 0:BLOCK] * small_eye, axis=1, keepdims=True)
            inv = pairs[m][:, BLOCK:] * lax.rsqrt(diag)
            solved.append(
                jnp.dot(
                    inv, work[m, k:lo, start:stop], precision=precise,
                    preferred_element_type=F32,
                )
            )
        for m in range(2):
            out_ref[m, k:lo, 0:stop - width] = solved[m][:, width - start:]
            if stop < 2 * width:
                out_ref[m, k:lo, stop - width:] = jnp.zeros((BLOCK, 2 * width - stop), F32)
        if lo < width:
            deltas = [tdot(rows[:, lo - start:width - start], rows, precise) for rows in solved]
            for m in range(2):
                work[m, lo:, start:stop] = work[m, lo:, start:stop] - deltas[m]
        yield


def apply_inverse(basis, inverse, precision):
    return lax.dot_general(
        basis, inverse, (((1,), (1,)), ((), ())), precision=precision, preferred_element_type=F32
    )


def sum_all(chips, deeps, x, total, core_buf, chip_buf, deep_buf, sems):
    me, deep, core, chip = places()
    core_sem, chip_sem, deep_sem, back_sem, last_sem = sems
    piece = chip_buf.shape[1]
    sibling = {"left": chip * 2 + (1 - core)}
    part_of = lambda q: pl.ds(pl.multiple_of(q * piece, 8), piece)
    firsts = []
    for o in range(1, chips + 1):
        q = part_of(lax.rem(chip + o, chips))
        firsts.append(send(x.at[1 - core, q], core_buf.at[q], core_sem, o - 1, sibling))
    yield
    copies = []
    for o in range(1, chips + 1):
        peer = lax.rem(chip + o, chips)
        q = part_of(peer)
        firsts[o - 1].wait()
        core_buf[q, :] += x[core, q, :]
        if o < chips:
            copies.append(
                send(core_buf.at[q], chip_buf.at[o - 1], chip_sem, o - 1, {"left": peer * 2 + core})
            )
    yield
    mine = part_of(chip)
    part = core_buf[mine, :]
    for o in range(1, chips):
        copies[o - 1].wait()
        part = part + chip_buf[o - 1]
    deep_buf[deep] = part
    copies = []
    for o in range(1, deeps):
        copies.append(
            send(
                deep_buf.at[deep], deep_buf.at[deep], deep_sem, o - 1,
                {"right": lax.rem(deep + o, deeps)},
            )
        )
    yield
    for copy in copies:
        copy.wait()
    part = deep_buf[0]
    for d in range(1, deeps):
        part = part + deep_buf[d]
    total[core, mine, :] = part
    copies = []
    for o in range(1, chips):
        copies.append(
            send(
                total.at[core, mine], total.at[core, mine], back_sem, o - 1,
                chip_peer(chip, core, o, chips),
            )
        )
    lasts = [send(total.at[core, mine], total.at[core, mine], last_sem, 0, sibling)]
    yield
    for o in range(1, chips):
        copies[o - 1].wait()
        q = part_of(lax.rem(chip + chips - o, chips))
        lasts.append(send(total.at[core, q], total.at[core, q], last_sem, o, sibling))
    yield
    for copy in lasts:
        copy.wait()


def whole_kernel(total, chips, deeps, *args):
    anys, (row_out, col_out, red_out), refs, rest = args[:8], args[8:11], args[11:19], args[19:]
    (
        tile_ref, row_own, col_own, left_scr, right_scr, sketch_scr, freq_scr, row_acc, col_acc,
        col_part, row_buf, core_buf, chip_buf, row_full, col_full,
        x_buf, t_buf, sum_core, sum_chip, sum_deep, x_last, t_last, last_core, last_chip, last_deep,
        work, inv1, inv2, mix_scr, low_scr, in_sem, out_sem, row_sem, core_sem, chip_sem, row_all, col_all, pair_all,
        *sum_sems,
    ) = rest
    lf_ref, rf_ref, ld_ref, la_ref, rd_ref, ra_ref, cs_ref, rs_ref = refs
    me, deep, core, chip = places()
    sibling = {"left": chip * 2 + (1 - core)}
    rows, cols = tile_ref.shape
    width, ports = row_out.shape[1], ld_ref.shape[0]
    chunks, blocks = rows // UNIT, cols // UNIT
    share, block = rows // deeps, col_own.shape[0] // 2
    seg, quarter = share // chunks, chips * block
    cols_at = lambda h, c: pl.multiple_of(h * 2 * quarter + core * quarter + c * block, 8)

    def sum_round(n, row, col):
        store_gram(x_buf.at[n], 0, tdot(row, row, precise))
        store_gram(x_buf.at[n], 1, tdot(col, col, precise))
        return sum_all(
            chips, deeps, x_buf.at[n], t_buf.at[n], sum_core.at[n], sum_chip.at[n],
            sum_deep.at[n], [s.at[n] for s in sum_sems],
        )

    steps = deeps.bit_length() - 1
    row_copies = [[] for _ in range(chunks)]

    def row_step(c, i):
        for copy in row_copies[c]:
            copy.wait()
        near = 1 << (steps - 1 - i)
        side = lax.rem(deep // near, 2)
        row_copies[c] = []
        for n in range(1 << i):
            d = n * 2 * near + lax.rem(deep, 2 * near)
            at = pl.ds(pl.multiple_of(d * share + c * seg, 8), seg)
            row_copies[c].append(
                send(
                    row_full.at[at], row_full.at[at], row_all.at[c], (1 << i) - 1 + n,
                    {"right": deep + (1 - 2 * side) * near},
                )
            )

    def col_spread(h):
        return [
            send(
                col_own.at[pl.ds(h * block, block)], col_full.at[pl.ds(cols_at(h, chip), block)],
                col_all.at[h], o - 1, chip_peer(chip, core, o, chips),
            )
            for o in range(1, chips)
        ]

    def col_share(h, copies):
        for copy in copies:
            copy.wait()
        own = pl.ds(cols_at(h, 0), quarter)
        return send(col_full.at[own], col_full.at[own], pair_all, h, sibling)

    def mixed(value, m, terms):
        return jnp.dot(
            join_parts(value, LEFT_PARTS[:terms], 1), mix_scr[m, 0:terms * width, :],
            preferred_element_type=F32,
        )

    col_copies = []
    images(
        total, chips, deeps, anys, refs, tile_ref, row_own, col_own,
        left_scr, right_scr, sketch_scr, freq_scr, row_acc, col_acc, col_part,
        row_buf, core_buf, chip_buf, in_sem, row_sem, core_sem, chip_sem,
        lambda: col_copies.append(col_spread(0)),
    )
    row_full[pl.ds(pl.multiple_of(deep * share, 8), share), :] = row_own[...]
    half = chunks // 2
    for c in range(half):
        row_step(c, 0)
    for h in range(2):
        col_full[pl.ds(cols_at(h, chip), block), :] = col_own[h * block:(h + 1) * block, :]
    for n, _ in enumerate(sum_round(0, row_own[...], col_own[...])):
        if n == 2:
            col_copies.append(col_spread(1))
        if n == 3:
            for c in range(half, chunks):
                row_step(c, 0)
    for c in range(half):
        row_step(c, 1)
    pair = [col_share(0, col_copies[0])]
    for n, _ in enumerate(factor(True, t_buf.at[0], inv1, work)):
        if n == 1:
            pair.append(col_share(1, col_copies[1]))
        if n == 2:
            for c in range(half, chunks):
                row_step(c, 1)
    for i in range(2, steps):
        for c in range(chunks):
            row_step(c, i)
    for m in range(2):
        mix_scr[m] = join_parts(inv1[m].T, RIGHT_PARTS, 0)
    row_out[...] = mixed(row_own[...], 0, 6)
    second = sum_round(1, row_out[...], mixed(col_own[...], 1, 6))
    next(second, None)
    work[0, 0:48, 0:width] = jnp.zeros((48, width), F32)

    def cols_of(which):
        per = quarter // UNIT

        @pl.loop(0, 2 * per)
        def _(i):
            b = (i // per) * 2 * per + which * per + lax.rem(i, per)
            cl = pl.ds(pl.multiple_of(b * UNIT, UNIT), UNIT)
            value = mixed(col_full[cl, :], 1, 6)
            col_part[cl, :] = value
            high = value.astype(BF16)
            low = (value - high.astype(F32)).astype(BF16)
            cs_ref[cl, :] = high
            low_scr[cl, :] = low
            right = join_parts(ra_ref[:, cl], (0, 1, 2), 0)
            work[0, 0:48, 0:width] += jnp.dot(
                jnp.concatenate([right, right], axis=1), jnp.concatenate([high, low], axis=0),
                preferred_element_type=F32,
            )

    cols_of(core)
    next(second, None)
    for copy in pair:
        copy.wait()
    cols_of(1 - core)
    next(second, None)

    def apply_rows(c):
        sl = pl.ds(pl.multiple_of(c * UNIT, UNIT), UNIT)
        tile = tile_ref[sl, :]
        row_acc[c] = jnp.dot(tile, cs_ref[...], preferred_element_type=F32) + jnp.dot(
            tile, low_scr[...], preferred_element_type=F32
        )

    for part in range(2):
        pl.loop(part * chunks // 2, (part + 1) * chunks // 2)(apply_rows)
        next(second, None)
    low = (work[0, 0:16, 0:width] + work[0, 16:32, 0:width] + work[0, 32:48, 0:width]) * (-1.0 / total)
    work[0, :, 0:width] = jnp.zeros((width, width), F32)
    for p in (0, 2, 5):
        at = (6 + p) * ports
        work[0, at:at + ports, 0:width] = low
    low = work[0, :, 0:width]
    work[0] = jnp.zeros((width, 2 * width), F32)
    work[1, :, 0:width] = jnp.zeros((width, width), F32)
    for copies in row_copies:
        for copy in copies:
            copy.wait()

    @pl.loop(0, chunks)
    def _(c):
        sl = pl.ds(pl.multiple_of(c * UNIT, UNIT), UNIT)
        applied = row_acc[c]
        freq = jnp.concatenate([freq_scr[sl, :] * (1.0 / total)] * (width // 128), axis=1)
        both = jnp.concatenate([applied, applied * freq], axis=1)
        both_hi = both.astype(BF16)
        both_lo = (both - both_hi.astype(F32)).astype(BF16)
        q = mixed(row_full[sl, :], 0, 6).T
        q_hi = q.astype(BF16)
        q_lo = (q - q_hi.astype(F32)).astype(BF16)
        work[0] += jnp.dot(
            jnp.concatenate([q_hi, q_hi, q_lo], axis=1),
            jnp.concatenate([both_hi, both_lo, both_hi], axis=0),
            preferred_element_type=F32,
        )
        left = left_scr[sl, :]
        work[1, :, 0:width] += jnp.dot(
            jnp.concatenate([q_hi, q_lo], axis=1), jnp.concatenate([left, left], axis=0),
            preferred_element_type=F32,
        )

    shifted = work[0, :, width:] + jnp.dot(
        work[1, :, 0:width], low, precision=precise, preferred_element_type=F32
    )
    for n in range(width // 128):
        x_last[0, n * width:(n + 1) * width, :] = work[0, :, n * 128:(n + 1) * 128]
        x_last[1, n * width:(n + 1) * width, :] = shifted[:, n * 128:(n + 1) * 128]
    for _ in second:
        pass
    last = sum_all(
        chips, deeps, x_last, t_last, last_core, last_chip, last_deep, [s.at[2] for s in sum_sems]
    )
    next(last, None)
    for _ in factor(False, t_buf.at[1], inv2, work):
        next(last, None)
    for m in range(2):
        mix_scr[m, 0:3 * width, :] = join_parts(inv2[m].T, RIGHT_PARTS[:3], 0)

    @pl.loop(0, blocks)
    def _(b):
        cl = pl.ds(pl.multiple_of(b * UNIT, UNIT), UNIT)
        col_part[cl, :] = mixed(col_part[cl, :], 1, 3) * math.sqrt(cols * deeps)
        pltpu.make_async_copy(col_part.at[cl], col_out.at[cl], out_sem.at[b]).start()

    row_out[...] = mixed(row_out[...], 0, 3) * math.sqrt(rows * chips * 2)
    for _ in last:
        pass
    for m in range(2):
        summed = jnp.concatenate(
            [t_last[m, n * width:(n + 1) * width, :] for n in range(width // 128)], axis=1
        )
        red_out[m] = apply_inverse(
            jnp.dot(inv2[0], summed, precision=precise, preferred_element_type=F32),
            inv2[1], precise,
        )
    for b in range(blocks):
        cl = pl.ds(b * UNIT, UNIT)
        pltpu.make_async_copy(col_part.at[cl], col_out.at[cl], out_sem.at[b]).wait()


def deliver_kernel(row_in, col_in, red_in, row_out, col_out, low_out, shift_out):
    col_out[...] = col_in[...]

    @pl.when(pl.program_id(0) == 0)
    def _():
        row_out[...] = row_in[...]
        low_out[...] = red_in[0]
        shift_out[...] = red_in[1]


def deliver(row_basis, col_basis, reduced):
    shapes = [row_basis.shape, col_basis.shape, reduced.shape[1:], reduced.shape[1:]]
    width, tall = row_basis.shape[1], col_basis.shape[0] // 4
    fixed = lambda shape: pl.BlockSpec(shape, lambda i: (0,) * len(shape))
    moving = pl.BlockSpec((tall, width), lambda i: (i, 0))
    return pl.pallas_call(
        deliver_kernel,
        grid=(4,),
        in_specs=[fixed(row_basis.shape), moving, fixed(reduced.shape)],
        out_specs=[fixed(shapes[0]), moving, fixed(shapes[2]), fixed(shapes[3])],
        out_shape=[jax.ShapeDtypeStruct(shape, F32) for shape in shapes],
        name="deliver",
    )(row_basis, col_basis, reduced)


def body(lf, rf, ld, la, rd, ra, cs, rs):
    rows, cols = lf.shape[0], rf.shape[0]
    ports, width = ld.shape[0], cs.shape[1]
    left_n, right_n = lax.axis_size("left"), lax.axis_size("right")
    total_rows = rows * left_n
    chips, deeps = left_n // 2, right_n
    steps = deeps.bit_length() - 1
    chunks, blocks = rows // UNIT, cols // UNIT
    block, share = cols // 4 // chips, rows // deeps
    high, full = 128 * len(triangle(width)), width * width // 128
    args = (lf[None, :], rf[None, :], ld, la, rd, ra, cs, rs)
    sems = lambda n, m: pltpu.SemaphoreType.DMA((n, 2, m))
    row_basis, col_basis, reduced = pl.pallas_call(
        functools.partial(whole_kernel, float(total_rows), chips, deeps),
        in_specs=[pl.BlockSpec(memory_space=pl.ANY)] * 8,
        out_specs=[
            pl.BlockSpec(memory_space=pltpu.VMEM),
            pl.BlockSpec(memory_space=pl.ANY),
            pl.BlockSpec(memory_space=pltpu.VMEM),
        ],
        out_shape=[
            jax.ShapeDtypeStruct((share, width), F32),
            jax.ShapeDtypeStruct((cols, width), F32),
            jax.ShapeDtypeStruct((2, width, width), F32),
        ],
        scratch_shapes=[pltpu.VMEM(x.shape, x.dtype) for x in args] + [
            pltpu.VMEM((rows, cols), BF16),
            pltpu.VMEM((share, width), F32),
            pltpu.VMEM((2 * block, width), F32),
            pltpu.VMEM((rows, 256), BF16),
            pltpu.VMEM((256, cols), BF16),
            pltpu.VMEM((chunks, width, UNIT), BF16),
            pltpu.VMEM((rows, 128), F32),
            pltpu.VMEM((chunks, UNIT, width), F32),
            pltpu.VMEM((blocks, width, UNIT), F32),
            pltpu.VMEM((cols, width), F32),
            pltpu.VMEM((chunks, UNIT, width), F32),
            pltpu.VMEM((2, cols // 4, width), F32),
            pltpu.VMEM((2, chips - 1, block, width), F32),
            pltpu.VMEM((rows, width), F32),
            pltpu.VMEM((cols, width), F32),
            pltpu.VMEM((2, 2, high, 128), F32),
            pltpu.VMEM((2, 2, high, 128), F32),
            pltpu.VMEM((2, high, 128), F32),
            pltpu.VMEM((2, chips - 1, high // chips, 128), F32),
            pltpu.VMEM((2, deeps, high // chips, 128), F32),
            pltpu.VMEM((2, full, 128), F32),
            pltpu.VMEM((2, full, 128), F32),
            pltpu.VMEM((full, 128), F32),
            pltpu.VMEM((chips - 1, full // chips, 128), F32),
            pltpu.VMEM((deeps, full // chips, 128), F32),
            pltpu.VMEM((2, width, 2 * width), F32),
            pltpu.VMEM((2, width, width), F32),
            pltpu.VMEM((2, width, width), F32),
            pltpu.VMEM((2, 6 * width, width), BF16),
            pltpu.VMEM((cols, width), BF16),
            pltpu.SemaphoreType.DMA((8,)),
            pltpu.SemaphoreType.DMA((blocks,)),
            sems(chunks, steps), sems(2, chips), sems(2, chips - 1),
            sems(chunks, deeps - 1), sems(2, chips - 1), pltpu.SemaphoreType.DMA((2, 2)),
            sems(3, chips), sems(3, chips - 1), sems(3, deeps - 1), sems(3, chips - 1),
            sems(3, chips),
        ],
        compiler_params=pltpu.CompilerParams(
            collective_id=1, has_side_effects=True, vmem_limit_bytes=63 << 20
        ),
        name="loewner",
    )(*args)
    return deliver(row_basis, col_basis, reduced)


def solution(mesh):
    in_specs = (
        P("left"), P("right"), P(None, "left"), P(None, "left"),
        P(None, "right"), P(None, "right"), P("right", None), P("left", None),
    )
    out_specs = (P(("left", "right"), None), P("right", None), P(), P())
    return jax.shard_map(body, mesh=mesh, in_specs=in_specs, out_specs=out_specs, check_vma=False)
```

```python
import functools
import math

import jax
import jax.numpy as jnp
from jax import lax
from jax.experimental import pallas as pl
from jax.experimental.pallas import tpu as pltpu
from jax.sharding import PartitionSpec as P

precise = lax.Precision.HIGHEST
F32 = jnp.float32
BF16 = jnp.bfloat16
LEFT_PARTS = (0, 0, 1, 0, 1, 2)
RIGHT_PARTS = (0, 1, 0, 2, 1, 0)


def tdot(a, b, precision=None):
    return lax.dot_general(
        a, b, (((0,), (0,)), ((), ())), precision=precision, preferred_element_type=F32
    )


def split3(x):
    one = x.astype(BF16).astype(F32)
    rest = x - one
    two = rest.astype(BF16).astype(F32)
    return (one, two, (rest - two).astype(BF16).astype(F32))


def join_parts(x, order, axis):
    parts = split3(x)
    return jnp.concatenate([parts[p].astype(BF16) for p in order], axis=axis)


def stack_parts(first, second, order):
    a, b = split3(first), split3(second)
    pieces = [a[p] for p in order] + [b[p] for p in order]
    pad = jnp.zeros((256 - 12 * first.shape[0], first.shape[1]), F32)
    return jnp.concatenate(pieces + [pad], axis=0)


UNIT = 512


def places():
    me, deep = lax.axis_index("left"), lax.axis_index("right")
    core = lax.rem(me, 2)
    return me, deep, core, me // 2


def chip_peer(chip, core, offset, chips):
    return {"left": lax.rem(chip + offset, chips) * 2 + core}


def peers_of(chips, deeps):
    me, deep, core, chip = places()
    peers = [{"left": chip * 2 + (1 - core)}]
    peers += [chip_peer(chip, core, o, chips) for o in range(1, chips)]
    peers += [{"right": lax.rem(deep + o, deeps)} for o in range(1, deeps)]
    return peers


def greet_start(chips, deeps):
    barrier = pltpu.get_barrier_semaphore()
    for peer in peers_of(chips, deeps):
        pl.semaphore_signal(
            barrier, inc=1, device_id=peer, device_id_type=pl.DeviceIdType.MESH
        )


def greet_end(chips, deeps):
    pl.semaphore_wait(pltpu.get_barrier_semaphore(), chips + deeps - 1)


def greet(chips, deeps):
    greet_start(chips, deeps)
    greet_end(chips, deeps)


def send(src, dst, sems, slot, peer):
    copy = pltpu.make_async_remote_copy(
        src_ref=src,
        dst_ref=dst,
        send_sem=sems.at[0, slot],
        recv_sem=sems.at[1, slot],
        device_id=peer,
        device_id_type=pl.DeviceIdType.MESH,
    )
    copy.start()
    return copy


def reversed_bits(p, bits):
    return sum(((p >> i) & 1) << (bits - 1 - i) for i in range(bits))


def images(
    total, chips, deeps, anys, refs, tile_ref, row_out, col_out,
    left_scr, right_scr, sketch_scr, freq_scr, row_acc, col_acc, col_part,
    row_buf, core_buf, chip_buf,
    in_sem, row_sem, core_sem, chip_sem, on_cols,
):
    lf_any, rf_any, ld_any, la_any, rd_any, ra_any, cs_any, rs_any = anys
    lf_ref, rf_ref, ld_ref, la_ref, rd_ref, ra_ref, cs_ref, rs_ref = refs
    me, deep, core, chip = places()
    rows, cols = tile_ref.shape
    width = row_out.shape[1]
    chunks, blocks = rows // UNIT, cols // UNIT
    steps = deeps.bit_length() - 1
    share, seg = rows // deeps, UNIT // deeps
    order = [reversed_bits(p, steps) for p in range(deeps)]
    sibling = {"left": chip * 2 + (1 - core)}
    loads = [
        pltpu.make_async_copy(src, dst, in_sem.at[n])
        for n, (src, dst) in enumerate(
            [
                (lf_any, lf_ref), (la_any, la_ref), (ld_any, ld_ref), (rs_any, rs_ref),
                (rf_any, rf_ref), (rd_any, rd_ref), (ra_any, ra_ref), (cs_any, cs_ref),
            ]
        )
    ]
    for load in loads:
        load.start()
    greet_start(chips, deeps)

    @pl.loop(0, chunks)
    def _(c):
        row_acc[c] = jnp.zeros((UNIT, width), F32)

    @pl.loop(0, blocks)
    def _(b):
        col_acc[b] = jnp.zeros((width, UNIT), F32)

    for load in loads[:4]:
        load.wait()
    for r in range(0, rows, UNIT):
        wide = jnp.broadcast_to(lf_ref[:, r:r + UNIT] * total, (128, UNIT))
        freq_scr[r:r + UNIT, :] = wide.T
        stacked = stack_parts(la_ref[:, r:r + UNIT], -ld_ref[:, r:r + UNIT], LEFT_PARTS)
        left_scr[r:r + UNIT, :] = stacked.T.astype(BF16)
    for c in range(chunks):
        part = jnp.concatenate(
            [rs_ref[d * share + c * seg:d * share + (c + 1) * seg, :] for d in order], axis=0
        )
        sketch_scr[c] = part.astype(F32).T.astype(BF16)
    for load in loads[4:]:
        load.wait()

    @pl.loop(0, blocks)
    def _(b):
        cl = pl.ds(pl.multiple_of(b * UNIT, UNIT), UNIT)
        right_scr[:, cl] = stack_parts(rd_ref[:, cl], ra_ref[:, cl], RIGHT_PARTS).astype(BF16)

    def tiles(c, low, high, last):
        own = [pl.ds(d * share + c * seg, seg) for d in order]

        @pl.loop(low, high)
        def _(b):
            cl = pl.ds(pl.multiple_of(b * UNIT, UNIT), UNIT)
            left = jnp.concatenate([left_scr[sl, :] for sl in own], axis=0)
            freq = jnp.concatenate([freq_scr[sl, :] for sl in own], axis=0)
            numer = jnp.dot(left, right_scr[:, cl], preferred_element_type=F32)
            gap = jnp.concatenate([freq] * (UNIT // 128), axis=1) - rf_ref[:, cl] * total
            tile = (numer / gap).astype(BF16)
            for p, sl in enumerate(own):
                tile_ref[sl, cl] = tile[p * seg:(p + 1) * seg, :]
            row_acc[c] += jnp.dot(tile, cs_ref[cl, :], preferred_element_type=F32)
            part = jnp.dot(sketch_scr[c], tile, preferred_element_type=F32)
            if last:
                col_part[cl, :] = (col_acc[b] + part).T
            else:
                col_acc[b] += part

    def bit(s):
        return lax.rem(deep // (1 << s), 2)

    def segment(s):
        start, size = 0, UNIT
        for t in range(s):
            size = size // 2
            start = start + bit(t) * size
        return start, size

    def halve(c, s):
        start, size = segment(s)
        half = size // 2
        src = pl.ds(pl.multiple_of(start + (1 - bit(s)) * half, 8), half)
        slot = pl.ds(UNIT - size, half)
        return send(
            row_acc.at[c, src], row_buf.at[c, slot], row_sem.at[c], s,
            {"right": deep + (1 - 2 * bit(s)) * (1 << s)},
        )

    def settle(c, s, copy):
        copy.wait()
        start, size = segment(s)
        half = size // 2
        mine = pl.ds(pl.multiple_of(start + bit(s) * half, 8), half)
        value = row_acc[c, mine, :] + row_buf[c, UNIT - size:UNIT - size + half, :]
        if s == steps - 1:
            row_out[c * seg:(c + 1) * seg, :] = value
            return None
        row_acc[c, mine, :] = value
        return halve(c, s + 1)

    half_cols, quarter = cols // 2, cols // 4
    piece = quarter // chips

    def pair_start(h):
        copies = []
        for o in range(1, chips + 1):
            peer = lax.rem(chip + o, chips)
            at = pl.multiple_of(peer * piece, 8)
            src = pl.ds(h * half_cols + (1 - core) * quarter + at, piece)
            copies.append(
                send(
                    col_part.at[src], core_buf.at[h, pl.ds(at, piece)], core_sem.at[h], o - 1,
                    sibling,
                )
            )
        return copies

    def pair_end(h, copies):
        sent = []
        for o in range(1, chips + 1):
            peer = lax.rem(chip + o, chips)
            at = pl.multiple_of(peer * piece, 8)
            copies[o - 1].wait()
            dst = pl.ds(at, piece)
            core_buf[h, dst, :] += col_part[pl.ds(h * half_cols + core * quarter + at, piece), :]
            if o < chips:
                sent.append(
                    send(
                        core_buf.at[h, dst], chip_buf.at[h, o - 1], chip_sem.at[h], o - 1,
                        {"left": peer * 2 + core},
                    )
                )
        return sent

    def chip_end(h, copies):
        value = core_buf[h, pl.ds(pl.multiple_of(chip * piece, 8), piece), :]
        for o in range(1, chips):
            copies[o - 1].wait()
            value = value + chip_buf[h, o - 1]
        col_out[h * piece:(h + 1) * piece, :] = value

    z = [None] * chunks
    mid = blocks // 2
    early = chunks // 2
    for c in range(early):
        tiles(c, 0, blocks, False)
        if c == 0:
            greet_end(chips, deeps)
        z[c] = halve(c, 0)
    for c in range(early, chunks):
        tiles(c, 0, mid, c == chunks - 1)
        if c == early:
            z[0] = settle(0, 0, z[0])
    pair = pair_start(0)
    for c in range(early, chunks):
        tiles(c, mid, blocks, c == chunks - 1)
        z[c] = halve(c, 0)
        if c == early:
            chip_first = pair_end(0, pair)
            for e in range(1, early):
                z[e] = settle(e, 0, z[e])
    pair = pair_start(1)
    chip_second = pair_end(1, pair)
    for s in range(1, steps):
        for c in range(early):
            z[c] = settle(c, s, z[c])
    for s in range(steps):
        if s == steps - 1:
            chip_end(0, chip_first)
            chip_end(1, chip_second)
            on_cols()
        for c in range(early, chunks):
            z[c] = settle(c, s, z[c])


BLOCK = 64
GROUP = 8


def triangle(width):
    return [(i, j) for i in range(width // 128) for j in range(i, width // 128)]


def store_gram(dst, m, gram):
    for n, (i, j) in enumerate(triangle(gram.shape[0])):
        dst[m, n * 128:(n + 1) * 128, :] = gram[i * 128:(i + 1) * 128, j * 128:(j + 1) * 128]


def factor(shifted, t_ref, out_ref, work):
    width = out_ref.shape[-1]
    row_id = lax.broadcasted_iota(jnp.int32, (width, width), 0)
    col_id = lax.broadcasted_iota(jnp.int32, (width, width), 1)
    eye = (row_id == col_id).astype(F32)
    for m in range(2):
        work[m, :, 0:width] = jnp.zeros((width, width), F32)
        for n, (i, j) in enumerate(triangle(width)):
            work[m, i * 128:(i + 1) * 128, j * 128:(j + 1) * 128] = t_ref[m, n * 128:(n + 1) * 128, :]
        if shifted:
            gram = work[m, :, 0:width]
            trace = jnp.sum(jnp.sum(gram * eye, axis=1, keepdims=True), axis=0, keepdims=True)
            work[m, :, 0:width] = gram + (1e-05 * trace / width) * eye
        work[m, :, width:] = eye
    brow = lax.broadcasted_iota(jnp.int32, (BLOCK, BLOCK), 0)
    bcol = lax.broadcasted_iota(jnp.int32, (BLOCK, BLOCK), 1)
    small_eye = (brow == bcol).astype(F32)
    low = lax.broadcasted_iota(jnp.int32, (BLOCK, 2 * BLOCK), 0)
    for k in range(0, width, BLOCK):
        pairs = [
            jnp.concatenate([work[m, k:k + BLOCK, k:k + BLOCK], small_eye], axis=1)
            for m in range(2)
        ]
        for base in range(0, BLOCK, GROUP):
            copies = [
                [jnp.broadcast_to(pair[:, s:s + 1], low.shape) for s in range(base, base + GROUP)]
                for pair in pairs
            ]
            for i in range(GROUP):
                s = base + i
                for m in range(2):
                    wide = copies[m]
                    top = 1.0 / wide[i][s:s + 1, :]
                    column = jnp.where(low > s, wide[i], 0.0)
                    for j in range(i + 1, GROUP):
                        wide[j] = wide[j] - column * (wide[j][s:s + 1, :] * top)
                    pairs[m] = pairs[m] - column * (pairs[m][s:s + 1, :] * top)
        lo = k + BLOCK
        start, stop = k // 128 * 128, width + (lo + 127) // 128 * 128
        solved = []
        for m in range(2):
            diag = jnp.sum(pairs[m][:, 0:BLOCK] * small_eye, axis=1, keepdims=True)
            inv = pairs[m][:, BLOCK:] * lax.rsqrt(diag)
            solved.append(
                jnp.dot(
                    inv, work[m, k:lo, start:stop], precision=precise,
                    preferred_element_type=F32,
                )
            )
        for m in range(2):
            out_ref[m, k:lo, 0:stop - width] = solved[m][:, width - start:]
            if stop < 2 * width:
                out_ref[m, k:lo, stop - width:] = jnp.zeros((BLOCK, 2 * width - stop), F32)
        if lo < width:
            deltas = [tdot(rows[:, lo - start:width - start], rows, precise) for rows in solved]
            for m in range(2):
                work[m, lo:, start:stop] = work[m, lo:, start:stop] - deltas[m]
        yield


def apply_inverse(basis, inverse, precision):
    return lax.dot_general(
        basis, inverse, (((1,), (1,)), ((), ())), precision=precision, preferred_element_type=F32
    )


def sum_all(chips, deeps, x, total, core_buf, chip_buf, deep_buf, sems):
    me, deep, core, chip = places()
    core_sem, chip_sem, deep_sem, back_sem, last_sem = sems
    piece = chip_buf.shape[1]
    sibling = {"left": chip * 2 + (1 - core)}
    part_of = lambda q: pl.ds(pl.multiple_of(q * piece, 8), piece)
    firsts = []
    for o in range(1, chips + 1):
        q = part_of(lax.rem(chip + o, chips))
        firsts.append(send(x.at[1 - core, q], core_buf.at[q], core_sem, o - 1, sibling))
    yield
    copies = []
    for o in range(1, chips + 1):
        peer = lax.rem(chip + o, chips)
        q = part_of(peer)
        firsts[o - 1].wait()
        core_buf[q, :] += x[core, q, :]
        if o < chips:
            copies.append(
                send(core_buf.at[q], chip_buf.at[o - 1], chip_sem, o - 1, {"left": peer * 2 + core})
            )
    yield
    mine = part_of(chip)
    part = core_buf[mine, :]
    for o in range(1, chips):
        copies[o - 1].wait()
        part = part + chip_buf[o - 1]
    deep_buf[deep] = part
    copies = []
    for o in range(1, deeps):
        copies.append(
            send(
                deep_buf.at[deep], deep_buf.at[deep], deep_sem, o - 1,
                {"right": lax.rem(deep + o, deeps)},
            )
        )
    yield
    for copy in copies:
        copy.wait()
    part = deep_buf[0]
    for d in range(1, deeps):
        part = part + deep_buf[d]
    total[core, mine, :] = part
    copies = []
    for o in range(1, chips):
        copies.append(
            send(
                total.at[core, mine], total.at[core, mine], back_sem, o - 1,
                chip_peer(chip, core, o, chips),
            )
        )
    lasts = [send(total.at[core, mine], total.at[core, mine], last_sem, 0, sibling)]
    yield
    for o in range(1, chips):
        copies[o - 1].wait()
        q = part_of(lax.rem(chip + chips - o, chips))
        lasts.append(send(total.at[core, q], total.at[core, q], last_sem, o, sibling))
    yield
    for copy in lasts:
        copy.wait()


def whole_kernel(total, chips, deeps, *args):
    anys, (row_out, col_out, red_out), refs, rest = args[:8], args[8:11], args[11:19], args[19:]
    (
        tile_ref, row_own, col_own, left_scr, right_scr, sketch_scr, freq_scr, row_acc, col_acc,
        col_part, row_buf, core_buf, chip_buf, row_full, col_full,
        x_buf, t_buf, sum_core, sum_chip, sum_deep, x_last, t_last, last_core, last_chip, last_deep,
        work, inv1, inv2, mix_scr, in_sem, out_sem, row_sem, core_sem, chip_sem, row_all, col_all, pair_all,
        *sum_sems,
    ) = rest
    lf_ref, rf_ref, ld_ref, la_ref, rd_ref, ra_ref, cs_ref, rs_ref = refs
    me, deep, core, chip = places()
    sibling = {"left": chip * 2 + (1 - core)}
    rows, cols = tile_ref.shape
    width, ports = row_out.shape[1], ld_ref.shape[0]
    chunks, blocks = rows // UNIT, cols // UNIT
    share, block = rows // deeps, col_own.shape[0] // 2
    seg, quarter = share // chunks, chips * block
    cols_at = lambda h, c: pl.multiple_of(h * 2 * quarter + core * quarter + c * block, 8)

    def sum_round(n, row, col):
        other = jnp.where(core == 0, col, row)
        store_gram(x_buf.at[n], 1 - core, tdot(other, other, precise))
        steps_of = sum_all(
            chips, deeps, x_buf.at[n], t_buf.at[n], sum_core.at[n], sum_chip.at[n],
            sum_deep.at[n], [s.at[n] for s in sum_sems],
        )
        next(steps_of)
        own = jnp.where(core == 0, row, col)
        store_gram(x_buf.at[n], core, tdot(own, own, precise))
        return steps_of

    steps = deeps.bit_length() - 1
    row_copies = [[] for _ in range(chunks)]

    def row_step(c, i):
        for copy in row_copies[c]:
            copy.wait()
        near = 1 << (steps - 1 - i)
        side = lax.rem(deep // near, 2)
        row_copies[c] = []
        for n in range(1 << i):
            d = n * 2 * near + lax.rem(deep, 2 * near)
            at = pl.ds(pl.multiple_of(d * share + c * seg, 8), seg)
            row_copies[c].append(
                send(
                    row_full.at[at], row_full.at[at], row_all.at[c], (1 << i) - 1 + n,
                    {"right": deep + (1 - 2 * side) * near},
                )
            )

    def col_spread(h):
        return [
            send(
                col_own.at[pl.ds(h * block, block)], col_full.at[pl.ds(cols_at(h, chip), block)],
                col_all.at[h], o - 1, chip_peer(chip, core, o, chips),
            )
            for o in range(1, chips)
        ]

    def col_share(h, copies):
        for copy in copies:
            copy.wait()
        own = pl.ds(cols_at(h, 0), quarter)
        return send(col_full.at[own], col_full.at[own], pair_all, h, sibling)

    def mixed(value, m, terms):
        return jnp.dot(
            join_parts(value, LEFT_PARTS[:terms], 1), mix_scr[m, 0:terms * width, :],
            preferred_element_type=F32,
        )

    col_copies = []
    images(
        total, chips, deeps, anys, refs, tile_ref, row_own, col_own,
        left_scr, right_scr, sketch_scr, freq_scr, row_acc, col_acc, col_part,
        row_buf, core_buf, chip_buf, in_sem, row_sem, core_sem, chip_sem,
        lambda: col_copies.append(col_spread(0)),
    )
    row_full[pl.ds(pl.multiple_of(deep * share, 8), share), :] = row_own[...]
    half = chunks // 2
    for c in range(half):
        row_step(c, 0)
    for h in range(2):
        col_full[pl.ds(cols_at(h, chip), block), :] = col_own[h * block:(h + 1) * block, :]
    for n, _ in enumerate(sum_round(0, row_own[...], col_own[...])):
        if n == 2:
            for c in range(half, chunks):
                row_step(c, 0)
        if n == 3:
            col_copies.append(col_spread(1))
    for c in range(half):
        row_step(c, 1)
    pair = [col_share(0, col_copies[0])]
    for n, _ in enumerate(factor(True, t_buf.at[0], inv1, work)):
        if n == 1:
            pair.append(col_share(1, col_copies[1]))
        if n == 2:
            for c in range(half, chunks):
                row_step(c, 1)
    for i in range(2, steps):
        for c in range(chunks):
            row_step(c, i)
    for m in range(2):
        mix_scr[m] = join_parts(inv1[m].T, RIGHT_PARTS, 0)
    row_out[...] = mixed(row_own[...], 0, 6)
    second = sum_round(1, row_out[...], mixed(col_own[...], 1, 6))
    work[0, 0:48, 0:width] = jnp.zeros((48, width), F32)

    def cols_of(which):
        per = quarter // UNIT

        @pl.loop(0, 2 * per)
        def _(i):
            b = (i // per) * 2 * per + which * per + lax.rem(i, per)
            cl = pl.ds(pl.multiple_of(b * UNIT, UNIT), UNIT)
            value = mixed(col_full[cl, :], 1, 6)
            col_part[cl, :] = value
            rounded = value.astype(BF16)
            cs_ref[cl, :] = rounded
            right = join_parts(ra_ref[:, cl], (0, 1, 2), 0)
            work[0, 0:48, 0:width] += jnp.dot(right, rounded, preferred_element_type=F32)

    cols_of(core)
    next(second, None)
    for copy in pair:
        copy.wait()
    cols_of(1 - core)
    next(second, None)

    def apply_rows(c):
        sl = pl.ds(pl.multiple_of(c * UNIT, UNIT), UNIT)
        row_acc[c] = jnp.dot(tile_ref[sl, :], cs_ref[...], preferred_element_type=F32)

    for part in range(2):
        pl.loop(part * chunks // 2, (part + 1) * chunks // 2)(apply_rows)
        next(second, None)
    low = (work[0, 0:16, 0:width] + work[0, 16:32, 0:width] + work[0, 32:48, 0:width]) * (-1.0 / total)
    work[0, :, 0:width] = jnp.zeros((width, width), F32)
    for p in (0, 2, 5):
        at = (6 + p) * ports
        work[0, at:at + ports, 0:width] = low
    low = work[0, :, 0:width]
    work[0] = jnp.zeros((width, 2 * width), F32)
    work[1, :, 0:width] = jnp.zeros((width, width), F32)
    for copies in row_copies:
        for copy in copies:
            copy.wait()

    @pl.loop(0, chunks)
    def _(c):
        sl = pl.ds(pl.multiple_of(c * UNIT, UNIT), UNIT)
        applied = row_acc[c]
        freq = jnp.concatenate([freq_scr[sl, :] * (1.0 / total)] * (width // 128), axis=1)
        both = jnp.concatenate([applied, applied * freq], axis=1)
        both_hi = both.astype(BF16)
        both_lo = (both - both_hi.astype(F32)).astype(BF16)
        q = mixed(row_full[sl, :], 0, 6).T
        q_hi = q.astype(BF16)
        q_lo = (q - q_hi.astype(F32)).astype(BF16)
        work[0] += jnp.dot(
            jnp.concatenate([q_hi, q_hi, q_lo], axis=1),
            jnp.concatenate([both_hi, both_lo, both_hi], axis=0),
            preferred_element_type=F32,
        )
        left = left_scr[sl, :]
        work[1, :, 0:width] += jnp.dot(
            jnp.concatenate([q_hi, q_lo], axis=1), jnp.concatenate([left, left], axis=0),
            preferred_element_type=F32,
        )

    shifted = work[0, :, width:] + jnp.dot(
        work[1, :, 0:width], low, precision=precise, preferred_element_type=F32
    )
    for n in range(width // 128):
        x_last[0, n * width:(n + 1) * width, :] = work[0, :, n * 128:(n + 1) * 128]
        x_last[1, n * width:(n + 1) * width, :] = shifted[:, n * 128:(n + 1) * 128]
    for _ in second:
        pass
    last = sum_all(
        chips, deeps, x_last, t_last, last_core, last_chip, last_deep, [s.at[2] for s in sum_sems]
    )
    next(last, None)
    for _ in factor(False, t_buf.at[1], inv2, work):
        next(last, None)
    for m in range(2):
        mix_scr[m, 0:3 * width, :] = join_parts(inv2[m].T, RIGHT_PARTS[:3], 0)

    @pl.loop(0, blocks)
    def _(b):
        cl = pl.ds(pl.multiple_of(b * UNIT, UNIT), UNIT)
        col_part[cl, :] = mixed(col_part[cl, :], 1, 3) * math.sqrt(cols * deeps)
        pltpu.make_async_copy(col_part.at[cl], col_out.at[cl], out_sem.at[b]).start()

    row_out[...] = mixed(row_out[...], 0, 3) * math.sqrt(rows * chips * 2)
    for _ in last:
        pass
    for m in range(2):
        summed = jnp.concatenate(
            [t_last[m, n * width:(n + 1) * width, :] for n in range(width // 128)], axis=1
        )
        red_out[m] = apply_inverse(
            jnp.dot(inv2[0], summed, precision=precise, preferred_element_type=F32),
            inv2[1], precise,
        )
    for b in range(blocks):
        cl = pl.ds(b * UNIT, UNIT)
        pltpu.make_async_copy(col_part.at[cl], col_out.at[cl], out_sem.at[b]).wait()


def deliver_kernel(row_in, col_in, red_in, row_out, col_out, low_out, shift_out):
    col_out[...] = col_in[...]

    @pl.when(pl.program_id(0) == 0)
    def _():
        row_out[...] = row_in[...]
        low_out[...] = red_in[0]
        shift_out[...] = red_in[1]


def deliver(row_basis, col_basis, reduced):
    shapes = [row_basis.shape, col_basis.shape, reduced.shape[1:], reduced.shape[1:]]
    width, tall = row_basis.shape[1], col_basis.shape[0] // 8
    fixed = lambda shape: pl.BlockSpec(shape, lambda i: (0,) * len(shape))
    moving = pl.BlockSpec((tall, width), lambda i: (i, 0))
    return pl.pallas_call(
        deliver_kernel,
        grid=(8,),
        in_specs=[fixed(row_basis.shape), moving, fixed(reduced.shape)],
        out_specs=[fixed(shapes[0]), moving, fixed(shapes[2]), fixed(shapes[3])],
        out_shape=[jax.ShapeDtypeStruct(shape, F32) for shape in shapes],
        name="deliver",
    )(row_basis, col_basis, reduced)


def body(lf, rf, ld, la, rd, ra, cs, rs):
    rows, cols = lf.shape[0], rf.shape[0]
    ports, width = ld.shape[0], cs.shape[1]
    left_n, right_n = lax.axis_size("left"), lax.axis_size("right")
    total_rows = rows * left_n
    chips, deeps = left_n // 2, right_n
    steps = deeps.bit_length() - 1
    chunks, blocks = rows // UNIT, cols // UNIT
    block, share = cols // 4 // chips, rows // deeps
    high, full = 128 * len(triangle(width)), width * width // 128
    args = (lf[None, :], rf[None, :], ld, la, rd, ra, cs, rs)
    sems = lambda n, m: pltpu.SemaphoreType.DMA((n, 2, m))
    row_basis, col_basis, reduced = pl.pallas_call(
        functools.partial(whole_kernel, float(total_rows), chips, deeps),
        in_specs=[pl.BlockSpec(memory_space=pl.ANY)] * 8,
        out_specs=[
            pl.BlockSpec(memory_space=pltpu.VMEM),
            pl.BlockSpec(memory_space=pl.ANY),
            pl.BlockSpec(memory_space=pltpu.VMEM),
        ],
        out_shape=[
            jax.ShapeDtypeStruct((share, width), F32),
            jax.ShapeDtypeStruct((cols, width), F32),
            jax.ShapeDtypeStruct((2, width, width), F32),
        ],
        scratch_shapes=[pltpu.VMEM(x.shape, x.dtype) for x in args] + [
            pltpu.VMEM((rows, cols), BF16),
            pltpu.VMEM((share, width), F32),
            pltpu.VMEM((2 * block, width), F32),
            pltpu.VMEM((rows, 256), BF16),
            pltpu.VMEM((256, cols), BF16),
            pltpu.VMEM((chunks, width, UNIT), BF16),
            pltpu.VMEM((rows, 128), F32),
            pltpu.VMEM((chunks, UNIT, width), F32),
            pltpu.VMEM((blocks, width, UNIT), F32),
            pltpu.VMEM((cols, width), F32),
            pltpu.VMEM((chunks, UNIT, width), F32),
            pltpu.VMEM((2, cols // 4, width), F32),
            pltpu.VMEM((2, chips - 1, block, width), F32),
            pltpu.VMEM((rows, width), F32),
            pltpu.VMEM((cols, width), F32),
            pltpu.VMEM((2, 2, high, 128), F32),
            pltpu.VMEM((2, 2, high, 128), F32),
            pltpu.VMEM((2, high, 128), F32),
            pltpu.VMEM((2, chips - 1, high // chips, 128), F32),
            pltpu.VMEM((2, deeps, high // chips, 128), F32),
            pltpu.VMEM((2, full, 128), F32),
            pltpu.VMEM((2, full, 128), F32),
            pltpu.VMEM((full, 128), F32),
            pltpu.VMEM((chips - 1, full // chips, 128), F32),
            pltpu.VMEM((deeps, full // chips, 128), F32),
            pltpu.VMEM((2, width, 2 * width), F32),
            pltpu.VMEM((2, width, width), F32),
            pltpu.VMEM((2, width, width), F32),
            pltpu.VMEM((2, 6 * width, width), BF16),
            pltpu.SemaphoreType.DMA((8,)),
            pltpu.SemaphoreType.DMA((blocks,)),
            sems(chunks, steps), sems(2, chips), sems(2, chips - 1),
            sems(chunks, deeps - 1), sems(2, chips - 1), pltpu.SemaphoreType.DMA((2, 2)),
            sems(3, chips), sems(3, chips - 1), sems(3, deeps - 1), sems(3, chips - 1),
            sems(3, chips),
        ],
        compiler_params=pltpu.CompilerParams(
            collective_id=1, has_side_effects=True, vmem_limit_bytes=63 << 20
        ),
        name="loewner",
    )(*args)
    return deliver(row_basis, col_basis, reduced)


def solution(mesh):
    in_specs = (
        P("left"), P("right"), P(None, "left"), P(None, "left"),
        P(None, "right"), P(None, "right"), P("right", None), P("left", None),
    )
    out_specs = (P(("left", "right"), None), P("right", None), P(), P())
    return jax.shard_map(body, mesh=mesh, in_specs=in_specs, out_specs=out_specs, check_vma=False)
```

```python
import functools
import math

import jax
import jax.numpy as jnp
from jax import lax
from jax.experimental import pallas as pl
from jax.experimental.pallas import tpu as pltpu
from jax.sharding import PartitionSpec as P

precise = lax.Precision.HIGHEST
F32 = jnp.float32
BF16 = jnp.bfloat16
LEFT_PARTS = (0, 0, 1, 0, 1, 2)
RIGHT_PARTS = (0, 1, 0, 2, 1, 0)


def tdot(a, b, precision=None):
    return lax.dot_general(
        a, b, (((0,), (0,)), ((), ())), precision=precision, preferred_element_type=F32
    )


def split3(x):
    one = x.astype(BF16).astype(F32)
    rest = x - one
    two = rest.astype(BF16).astype(F32)
    return (one, two, (rest - two).astype(BF16).astype(F32))


def join_parts(x, order, axis):
    parts = split3(x)
    return jnp.concatenate([parts[p].astype(BF16) for p in order], axis=axis)


def stack_parts(first, second, order):
    a, b = split3(first), split3(second)
    pieces = [a[p] for p in order] + [b[p] for p in order]
    pad = jnp.zeros((256 - 12 * first.shape[0], first.shape[1]), F32)
    return jnp.concatenate(pieces + [pad], axis=0)


UNIT = 512


def places():
    me, deep = lax.axis_index("left"), lax.axis_index("right")
    core = lax.rem(me, 2)
    return me, deep, core, me // 2


def chip_peer(chip, core, offset, chips):
    return {"left": lax.rem(chip + offset, chips) * 2 + core}


def peers_of(chips, deeps):
    me, deep, core, chip = places()
    peers = [{"left": chip * 2 + (1 - core)}]
    peers += [chip_peer(chip, core, o, chips) for o in range(1, chips)]
    peers += [{"right": lax.rem(deep + o, deeps)} for o in range(1, deeps)]
    return peers


def greet_start(chips, deeps):
    barrier = pltpu.get_barrier_semaphore()
    for peer in peers_of(chips, deeps):
        pl.semaphore_signal(
            barrier, inc=1, device_id=peer, device_id_type=pl.DeviceIdType.MESH
        )


def greet_end(chips, deeps):
    pl.semaphore_wait(pltpu.get_barrier_semaphore(), chips + deeps - 1)


def greet(chips, deeps):
    greet_start(chips, deeps)
    greet_end(chips, deeps)


def send(src, dst, sems, slot, peer):
    copy = pltpu.make_async_remote_copy(
        src_ref=src,
        dst_ref=dst,
        send_sem=sems.at[0, slot],
        recv_sem=sems.at[1, slot],
        device_id=peer,
        device_id_type=pl.DeviceIdType.MESH,
    )
    copy.start()
    return copy


def reversed_bits(p, bits):
    return sum(((p >> i) & 1) << (bits - 1 - i) for i in range(bits))


def images(
    total, chips, deeps, anys, refs, tile_ref, row_out, col_out,
    left_scr, right_scr, sketch_scr, freq_scr, row_acc, col_acc, col_part,
    row_buf, core_buf, chip_buf,
    in_sem, row_sem, core_sem, chip_sem, on_cols,
):
    lf_any, rf_any, ld_any, la_any, rd_any, ra_any, cs_any, rs_any = anys
    lf_ref, rf_ref, ld_ref, la_ref, rd_ref, ra_ref, cs_ref, rs_ref = refs
    me, deep, core, chip = places()
    rows, cols = tile_ref.shape
    width = row_out.shape[1]
    chunks, blocks = rows // UNIT, cols // UNIT
    steps = deeps.bit_length() - 1
    share, seg = rows // deeps, UNIT // deeps
    order = [reversed_bits(p, steps) for p in range(deeps)]
    sibling = {"left": chip * 2 + (1 - core)}
    loads = [
        pltpu.make_async_copy(src, dst, in_sem.at[n])
        for n, (src, dst) in enumerate(
            [
                (lf_any, lf_ref), (la_any, la_ref), (ld_any, ld_ref), (rs_any, rs_ref),
                (rf_any, rf_ref), (rd_any, rd_ref), (ra_any, ra_ref), (cs_any, cs_ref),
            ]
        )
    ]
    for load in loads:
        load.start()
    greet_start(chips, deeps)

    @pl.loop(0, chunks)
    def _(c):
        row_acc[c] = jnp.zeros((UNIT, width), F32)

    @pl.loop(0, blocks)
    def _(b):
        col_acc[b] = jnp.zeros((width, UNIT), F32)

    for load in loads[:4]:
        load.wait()
    for r in range(0, rows, UNIT):
        wide = jnp.broadcast_to(lf_ref[:, r:r + UNIT] * total, (128, UNIT))
        freq_scr[r:r + UNIT, :] = wide.T
        stacked = stack_parts(la_ref[:, r:r + UNIT], -ld_ref[:, r:r + UNIT], LEFT_PARTS)
        left_scr[r:r + UNIT, :] = stacked.T.astype(BF16)
    for c in range(chunks):
        part = jnp.concatenate(
            [rs_ref[d * share + c * seg:d * share + (c + 1) * seg, :] for d in order], axis=0
        )
        sketch_scr[c] = part.astype(F32).T.astype(BF16)
    for load in loads[4:]:
        load.wait()

    @pl.loop(0, blocks)
    def _(b):
        cl = pl.ds(pl.multiple_of(b * UNIT, UNIT), UNIT)
        right_scr[:, cl] = stack_parts(rd_ref[:, cl], ra_ref[:, cl], RIGHT_PARTS).astype(BF16)

    def tiles(c, low, high, last):
        own = [pl.ds(d * share + c * seg, seg) for d in order]

        @pl.loop(low, high)
        def _(b):
            cl = pl.ds(pl.multiple_of(b * UNIT, UNIT), UNIT)
            left = jnp.concatenate([left_scr[sl, :] for sl in own], axis=0)
            freq = jnp.concatenate([freq_scr[sl, :] for sl in own], axis=0)
            numer = jnp.dot(left, right_scr[:, cl], preferred_element_type=F32)
            gap = jnp.concatenate([freq] * (UNIT // 128), axis=1) - rf_ref[:, cl] * total
            tile = (numer / gap).astype(BF16)
            for p, sl in enumerate(own):
                tile_ref[sl, cl] = tile[p * seg:(p + 1) * seg, :]
            row_acc[c] += jnp.dot(tile, cs_ref[cl, :], preferred_element_type=F32)
            part = jnp.dot(sketch_scr[c], tile, preferred_element_type=F32)
            if last:
                col_part[cl, :] = (col_acc[b] + part).T
            else:
                col_acc[b] += part

    def bit(s):
        return lax.rem(deep // (1 << s), 2)

    def segment(s):
        start, size = 0, UNIT
        for t in range(s):
            size = size // 2
            start = start + bit(t) * size
        return start, size

    def halve(c, s):
        start, size = segment(s)
        half = size // 2
        src = pl.ds(pl.multiple_of(start + (1 - bit(s)) * half, 8), half)
        slot = pl.ds(UNIT - size, half)
        return send(
            row_acc.at[c, src], row_buf.at[c, slot], row_sem.at[c], s,
            {"right": deep + (1 - 2 * bit(s)) * (1 << s)},
        )

    def settle(c, s, copy):
        copy.wait()
        start, size = segment(s)
        half = size // 2
        mine = pl.ds(pl.multiple_of(start + bit(s) * half, 8), half)
        value = row_acc[c, mine, :] + row_buf[c, UNIT - size:UNIT - size + half, :]
        if s == steps - 1:
            row_out[c * seg:(c + 1) * seg, :] = value
            return None
        row_acc[c, mine, :] = value
        return halve(c, s + 1)

    half_cols, quarter = cols // 2, cols // 4
    piece = quarter // chips

    def pair_start(h):
        copies = []
        for o in range(1, chips + 1):
            peer = lax.rem(chip + o, chips)
            at = pl.multiple_of(peer * piece, 8)
            src = pl.ds(h * half_cols + (1 - core) * quarter + at, piece)
            copies.append(
                send(
                    col_part.at[src], core_buf.at[h, pl.ds(at, piece)], core_sem.at[h], o - 1,
                    sibling,
                )
            )
        return copies

    def pair_end(h, copies):
        sent = []
        for o in range(1, chips + 1):
            peer = lax.rem(chip + o, chips)
            at = pl.multiple_of(peer * piece, 8)
            copies[o - 1].wait()
            dst = pl.ds(at, piece)
            core_buf[h, dst, :] += col_part[pl.ds(h * half_cols + core * quarter + at, piece), :]
            if o < chips:
                sent.append(
                    send(
                        core_buf.at[h, dst], chip_buf.at[h, o - 1], chip_sem.at[h], o - 1,
                        {"left": peer * 2 + core},
                    )
                )
        return sent

    def chip_end(h, copies):
        value = core_buf[h, pl.ds(pl.multiple_of(chip * piece, 8), piece), :]
        for o in range(1, chips):
            copies[o - 1].wait()
            value = value + chip_buf[h, o - 1]
        col_out[h * piece:(h + 1) * piece, :] = value

    z = [None] * chunks
    mid = blocks // 2
    early = chunks // 2
    for c in range(early):
        tiles(c, 0, blocks, False)
        if c == 0:
            greet_end(chips, deeps)
        z[c] = halve(c, 0)
    for c in range(early, chunks):
        tiles(c, 0, mid, c == chunks - 1)
        if c == early:
            z[0] = settle(0, 0, z[0])
    pair = pair_start(0)
    for c in range(early, chunks):
        tiles(c, mid, blocks, c == chunks - 1)
        z[c] = halve(c, 0)
        if c == early:
            chip_first = pair_end(0, pair)
            for e in range(1, early):
                z[e] = settle(e, 0, z[e])
    pair = pair_start(1)
    chip_second = pair_end(1, pair)
    for s in range(1, steps):
        for c in range(early):
            z[c] = settle(c, s, z[c])
    for s in range(steps):
        if s == steps - 1:
            chip_end(0, chip_first)
            chip_end(1, chip_second)
            on_cols()
        for c in range(early, chunks):
            z[c] = settle(c, s, z[c])


BLOCK = 64
GROUP = 8


def triangle(width):
    return [(i, j) for i in range(width // 128) for j in range(i, width // 128)]


def store_gram(dst, m, gram):
    for n, (i, j) in enumerate(triangle(gram.shape[0])):
        dst[m, n * 128:(n + 1) * 128, :] = gram[i * 128:(i + 1) * 128, j * 128:(j + 1) * 128]


def factor(shifted, t_ref, out_ref, work):
    width = out_ref.shape[-1]
    row_id = lax.broadcasted_iota(jnp.int32, (width, width), 0)
    col_id = lax.broadcasted_iota(jnp.int32, (width, width), 1)
    eye = (row_id == col_id).astype(F32)
    for m in range(2):
        work[m, :, 0:width] = jnp.zeros((width, width), F32)
        for n, (i, j) in enumerate(triangle(width)):
            work[m, i * 128:(i + 1) * 128, j * 128:(j + 1) * 128] = t_ref[m, n * 128:(n + 1) * 128, :]
        if shifted:
            gram = work[m, :, 0:width]
            trace = jnp.sum(jnp.sum(gram * eye, axis=1, keepdims=True), axis=0, keepdims=True)
            work[m, :, 0:width] = gram + (1e-05 * trace / width) * eye
        work[m, :, width:] = eye
    brow = lax.broadcasted_iota(jnp.int32, (BLOCK, BLOCK), 0)
    bcol = lax.broadcasted_iota(jnp.int32, (BLOCK, BLOCK), 1)
    small_eye = (brow == bcol).astype(F32)
    low = lax.broadcasted_iota(jnp.int32, (BLOCK, 2 * BLOCK), 0)
    for k in range(0, width, BLOCK):
        pairs = [
            jnp.concatenate([work[m, k:k + BLOCK, k:k + BLOCK], small_eye], axis=1)
            for m in range(2)
        ]
        for base in range(0, BLOCK, GROUP):
            copies = [
                [jnp.broadcast_to(pair[:, s:s + 1], low.shape) for s in range(base, base + GROUP)]
                for pair in pairs
            ]
            for i in range(GROUP):
                s = base + i
                for m in range(2):
                    wide = copies[m]
                    top = 1.0 / wide[i][s:s + 1, :]
                    column = jnp.where(low > s, wide[i], 0.0)
                    for j in range(i + 1, GROUP):
                        wide[j] = wide[j] - column * (wide[j][s:s + 1, :] * top)
                    pairs[m] = pairs[m] - column * (pairs[m][s:s + 1, :] * top)
        lo = k + BLOCK
        start, stop = k // 128 * 128, width + (lo + 127) // 128 * 128
        solved = []
        for m in range(2):
            diag = jnp.sum(pairs[m][:, 0:BLOCK] * small_eye, axis=1, keepdims=True)
            inv = pairs[m][:, BLOCK:] * lax.rsqrt(diag)
            solved.append(
                jnp.dot(
                    inv, work[m, k:lo, start:stop], precision=precise,
                    preferred_element_type=F32,
                )
            )
        for m in range(2):
            out_ref[m, k:lo, 0:stop - width] = solved[m][:, width - start:]
            if stop < 2 * width:
                out_ref[m, k:lo, stop - width:] = jnp.zeros((BLOCK, 2 * width - stop), F32)
        if lo < width:
            deltas = [tdot(rows[:, lo - start:width - start], rows, precise) for rows in solved]
            for m in range(2):
                work[m, lo:, start:stop] = work[m, lo:, start:stop] - deltas[m]
        yield


def apply_inverse(basis, inverse, precision):
    return lax.dot_general(
        basis, inverse, (((1,), (1,)), ((), ())), precision=precision, preferred_element_type=F32
    )


def sum_all(chips, deeps, x, total, core_buf, chip_buf, deep_buf, sems):
    me, deep, core, chip = places()
    core_sem, chip_sem, deep_sem, back_sem, last_sem = sems
    piece = chip_buf.shape[1]
    sibling = {"left": chip * 2 + (1 - core)}
    part_of = lambda q: pl.ds(pl.multiple_of(q * piece, 8), piece)
    firsts = []
    for o in range(1, chips + 1):
        q = part_of(lax.rem(chip + o, chips))
        firsts.append(send(x.at[1 - core, q], core_buf.at[q], core_sem, o - 1, sibling))
    yield
    copies = []
    for o in range(1, chips + 1):
        peer = lax.rem(chip + o, chips)
        q = part_of(peer)
        firsts[o - 1].wait()
        core_buf[q, :] += x[core, q, :]
        if o < chips:
            copies.append(
                send(core_buf.at[q], chip_buf.at[o - 1], chip_sem, o - 1, {"left": peer * 2 + core})
            )
    yield
    mine = part_of(chip)
    part = core_buf[mine, :]
    for o in range(1, chips):
        copies[o - 1].wait()
        part = part + chip_buf[o - 1]
    deep_buf[deep] = part
    copies = []
    for o in range(1, deeps):
        copies.append(
            send(
                deep_buf.at[deep], deep_buf.at[deep], deep_sem, o - 1,
                {"right": lax.rem(deep + o, deeps)},
            )
        )
    yield
    for copy in copies:
        copy.wait()
    part = deep_buf[0]
    for d in range(1, deeps):
        part = part + deep_buf[d]
    total[core, mine, :] = part
    copies = []
    for o in range(1, chips):
        copies.append(
            send(
                total.at[core, mine], total.at[core, mine], back_sem, o - 1,
                chip_peer(chip, core, o, chips),
            )
        )
    lasts = [send(total.at[core, mine], total.at[core, mine], last_sem, 0, sibling)]
    yield
    for o in range(1, chips):
        copies[o - 1].wait()
        q = part_of(lax.rem(chip + chips - o, chips))
        lasts.append(send(total.at[core, q], total.at[core, q], last_sem, o, sibling))
    yield
    for copy in lasts:
        copy.wait()


def whole_kernel(total, chips, deeps, *args):
    anys, (row_out, col_out, red_out), refs, rest = args[:8], args[8:11], args[11:19], args[19:]
    (
        tile_ref, row_own, col_own, left_scr, right_scr, sketch_scr, freq_scr, row_acc, col_acc,
        col_part, row_buf, core_buf, chip_buf, row_full, col_full,
        x_buf, t_buf, sum_core, sum_chip, sum_deep, x_last, t_last, last_core, last_chip, last_deep,
        work, inv1, inv2, mix_scr, in_sem, out_sem, row_sem, core_sem, chip_sem, row_all, col_all, pair_all,
        *sum_sems,
    ) = rest
    lf_ref, rf_ref, ld_ref, la_ref, rd_ref, ra_ref, cs_ref, rs_ref = refs
    me, deep, core, chip = places()
    sibling = {"left": chip * 2 + (1 - core)}
    rows, cols = tile_ref.shape
    width, ports = row_out.shape[1], ld_ref.shape[0]
    chunks, blocks = rows // UNIT, cols // UNIT
    share, block = rows // deeps, col_own.shape[0] // 2
    seg, quarter = share // chunks, chips * block
    cols_at = lambda h, c: pl.multiple_of(h * 2 * quarter + core * quarter + c * block, 8)

    def sum_round(n, row, col):
        other = jnp.where(core == 0, col, row)
        store_gram(x_buf.at[n], 1 - core, tdot(other, other, precise))
        steps_of = sum_all(
            chips, deeps, x_buf.at[n], t_buf.at[n], sum_core.at[n], sum_chip.at[n],
            sum_deep.at[n], [s.at[n] for s in sum_sems],
        )
        next(steps_of)
        own = jnp.where(core == 0, row, col)
        store_gram(x_buf.at[n], core, tdot(own, own, precise))
        return steps_of

    steps = deeps.bit_length() - 1
    row_copies = [[] for _ in range(chunks)]

    def row_step(c, i):
        for copy in row_copies[c]:
            copy.wait()
        near = 1 << (steps - 1 - i)
        side = lax.rem(deep // near, 2)
        row_copies[c] = []
        for n in range(1 << i):
            d = n * 2 * near + lax.rem(deep, 2 * near)
            at = pl.ds(pl.multiple_of(d * share + c * seg, 8), seg)
            row_copies[c].append(
                send(
                    row_full.at[at], row_full.at[at], row_all.at[c], (1 << i) - 1 + n,
                    {"right": deep + (1 - 2 * side) * near},
                )
            )

    def col_spread(h):
        return [
            send(
                col_own.at[pl.ds(h * block, block)], col_full.at[pl.ds(cols_at(h, chip), block)],
                col_all.at[h], o - 1, chip_peer(chip, core, o, chips),
            )
            for o in range(1, chips)
        ]

    def col_share(h, copies):
        for copy in copies:
            copy.wait()
        own = pl.ds(cols_at(h, 0), quarter)
        return send(col_full.at[own], col_full.at[own], pair_all, h, sibling)

    def mixed(value, m, terms):
        return jnp.dot(
            join_parts(value, LEFT_PARTS[:terms], 1), mix_scr[m, 0:terms * width, :],
            preferred_element_type=F32,
        )

    col_copies = []
    images(
        total, chips, deeps, anys, refs, tile_ref, row_own, col_own,
        left_scr, right_scr, sketch_scr, freq_scr, row_acc, col_acc, col_part,
        row_buf, core_buf, chip_buf, in_sem, row_sem, core_sem, chip_sem,
        lambda: col_copies.append(col_spread(0)),
    )
    row_full[pl.ds(pl.multiple_of(deep * share, 8), share), :] = row_own[...]
    half = chunks // 2
    for c in range(half):
        row_step(c, 0)
    for h in range(2):
        col_full[pl.ds(cols_at(h, chip), block), :] = col_own[h * block:(h + 1) * block, :]
    for n, _ in enumerate(sum_round(0, row_own[...], col_own[...])):
        if n == 2:
            for c in range(half, chunks):
                row_step(c, 0)
        if n == 3:
            col_copies.append(col_spread(1))
    for c in range(half):
        row_step(c, 1)
    pair = [col_share(0, col_copies[0])]
    for n, _ in enumerate(factor(True, t_buf.at[0], inv1, work)):
        if n == 1:
            pair.append(col_share(1, col_copies[1]))
        if n == 2:
            for c in range(half, chunks):
                row_step(c, 1)
    for i in range(2, steps):
        for c in range(chunks):
            row_step(c, i)
    for m in range(2):
        mix_scr[m] = join_parts(inv1[m].T, RIGHT_PARTS, 0)
    row_out[...] = mixed(row_own[...], 0, 6)
    second = sum_round(1, row_out[...], mixed(col_own[...], 1, 6))
    work[0, 0:48, 0:width] = jnp.zeros((48, width), F32)

    def cols_of(which):
        per = quarter // UNIT

        @pl.loop(0, 2 * per)
        def _(i):
            b = (i // per) * 2 * per + which * per + lax.rem(i, per)
            cl = pl.ds(pl.multiple_of(b * UNIT, UNIT), UNIT)
            value = mixed(col_full[cl, :], 1, 6)
            col_part[cl, :] = value
            rounded = value.astype(BF16)
            cs_ref[cl, :] = rounded
            right = join_parts(ra_ref[:, cl], (0, 1, 2), 0)
            work[0, 0:48, 0:width] += jnp.dot(right, rounded, preferred_element_type=F32)

    cols_of(core)
    next(second, None)
    for copy in pair:
        copy.wait()
    cols_of(1 - core)
    next(second, None)

    def apply_rows(c):
        sl = pl.ds(pl.multiple_of(c * UNIT, UNIT), UNIT)
        row_acc[c] = jnp.dot(tile_ref[sl, :], cs_ref[...], preferred_element_type=F32)

    for part in range(2):
        pl.loop(part * chunks // 2, (part + 1) * chunks // 2)(apply_rows)
        next(second, None)
    low = (work[0, 0:16, 0:width] + work[0, 16:32, 0:width] + work[0, 32:48, 0:width]) * (-1.0 / total)
    work[0, :, 0:width] = jnp.zeros((width, width), F32)
    for p in (0, 2, 5):
        at = (6 + p) * ports
        work[0, at:at + ports, 0:width] = low
    low = work[0, :, 0:width]
    work[0] = jnp.zeros((width, 2 * width), F32)
    work[1, :, 0:width] = jnp.zeros((width, width), F32)

    def project_rows(d):
        at = pl.multiple_of(d * share, share)
        sl = pl.ds(at, share)
        applied = row_acc[at // UNIT, pl.ds(pl.multiple_of(lax.rem(at, UNIT), 8), share), :]
        freq = jnp.concatenate([freq_scr[sl, :] * (1.0 / total)] * (width // 128), axis=1)
        both = jnp.concatenate([applied, applied * freq], axis=1)
        both_hi = both.astype(BF16)
        both_lo = (both - both_hi.astype(F32)).astype(BF16)
        q = mixed(row_full[sl, :], 0, 6).T
        q_hi = q.astype(BF16)
        q_lo = (q - q_hi.astype(F32)).astype(BF16)
        work[0] += jnp.dot(
            jnp.concatenate([q_hi, q_hi, q_lo], axis=1),
            jnp.concatenate([both_hi, both_lo, both_hi], axis=0),
            preferred_element_type=F32,
        )
        left = left_scr[sl, :]
        work[1, :, 0:width] += jnp.dot(
            jnp.concatenate([q_hi, q_lo], axis=1), jnp.concatenate([left, left], axis=0),
            preferred_element_type=F32,
        )

    side = lax.rem(deep, 2)
    pl.loop(0, deeps // 2)(lambda n: project_rows(2 * n + side))
    for copies in row_copies:
        for copy in copies:
            copy.wait()
    pl.loop(0, deeps // 2)(lambda n: project_rows(2 * n + 1 - side))
    shifted = work[0, :, width:] + jnp.dot(
        work[1, :, 0:width], low, precision=precise, preferred_element_type=F32
    )
    for n in range(width // 128):
        x_last[0, n * width:(n + 1) * width, :] = work[0, :, n * 128:(n + 1) * 128]
        x_last[1, n * width:(n + 1) * width, :] = shifted[:, n * 128:(n + 1) * 128]
    for _ in second:
        pass
    last = sum_all(
        chips, deeps, x_last, t_last, last_core, last_chip, last_deep, [s.at[2] for s in sum_sems]
    )
    next(last, None)
    for _ in factor(False, t_buf.at[1], inv2, work):
        next(last, None)
    for m in range(2):
        mix_scr[m, 0:3 * width, :] = join_parts(inv2[m].T, RIGHT_PARTS[:3], 0)

    @pl.loop(0, blocks)
    def _(b):
        cl = pl.ds(pl.multiple_of(b * UNIT, UNIT), UNIT)
        col_part[cl, :] = mixed(col_part[cl, :], 1, 3) * math.sqrt(cols * deeps)
        pltpu.make_async_copy(col_part.at[cl], col_out.at[cl], out_sem.at[b]).start()

    row_out[...] = mixed(row_out[...], 0, 3) * math.sqrt(rows * chips * 2)
    for _ in last:
        pass
    for m in range(2):
        summed = jnp.concatenate(
            [t_last[m, n * width:(n + 1) * width, :] for n in range(width // 128)], axis=1
        )
        red_out[m] = apply_inverse(
            jnp.dot(inv2[0], summed, precision=precise, preferred_element_type=F32),
            inv2[1], precise,
        )
    for b in range(blocks):
        cl = pl.ds(b * UNIT, UNIT)
        pltpu.make_async_copy(col_part.at[cl], col_out.at[cl], out_sem.at[b]).wait()


def deliver_kernel(row_in, col_in, red_in, row_out, col_out, low_out, shift_out):
    col_out[...] = col_in[...]

    @pl.when(pl.program_id(0) == 0)
    def _():
        row_out[...] = row_in[...]
        low_out[...] = red_in[0]
        shift_out[...] = red_in[1]


def deliver(row_basis, col_basis, reduced):
    shapes = [row_basis.shape, col_basis.shape, reduced.shape[1:], reduced.shape[1:]]
    width, tall = row_basis.shape[1], col_basis.shape[0] // 8
    fixed = lambda shape: pl.BlockSpec(shape, lambda i: (0,) * len(shape))
    moving = pl.BlockSpec((tall, width), lambda i: (i, 0))
    return pl.pallas_call(
        deliver_kernel,
        grid=(8,),
        in_specs=[fixed(row_basis.shape), moving, fixed(reduced.shape)],
        out_specs=[fixed(shapes[0]), moving, fixed(shapes[2]), fixed(shapes[3])],
        out_shape=[jax.ShapeDtypeStruct(shape, F32) for shape in shapes],
        name="deliver",
    )(row_basis, col_basis, reduced)


def body(lf, rf, ld, la, rd, ra, cs, rs):
    rows, cols = lf.shape[0], rf.shape[0]
    ports, width = ld.shape[0], cs.shape[1]
    left_n, right_n = lax.axis_size("left"), lax.axis_size("right")
    total_rows = rows * left_n
    chips, deeps = left_n // 2, right_n
    steps = deeps.bit_length() - 1
    chunks, blocks = rows // UNIT, cols // UNIT
    block, share = cols // 4 // chips, rows // deeps
    high, full = 128 * len(triangle(width)), width * width // 128
    args = (lf[None, :], rf[None, :], ld, la, rd, ra, cs, rs)
    sems = lambda n, m: pltpu.SemaphoreType.DMA((n, 2, m))
    row_basis, col_basis, reduced = pl.pallas_call(
        functools.partial(whole_kernel, float(total_rows), chips, deeps),
        in_specs=[pl.BlockSpec(memory_space=pl.ANY)] * 8,
        out_specs=[
            pl.BlockSpec(memory_space=pltpu.VMEM),
            pl.BlockSpec(memory_space=pl.ANY),
            pl.BlockSpec(memory_space=pltpu.VMEM),
        ],
        out_shape=[
            jax.ShapeDtypeStruct((share, width), F32),
            jax.ShapeDtypeStruct((cols, width), F32),
            jax.ShapeDtypeStruct((2, width, width), F32),
        ],
        scratch_shapes=[pltpu.VMEM(x.shape, x.dtype) for x in args] + [
            pltpu.VMEM((rows, cols), BF16),
            pltpu.VMEM((share, width), F32),
            pltpu.VMEM((2 * block, width), F32),
            pltpu.VMEM((rows, 256), BF16),
            pltpu.VMEM((256, cols), BF16),
            pltpu.VMEM((chunks, width, UNIT), BF16),
            pltpu.VMEM((rows, 128), F32),
            pltpu.VMEM((chunks, UNIT, width), F32),
            pltpu.VMEM((blocks, width, UNIT), F32),
            pltpu.VMEM((cols, width), F32),
            pltpu.VMEM((chunks, UNIT, width), F32),
            pltpu.VMEM((2, cols // 4, width), F32),
            pltpu.VMEM((2, chips - 1, block, width), F32),
            pltpu.VMEM((rows, width), F32),
            pltpu.VMEM((cols, width), F32),
            pltpu.VMEM((2, 2, high, 128), F32),
            pltpu.VMEM((2, 2, high, 128), F32),
            pltpu.VMEM((2, high, 128), F32),
            pltpu.VMEM((2, chips - 1, high // chips, 128), F32),
            pltpu.VMEM((2, deeps, high // chips, 128), F32),
            pltpu.VMEM((2, full, 128), F32),
            pltpu.VMEM((2, full, 128), F32),
            pltpu.VMEM((full, 128), F32),
            pltpu.VMEM((chips - 1, full // chips, 128), F32),
            pltpu.VMEM((deeps, full // chips, 128), F32),
            pltpu.VMEM((2, width, 2 * width), F32),
            pltpu.VMEM((2, width, width), F32),
            pltpu.VMEM((2, width, width), F32),
            pltpu.VMEM((2, 6 * width, width), BF16),
            pltpu.SemaphoreType.DMA((8,)),
            pltpu.SemaphoreType.DMA((blocks,)),
            sems(chunks, steps), sems(2, chips), sems(2, chips - 1),
            sems(chunks, deeps - 1), sems(2, chips - 1), pltpu.SemaphoreType.DMA((2, 2)),
            sems(3, chips), sems(3, chips - 1), sems(3, deeps - 1), sems(3, chips - 1),
            sems(3, chips),
        ],
        compiler_params=pltpu.CompilerParams(
            collective_id=1, has_side_effects=True, vmem_limit_bytes=63 << 20
        ),
        name="loewner",
    )(*args)
    return deliver(row_basis, col_basis, reduced)


def solution(mesh):
    in_specs = (
        P("left"), P("right"), P(None, "left"), P(None, "left"),
        P(None, "right"), P(None, "right"), P("right", None), P("left", None),
    )
    out_specs = (P(("left", "right"), None), P("right", None), P(), P())
    return jax.shard_map(body, mesh=mesh, in_specs=in_specs, out_specs=out_specs, check_vma=False)
```
